128 devices in a mesh: rows: 32 (over x, z, core), sub: 4 (over y).
Axes of the slice: x: 4, y: 4, z: 4, core: 2. Of those that a mesh axis runs over, the one named last changes fastest.
Arguments:
- diag_blocks: bfloat16 [2048, 128, 128], P(('rows', 'sub')), may hold values from -1 to 4
- off_blocks: bfloat16 [2048, 8, 128, 128], P(('rows', 'sub')), may hold values from -0.5 to 0.5
- col_blocks: int32 [2048, 8], P(('rows', 'sub')), may hold values from 0 to 2047, as said below
- sketch: bfloat16 [262144, 256], P(('rows', 'sub')), may hold values from -6 to 6
Outputs:
- basis: float32 [262144, 256], P(('rows', 'sub'))
- factor: float32 [256, 256], replicated
The draws below stay inside these ranges and needn't reach their ends.
Inputs may be any that keep to these rules, and one draw needn't show every extreme that they name: `col_blocks`: in the 128 entries of the rows of one device (16 block rows), at most 2 lie in the range of any one device's 16 block rows; in every draw the range of some device receives exactly 2 from every device.
All inputs are finite; a program needn't handle non-finite values.
Results may differ from the reference program's by a relative error of at most 0.002.
Values may be sent and summed in bfloat16 or wider, within the bound.
A program may use at most 256 MiB of HBM per device.

```python
import jax
import jax.numpy as jnp
from jax import lax

BLOCK = 128
SKETCH = 256
K = 8
BR = 16
DEVICE_TOTAL = 128
MAX_COLUMN_HITS = 2
NB = 2048
ROWS = 262144


def draw_diag_blocks(key, part):
    noise = jax.random.normal(key, (NB, BLOCK, BLOCK), jnp.float32)
    scale_sym = 0.3 / (2.0 * (2.0 * BLOCK) ** 0.5)
    symmetric = (noise + jnp.transpose(noise, (0, 2, 1))) * scale_sym
    position = jnp.arange(NB).astype(jnp.float32) / max(NB - 1, 1)
    level = 1.0 + 2.0 * position
    identity = jnp.eye(BLOCK, dtype=jnp.float32)
    return (identity[None, :, :] * level[:, None, None] + symmetric).astype(jnp.bfloat16)


def draw_col_blocks(key, part):
    key_extra = jax.random.fold_in(key, 11)
    key_hot = jax.random.fold_in(key, 12)
    key_rest = jax.random.fold_in(key, 13)
    target_positions = DEVICE_TOTAL * MAX_COLUMN_HITS
    extra_weight = jax.random.randint(key_extra, (DEVICE_TOTAL,), 0, 4) * target_positions
    busiest_device = jax.random.randint(key_hot, (), 0, DEVICE_TOTAL)
    extra_weight = jnp.where(jnp.arange(DEVICE_TOTAL) == busiest_device, 8 * target_positions, extra_weight)
    extra_positions = jnp.repeat(extra_weight, MAX_COLUMN_HITS)

    def one_device(device):
        device_key = jax.random.fold_in(key_rest, device)
        key_first = jax.random.fold_in(device_key, 1)
        key_two = jax.random.fold_in(device_key, 2)
        key_three = jax.random.fold_in(device_key, 3)
        device_scores = extra_positions + jax.random.permutation(key_first, target_positions)
        unused, chosen = lax.top_k(device_scores, BR * K)
        chosen = chosen[jax.random.permutation(key_two, BR * K)]
        owners = chosen // MAX_COLUMN_HITS
        local = jax.random.randint(key_three, (BR * K,), 0, BR)
        return (owners * BR + local).reshape(BR, K)
    return jax.vmap(one_device)(jnp.arange(DEVICE_TOTAL)).reshape(NB, K).astype(jnp.int32)


def block_levels(own_key, extent, pieces, low, top_value):
    gain, own = 1.0, jax.random.fold_in(own_key, 6)
    for dim, parts in pieces:
        steps = jnp.exp(jax.random.uniform(jax.random.fold_in(own, dim), (parts,), jnp.float32, low / len(pieces), top_value / len(pieces)))
        gain = gain * jnp.repeat(steps, extent[dim] // parts).reshape([-1 if axis == dim else 1 for axis in range(len(extent))])
    return gain


def gaussian(stream_key, extent, scale, reach, pieces=(), kind=jnp.bfloat16):
    gain = block_levels(stream_key, extent, pieces, -0.22, 0.18) if pieces else 1.0
    array = jax.random.normal(stream_key, extent, jnp.float32) * scale * gain
    return jnp.minimum(jnp.maximum(array, -reach), reach).astype(kind)


def setup_inputs(seed: int = 0) -> dict:
    seeds = jax.random.split(jax.random.key(seed), 5)
    return {
        "diag_blocks": draw_diag_blocks(jax.random.fold_in(seeds[4], 71), 0),
        "off_blocks": gaussian(seeds[1], (NB, K, BLOCK, BLOCK), BLOCK ** -0.5, 0.5, ((0, 128),)),
        "col_blocks": draw_col_blocks(jax.random.fold_in(seeds[4], 71), 0),
        "sketch": gaussian(seeds[3], (ROWS, SKETCH), 1.0, 6.0, ((0, 128),)),
    }


def reference(diag_blocks, off_blocks, col_blocks, sketch):
    omega = sketch.reshape(NB, BLOCK, SKETCH)

    def advance(index, image):
        blocks = off_blocks[index].astype(jnp.float32)
        targets = col_blocks[index].astype(jnp.int32)
        here = omega[index].astype(jnp.float32)
        near = jnp.dot(diag_blocks[index].astype(jnp.float32), omega[index].astype(jnp.float32), preferred_element_type=jnp.float32)
        remote = omega[targets].astype(jnp.float32)
        far = jnp.einsum('kij,kjc->ic', blocks, remote)
        mirror = jnp.einsum('kji,jc->kic', blocks, here).astype(jnp.bfloat16)
        mirror = lax.optimization_barrier(mirror).astype(jnp.float32)
        image = image.at[index].add(near + far)
        return image.at[targets].add(mirror)
    image = lax.fori_loop(0, NB, advance, jnp.zeros((NB, BLOCK, SKETCH), jnp.float32))
    image = image.reshape(ROWS, SKETCH)
    gram = jnp.dot(image.T.astype(jnp.float32), image.astype(jnp.float32), precision=lax.Precision.HIGHEST, preferred_element_type=jnp.float32) / ROWS
    lower = jnp.linalg.cholesky(gram)
    basis = lax.linalg.triangular_solve(lower, image, left_side=False, lower=True, transpose_a=True)
    return (basis, lower.T)
```

```python
import functools

import jax
import jax.numpy as jnp
from jax import lax
from jax.experimental import pallas as pl
from jax.experimental.pallas import tpu as pltpu
from jax.sharding import PartitionSpec as P

MESH = pl.DeviceIdType.MESH
HIGHEST = lax.Precision.HIGHEST


def dot(a, b, dims, precision=HIGHEST):
    return lax.dot_general(a, b, (dims, ((), ())), precision=precision, preferred_element_type=jnp.float32)


def factor_half(work, s):
    n = s.shape[0]
    lane = lax.broadcasted_iota(jnp.int32, (n, n), 1)
    sub = lax.broadcasted_iota(jnp.int32, (n, 1), 0)
    lane1 = lax.broadcasted_iota(jnp.int32, (1, n), 1)
    work[:, :n] = s
    work[:, n:] = (lax.broadcasted_iota(jnp.int32, (n, n), 0) == lane).astype(jnp.float32)

    def step(k, carry):
        row = work[pl.ds(k, 1), :]
        full = work[...]
        col = jnp.sum(jnp.where(lane == k, full[:, :n], 0.0), axis=1, keepdims=True)
        pivot = jnp.sum(jnp.where(lane1 == k, row[:, :n], 0.0), axis=1, keepdims=True)
        scale = 1.0 / jnp.sqrt(pivot)
        row = row * scale
        work[...] = full - jnp.where(sub > k, col * scale, 0.0) * row
        work[pl.ds(k, 1), :] = row
        return carry

    lax.fori_loop(0, n, step, 0)
    keep = lax.broadcasted_iota(jnp.int32, (n, n), 0) <= lane
    return jnp.where(keep, work[:, :n], 0.0), work[:, n:]


def finish_kernel(total_rows, image, basis, upper, gram, tiles, landed, summed, work, linv, s1, r1, s2, r2):
    rows, columns = image.shape
    n_rows, n_sub = 32, 4
    r, y = lax.axis_index("rows"), lax.axis_index("sub")
    me = r * n_sub + y
    reducer = r % 2 == 0
    mine = (r // 2) * n_sub + y
    gram[...] = jnp.zeros_like(gram)

    def partial(i, c):
        part = image[pl.ds(pl.multiple_of(i * 256, 256), 256), :]
        gram[...] += dot(part, part, ((0,), (0,)))
        return c

    lax.fori_loop(0, rows // 256, partial, 0)
    for i in range(32):
        for j in range(2):
            tiles[2 * i + j] = gram[8 * i : 8 * i + 8, 128 * j : 128 * j + 128] * (1.0 / total_rows)

    def scatter(i, c):
        t = (mine + i) % 64

        @pl.when(jnp.logical_or(i > 0, r % 2 == 1))
        def _():
            pltpu.make_async_remote_copy(
                src_ref=tiles.at[t], dst_ref=landed.at[me], send_sem=s1, recv_sem=r1,
                device_id=((t // n_sub) * 2, t % n_sub), device_id_type=MESH).start()

        return c

    lax.fori_loop(0, 64, scatter, 0)

    @pl.when(reducer)
    def _():
        landed[me] = tiles[mine]
        pltpu.make_async_copy(landed.at[pl.ds(0, 127)], landed.at[pl.ds(0, 127)], r1).wait()
        summed[mine] = jnp.sum(landed[...], axis=0)

        def spread(i, c):
            d = (me + i) % 128
            pltpu.make_async_remote_copy(
                src_ref=summed.at[mine], dst_ref=summed.at[mine], send_sem=s2, recv_sem=r2,
                device_id=(d // n_sub, d % n_sub), device_id_type=MESH).start()
            return c

        lax.fori_loop(1, 128, spread, 0)
        pltpu.make_async_copy(tiles.at[pl.ds(0, 63)], tiles.at[pl.ds(0, 63)], s1).wait()
        pltpu.make_async_copy(summed.at[pl.ds(0, 63)], summed.at[pl.ds(0, 63)], r2).wait()

    @pl.when(jnp.logical_not(reducer))
    def _():
        pltpu.make_async_copy(tiles, tiles, s1).wait()
        pltpu.make_async_copy(summed, summed, r2).wait()

    for i in range(32):
        for j in range(2):
            gram[8 * i : 8 * i + 8, 128 * j : 128 * j + 128] = summed[2 * i + j]
    r11, i11 = factor_half(work, gram[:128, :128])
    r12 = dot(i11, gram[:128, 128:], ((1,), (0,)))
    upper[:128, :128] = r11
    upper[:128, 128:] = r12
    linv[:128, :128] = i11
    linv[:128, 128:] = jnp.zeros((128, 128), jnp.float32)
    r22, i22 = factor_half(work, gram[128:, 128:] - dot(r12, r12, ((0,), (0,))))
    upper[128:, :128] = jnp.zeros((128, 128), jnp.float32)
    upper[128:, 128:] = r22
    linv[128:, :128] = -dot(i22, dot(r12, i11, ((0,), (0,))), ((1,), (0,)))
    linv[128:, 128:] = i22

    def rows_out(i, c):
        at = pl.ds(pl.multiple_of(i * 256, 256), 256)
        basis[at, :] = dot(image[at, :], linv[...], ((1,), (1,)))
        return c

    lax.fori_loop(0, rows // 256, rows_out, 0)

    @pl.when(reducer)
    def _():
        pltpu.make_async_copy(landed.at[pl.ds(0, 127)], landed.at[pl.ds(0, 127)], s2).wait()


def finish(image, total_rows):
    f32 = jnp.float32
    vmem = pl.BlockSpec(memory_space=pltpu.VMEM)
    return pl.pallas_call(
        functools.partial(finish_kernel, total_rows),
        out_shape=(jax.ShapeDtypeStruct(image.shape, f32), jax.ShapeDtypeStruct((256, 256), f32)),
        in_specs=[vmem],
        out_specs=(vmem, vmem),
        scratch_shapes=[
            pltpu.VMEM((256, 256), f32),
            pltpu.VMEM((64, 8, 128), f32),
            pltpu.VMEM((128, 8, 128), f32),
            pltpu.VMEM((64, 8, 128), f32),
            pltpu.VMEM((128, 256), f32),
            pltpu.VMEM((256, 256), f32),
        ]
        + [pltpu.SemaphoreType.DMA] * 4,
        compiler_params=pltpu.CompilerParams(has_side_effects=True, vmem_limit_bytes=24 << 20),
        name="finish",
    )(image)


def far_kernel(where_ref, off_ref, diag_ref, omega_ref, back_ref, *refs):
    out = refs[-1]
    total = back_ref[0] + dot(diag_ref[0], omega_ref[0], ((1,), (0,)), None)
    for k in range(8):
        total += dot(off_ref[0, k], refs[k][0], ((1,), (0,)), None)
    out[0] = total


def far_image(where_to, off_blocks, diag_blocks, omega, returned, answered):
    def pick(k):
        return pl.BlockSpec((1, 128, 256), lambda b, w: (w[b * 8 + k], 0, 0))

    return pl.pallas_call(
        far_kernel,
        grid_spec=pltpu.PrefetchScalarGridSpec(
            num_scalar_prefetch=1,
            grid=(16,),
            in_specs=[
                pl.BlockSpec((1, 8, 128, 128), lambda b, w: (b, 0, 0, 0)),
                pl.BlockSpec((1, 128, 128), lambda b, w: (b, 0, 0)),
                pl.BlockSpec((1, 128, 256), lambda b, w: (b, 0, 0)),
                pl.BlockSpec((1, 128, 256), lambda b, w: (b, 0, 0)),
            ]
            + [pick(k) for k in range(8)],
            out_specs=pl.BlockSpec((1, 128, 256), lambda b, w: (b, 0, 0)),
        ),
        out_shape=jax.ShapeDtypeStruct((16, 128, 256), jnp.float32),
        compiler_params=pltpu.CompilerParams(vmem_limit_bytes=24 << 20),
        name="far",
    )(where_to, off_blocks, diag_blocks, omega, returned, *([answered] * 8))


def send_out(outgoing, labels):
    received, tags = (
        lax.all_to_all(outgoing, ("rows", "sub"), split_axis=0, concat_axis=0, tiled=True),
        lax.all_to_all(labels, ("rows", "sub"), split_axis=0, concat_axis=0, tiled=True),
    )
    return (received, tags)


def send_back(reply):
    answered = lax.all_to_all(reply, ("rows", "sub"), split_axis=0, concat_axis=0, tiled=True)
    return answered


def on_device(diag_blocks, off_blocks, col_blocks, sketch):
    block_rows, per_row = col_blocks.shape
    edge = diag_blocks.shape[1]
    columns = sketch.shape[1]
    peers = lax.axis_size(("rows", "sub"))
    most = max(2, (2 * block_rows * per_row + peers - 1) // peers)
    requests = block_rows * per_row
    target_positions = peers * most
    flat = col_blocks.reshape(requests)
    owners = flat // block_rows
    local_id = flat % block_rows
    order = jnp.arange(requests)
    earlier = (owners[:, None] == owners[None, :]) & (order[None, :] < order[:, None])
    ranks = jnp.sum(earlier.astype(jnp.int32), axis=1)
    where_to = owners * most + ranks
    omega = sketch.reshape(block_rows, edge, columns)
    mirror = jnp.einsum("bkji,bjc->bkic", off_blocks, omega, preferred_element_type=jnp.float32)
    mirror = mirror.astype(jnp.bfloat16).reshape(requests, edge, columns)
    outgoing = jnp.zeros((target_positions, edge, columns), jnp.bfloat16).at[where_to].set(mirror)
    labels = (
        jnp.full((target_positions,), -1.0, jnp.float32)
        .at[where_to]
        .set(local_id.astype(jnp.float32))
    )
    labels = labels.astype(jnp.bfloat16)
    received, tags = send_out(
        outgoing.reshape(peers, most, edge, columns), labels.reshape(peers, most)
    )
    selector = (
        tags.reshape(target_positions).astype(jnp.int32)[None, :] == jnp.arange(block_rows)[:, None]
    ).astype(jnp.bfloat16)
    returned = jnp.dot(
        selector,
        received.reshape(target_positions, edge * columns),
        preferred_element_type=jnp.float32,
    )
    returned = returned.reshape(block_rows, edge, columns)
    reply = jnp.einsum(
        "rs,rk->sk",
        selector,
        omega.reshape(block_rows, edge * columns),
        preferred_element_type=jnp.float32,
    )
    reply = reply.astype(jnp.bfloat16).reshape(peers, most, edge, columns)
    answered = send_back(reply).reshape(target_positions, edge, columns)
    image = far_image(where_to, off_blocks, diag_blocks, omega, returned, answered)
    image = image.reshape(block_rows * edge, columns)
    total_rows = block_rows * edge * peers
    return finish(image, total_rows)


def solution(mesh):
    placed = (
        P(("rows", "sub"), None, None),
        P(("rows", "sub"), None, None, None),
        P(("rows", "sub"), None),
        P(("rows", "sub"), None),
    )
    return jax.shard_map(
        on_device,
        mesh=mesh,
        in_specs=placed,
        out_specs=(P(("rows", "sub"), None), P()),
        check_vma=False,
    )
```

```python
import functools

import jax
import jax.numpy as jnp
from jax import lax
from jax.experimental import pallas as pl
from jax.experimental.pallas import tpu as pltpu
from jax.sharding import PartitionSpec as P

MESH = pl.DeviceIdType.MESH
HIGHEST = lax.Precision.HIGHEST


def dot(a, b, dims, precision=HIGHEST):
    return lax.dot_general(a, b, (dims, ((), ())), precision=precision, preferred_element_type=jnp.float32)


def factor_half(work, s):
    n = s.shape[0]
    lane = lax.broadcasted_iota(jnp.int32, (n, n), 1)
    sub = lax.broadcasted_iota(jnp.int32, (n, 1), 0)
    lane1 = lax.broadcasted_iota(jnp.int32, (1, n), 1)
    work[:, :n] = s
    work[:, n:] = (lax.broadcasted_iota(jnp.int32, (n, n), 0) == lane).astype(jnp.float32)

    def step(k, carry):
        row = work[pl.ds(k, 1), :]
        full = work[...]
        col = jnp.sum(jnp.where(lane == k, full[:, :n], 0.0), axis=1, keepdims=True)
        pivot = jnp.sum(jnp.where(lane1 == k, row[:, :n], 0.0), axis=1, keepdims=True)
        scale = 1.0 / jnp.sqrt(pivot)
        row = row * scale
        work[...] = full - jnp.where(sub > k, col * scale, 0.0) * row
        work[pl.ds(k, 1), :] = row
        return carry

    lax.fori_loop(0, n, step, 0)
    keep = lax.broadcasted_iota(jnp.int32, (n, n), 0) <= lane
    return jnp.where(keep, work[:, :n], 0.0), work[:, n:]


def finish_kernel(total_rows, image, basis, upper, gram, tiles, landed, summed, work, linv, s1, r1, s2, r2):
    rows, columns = image.shape
    n_rows, n_sub = 32, 4
    r, y = lax.axis_index("rows"), lax.axis_index("sub")
    me = r * n_sub + y
    reducer = r % 2 == 0
    mine = (r // 2) * n_sub + y
    gram[...] = jnp.zeros_like(gram)

    def partial(i, c):
        part = image[pl.ds(pl.multiple_of(i * 256, 256), 256), :]
        gram[...] += dot(part, part, ((0,), (0,)))
        return c

    lax.fori_loop(0, rows // 256, partial, 0)
    for i in range(32):
        for j in range(2):
            tiles[2 * i + j] = gram[8 * i : 8 * i + 8, 128 * j : 128 * j + 128] * (1.0 / total_rows)

    def scatter(i, c):
        t = (mine + i) % 64

        @pl.when(jnp.logical_or(i > 0, r % 2 == 1))
        def _():
            pltpu.make_async_remote_copy(
                src_ref=tiles.at[t], dst_ref=landed.at[me], send_sem=s1, recv_sem=r1,
                device_id=((t // n_sub) * 2, t % n_sub), device_id_type=MESH).start()

        return c

    lax.fori_loop(0, 64, scatter, 0)

    @pl.when(reducer)
    def _():
        landed[me] = tiles[mine]
        pltpu.make_async_copy(landed.at[pl.ds(0, 127)], landed.at[pl.ds(0, 127)], r1).wait()
        summed[mine] = jnp.sum(landed[...], axis=0)

        def spread(i, c):
            d = (me + i) % 128
            pltpu.make_async_remote_copy(
                src_ref=summed.at[mine], dst_ref=summed.at[mine], send_sem=s2, recv_sem=r2,
                device_id=(d // n_sub, d % n_sub), device_id_type=MESH).start()
            return c

        lax.fori_loop(1, 128, spread, 0)
        pltpu.make_async_copy(tiles.at[pl.ds(0, 63)], tiles.at[pl.ds(0, 63)], s1).wait()
        pltpu.make_async_copy(summed.at[pl.ds(0, 63)], summed.at[pl.ds(0, 63)], r2).wait()

    @pl.when(jnp.logical_not(reducer))
    def _():
        pltpu.make_async_copy(tiles, tiles, s1).wait()
        pltpu.make_async_copy(summed, summed, r2).wait()

    for i in range(32):
        for j in range(2):
            gram[8 * i : 8 * i + 8, 128 * j : 128 * j + 128] = summed[2 * i + j]
    r11, i11 = factor_half(work, gram[:128, :128])
    r12 = dot(i11, gram[:128, 128:], ((1,), (0,)))
    upper[:128, :128] = r11
    upper[:128, 128:] = r12
    linv[:128, :128] = i11
    linv[:128, 128:] = jnp.zeros((128, 128), jnp.float32)
    r22, i22 = factor_half(work, gram[128:, 128:] - dot(r12, r12, ((0,), (0,))))
    upper[128:, :128] = jnp.zeros((128, 128), jnp.float32)
    upper[128:, 128:] = r22
    linv[128:, :128] = -dot(i22, dot(r12, i11, ((0,), (0,))), ((1,), (0,)))
    linv[128:, 128:] = i22

    def rows_out(i, c):
        at = pl.ds(pl.multiple_of(i * 256, 256), 256)
        basis[at, :] = dot(image[at, :], linv[...], ((1,), (1,)))
        return c

    lax.fori_loop(0, rows // 256, rows_out, 0)

    @pl.when(reducer)
    def _():
        pltpu.make_async_copy(landed.at[pl.ds(0, 127)], landed.at[pl.ds(0, 127)], s2).wait()


def place():
    r, y = lax.axis_index("rows"), lax.axis_index("sub")
    return r // 8, y, (r // 2) % 4, r % 2


def remote(src, dst, sems, k, x, y, z, c):
    send, recv = sems
    return pltpu.make_async_remote_copy(
        src_ref=src, dst_ref=dst, send_sem=send.at[k], recv_sem=recv.at[k],
        device_id=((x % 4) * 8 + (z % 4) * 2 + c % 2, y % 4), device_id_type=MESH)


def line_offsets():
    return [(i, d) for i in range(4) for d in range(2) if (i, d) != (0, 0)]


def gather_kernel(packed, sketch, meta, blocks, line, plane, metas, send, recv, local):
    x, y, z, c = place()
    sems = (send, recv)
    a, b = x * (1 - c) + z * c, z * (1 - c) + x * c
    me = y * 2 + c
    own_q = a * 4 + b

    def along(i, j):
        return x + (1 - c) * i + c * j, y, z + c * i + (1 - c) * j, c

    keep = [
        pltpu.make_async_copy(sketch, plane.at[own_q], local.at[0]),
        pltpu.make_async_copy(sketch, line.at[me], local.at[1]),
        pltpu.make_async_copy(packed.at[me], blocks.at[me], local.at[2]),
        pltpu.make_async_copy(meta, metas.at[me], local.at[3]),
    ]
    first = [remote(sketch, plane.at[own_q], sems, i - 1, *along(i, 0)) for i in range(1, 4)]
    same = [remote(sketch, line.at[me], sems, 14 + i, x, y + i, z, c) for i in range(1, 4)]
    mate = [remote(sketch, line.at[me], sems, 18, x, y, z, c + 1)]
    second = [[remote(sketch, plane.at[own_q], sems, 2 + j, *along(0, j)) for j in range(1, 4)]]
    for i in range(1, 4):
        q = ((a + 4 - i) % 4) * 4 + b
        second.append([remote(plane.at[q], plane.at[q], sems, 2 + 3 * i + j, *along(0, j)) for j in range(1, 4)])
        l = ((y + 4 - i) % 4) * 2 + c
        mate.append(remote(line.at[l], line.at[l], sems, 18 + i, x, y, z, c + 1))
    across, labels = [], []
    for n, (i, d) in enumerate(line_offsets()):
        to = ((y + i) % 4) * 2 + (c + d) % 2
        across.append(remote(packed.at[to], blocks.at[me], sems, 22 + n, x, y + i, z, c + d))
        labels.append(remote(meta, metas.at[me], sems, 29 + n, x, y + i, z, c + d))
    for cp in labels + first + same + second[0] + across + mate[:1] + keep:
        cp.start()
    for i in range(1, 4):
        first[i - 1].wait_recv()
        for cp in second[i]:
            cp.start()
        same[i - 1].wait_recv()
        mate[i].start()
    for cp in first + same:
        cp.wait_send()
    for cp in labels + across + mate + [cp for group in second for cp in group] + keep:
        cp.wait()


def gather_all(packed, sketch, meta):
    anyspec = pl.BlockSpec(memory_space=pl.ANY)
    bf16 = jnp.bfloat16
    return pl.pallas_call(
        gather_kernel,
        out_shape=(
            jax.ShapeDtypeStruct((8, 32, 128, 128), bf16),
            jax.ShapeDtypeStruct((8, 2048, 256), bf16),
            jax.ShapeDtypeStruct((16, 2048, 256), bf16),
            jax.ShapeDtypeStruct((8, 8, 128), jnp.int32),
        ),
        in_specs=[anyspec] * 3,
        out_specs=(anyspec,) * 4,
        scratch_shapes=[pltpu.SemaphoreType.DMA((36,)), pltpu.SemaphoreType.DMA((36,)), pltpu.SemaphoreType.DMA((4,))],
        compiler_params=pltpu.CompilerParams(has_side_effects=True),
        name="gather",
    )(packed, sketch, meta)


def pack_kernel(slot, off, packed, sem):
    def go(e, carry):
        pltpu.make_async_copy(off.at[e], packed.at[slot[e]], sem).start()
        return carry

    lax.fori_loop(0, 128, go, 0)
    pltpu.make_async_copy(off, off, sem).wait()


def pack(slot, off):
    return pl.pallas_call(
        pack_kernel,
        out_shape=jax.ShapeDtypeStruct((256, 128, 128), jnp.bfloat16),
        in_specs=[pl.BlockSpec(memory_space=pltpu.SMEM), pl.BlockSpec(memory_space=pl.ANY)],
        out_specs=pl.BlockSpec(memory_space=pl.ANY),
        scratch_shapes=[pltpu.SemaphoreType.DMA],
        name="pack",
    )(slot, off)


def product_kernel(count, row, col, blocks, line, plane, far, mirrors, acc, sums, stage, sem):
    s = pl.program_id(0)

    @pl.when(s == 0)
    def _():
        def clear(i, carry):
            sums[i] = jnp.zeros((128, 256), jnp.float32)
            return carry

        lax.fori_loop(0, 256, clear, 0)

    acc[...] = jnp.zeros_like(acc)

    def one(t, carry):
        r, q = row[s * 32 + t], col[s * 32 + t]
        block = blocks[0, t]
        acc[r] += dot(block, plane[q], ((1,), (0,)), None)
        mirror = dot(block, line[0, r], ((0,), (0,)), None).astype(jnp.bfloat16)
        sums[q] += mirror.astype(jnp.float32)
        return carry

    lax.fori_loop(0, count[s], one, 0)
    far[0] = acc[...].astype(jnp.bfloat16)

    @pl.when(s == 7)
    def _():
        for n in range(16):
            if n >= 2:
                pltpu.make_async_copy(stage.at[n % 2], mirrors.at[pl.ds(16 * (n - 2), 16)], sem.at[n % 2]).wait()

            def out(i, carry):
                stage[n % 2, i] = sums[16 * n + i].astype(jnp.bfloat16)
                return carry

            lax.fori_loop(0, 16, out, 0)
            pltpu.make_async_copy(stage.at[n % 2], mirrors.at[pl.ds(16 * n, 16)], sem.at[n % 2]).start()
        for n in (14, 15):
            pltpu.make_async_copy(stage.at[n % 2], mirrors.at[pl.ds(16 * n, 16)], sem.at[n % 2]).wait()


def products(count, row, col, blocks, line, plane):
    bf16 = jnp.bfloat16
    return pl.pallas_call(
        product_kernel,
        grid_spec=pltpu.PrefetchScalarGridSpec(
            num_scalar_prefetch=3,
            grid=(8,),
            in_specs=[
                pl.BlockSpec((1, 32, 128, 128), lambda s, *_: (s, 0, 0, 0)),
                pl.BlockSpec((1, 16, 128, 256), lambda s, *_: (s, 0, 0, 0)),
                pl.BlockSpec((256, 128, 256), lambda s, *_: (0, 0, 0), pipeline_mode=pl.Buffered(1)),
            ],
            out_specs=(
                pl.BlockSpec((1, 16, 128, 256), lambda s, *_: (s, 0, 0, 0)),
                pl.BlockSpec(memory_space=pl.ANY),
            ),
            scratch_shapes=[
                pltpu.VMEM((16, 128, 256), jnp.float32),
                pltpu.VMEM((256, 128, 256), jnp.float32),
                pltpu.VMEM((2, 16, 128, 256), bf16),
                pltpu.SemaphoreType.DMA((2,)),
            ],
        ),
        out_shape=(
            jax.ShapeDtypeStruct((8, 16, 128, 256), bf16),
            jax.ShapeDtypeStruct((256, 128, 256), bf16),
        ),
        compiler_params=pltpu.CompilerParams(vmem_limit_bytes=60 << 20),
        name="products",
    )(count, row, col, blocks, line, plane)


def combine_kernel(total_rows, diag, sketch, far, mirrors, basis, upper,
                   image, own, one, sums, two, back, gram, tiles, landed, summed, work, linv,
                   send, recv, local, s1, r1, s2, r2):
    f32 = jnp.float32
    x, y, z, c = place()
    sems = (send, recv)
    a, b = x * (1 - c) + z * c, z * (1 - c) + x * c
    me = y * 2 + c

    def along(i, j):
        return x + (1 - c) * i + c * j, y, z + c * i + (1 - c) * j, c

    order = (1, 2, 3, 0)
    first = {}
    for t in order:
        for i in range(1, 4):
            q = ((a + i) % 4) * 4 + (b + t) % 4
            first[i, t] = remote(mirrors.at[q], one.at[i - 1, t], sems, 3 * t + i - 1, *along(i, 0))
    lines = []
    for n, (i, d) in enumerate(line_offsets()):
        to = ((y + i) % 4) * 2 + (c + d) % 2
        lines.append(remote(far.at[to], back.at[n + 1], sems, 12 + n, x, y + i, z, c + d))
    keep = [pltpu.make_async_copy(mirrors.at[a * 4 + (b + t) % 4], own.at[t], local.at[t]) for t in range(4)]
    keep.append(pltpu.make_async_copy(far.at[me], back.at[0], local.at[4]))
    second = [remote(sums.at[t - 1], two.at[t - 1], sems, 18 + t, *along(0, t)) for t in range(1, 4)]
    for t in order:
        for i in (1, 3, 2):
            first[i, t].start()
        if t == 1:
            for cp in lines:
                cp.start()
    for cp in keep:
        cp.start()

    def near(i, carry):
        at = pl.ds(pl.multiple_of(i * 128, 128), 128)
        image[at, :] = dot(diag[i], sketch[at, :], ((1,), (0,)), None)
        return carry

    lax.fori_loop(0, 16, near, 0)
    for t in order:
        keep[t].wait()
        for i in range(1, 4):
            first[i, t].wait_recv()

        def add(i, carry):
            at = pl.ds(pl.multiple_of(i * 128, 128), 128)
            total = own[t, at, :].astype(f32) + one[0, t, at, :].astype(f32)
            total += one[1, t, at, :].astype(f32) + one[2, t, at, :].astype(f32)
            if t:
                sums[t - 1, at, :] = total.astype(jnp.bfloat16)
            else:
                image[at, :] += total
            return carry

        lax.fori_loop(0, 16, add, 0)
        if t:
            second[t - 1].start()
    keep[4].wait()
    for cp in lines:
        cp.wait_recv()

    def add_far(i, carry):
        at = pl.ds(pl.multiple_of(i * 128, 128), 128)
        total = image[at, :]
        for n in range(8):
            total += back[n, at, :].astype(f32)
        image[at, :] = total
        return carry

    lax.fori_loop(0, 16, add_far, 0)
    for cp in second:
        cp.wait_recv()

    def add_two(i, carry):
        at = pl.ds(pl.multiple_of(i * 128, 128), 128)
        image[at, :] += two[0, at, :].astype(f32) + two[1, at, :].astype(f32) + two[2, at, :].astype(f32)
        return carry

    lax.fori_loop(0, 16, add_two, 0)
    for cp in list(first.values()) + lines + second:
        cp.wait_send()
    finish_kernel(total_rows, image, basis, upper, gram, tiles, landed, summed, work, linv, s1, r1, s2, r2)


def combine(total_rows, diag, sketch, far, mirrors):
    f32, bf16 = jnp.float32, jnp.bfloat16
    vmem = pl.BlockSpec(memory_space=pltpu.VMEM)
    anyspec = pl.BlockSpec(memory_space=pl.ANY)
    return pl.pallas_call(
        functools.partial(combine_kernel, total_rows),
        out_shape=(jax.ShapeDtypeStruct((2048, 256), f32), jax.ShapeDtypeStruct((256, 256), f32)),
        in_specs=[vmem, vmem, anyspec, anyspec],
        out_specs=(vmem, vmem),
        scratch_shapes=[
            pltpu.VMEM((2048, 256), f32),
            pltpu.VMEM((4, 2048, 256), bf16),
            pltpu.VMEM((3, 4, 2048, 256), bf16),
            pltpu.VMEM((3, 2048, 256), bf16),
            pltpu.VMEM((3, 2048, 256), bf16),
            pltpu.VMEM((8, 2048, 256), bf16),
            pltpu.VMEM((256, 256), f32),
            pltpu.VMEM((64, 8, 128), f32),
            pltpu.VMEM((128, 8, 128), f32),
            pltpu.VMEM((64, 8, 128), f32),
            pltpu.VMEM((128, 256), f32),
            pltpu.VMEM((256, 256), f32),
            pltpu.SemaphoreType.DMA((22,)),
            pltpu.SemaphoreType.DMA((22,)),
            pltpu.SemaphoreType.DMA((5,)),
        ]
        + [pltpu.SemaphoreType.DMA] * 4,
        compiler_params=pltpu.CompilerParams(has_side_effects=True, vmem_limit_bytes=48 << 20),
        name="combine",
    )(diag, sketch, far, mirrors)


def split_owner(col):
    owner = col // 16
    r, y = owner // 4, owner % 4
    c = r % 2
    x, z = r // 8, (r // 2) % 4
    a, b = jnp.where(c == 0, x, z), jnp.where(c == 0, z, x)
    return y * 2 + c, (a * 4 + b) * 16 + col % 16


def on_device(diag_blocks, off_blocks, col_blocks, sketch):
    entries = 128
    flat = col_blocks.reshape(entries)
    order = jnp.arange(entries)
    before = order[None, :] < order[:, None]
    group, _ = split_owner(flat)
    rank = jnp.sum(((group[:, None] == group[None, :]) & before).astype(jnp.int32), axis=1)
    packed = pack(group * 32 + rank, off_blocks.reshape(entries, 128, 128))
    meta = jnp.broadcast_to(flat[None, :], (8, entries))
    blocks, line, plane, metas = gather_all(packed.reshape(8, 32, 128, 128), sketch, meta)
    mine = lax.axis_index("sub") * 2 + lax.axis_index("rows") % 2
    group, spot = split_owner(metas[:, 0, :])
    hit = group == mine
    rank = jnp.sum((hit[:, None, :] & before[None]).astype(jnp.int32), axis=2)
    chosen = (hit[:, None, :] & (rank[:, None, :] == jnp.arange(32)[None, :, None])).astype(jnp.int32)
    row = jnp.sum(chosen * (order // 8)[None, None, :], axis=2).reshape(256)
    col = jnp.sum(chosen * spot[:, None, :], axis=2).reshape(256)
    count = jnp.sum(hit.astype(jnp.int32), axis=1)
    far, mirrors = products(
        count, row, col, blocks, line.reshape(8, 16, 128, 256), plane.reshape(256, 128, 256)
    )
    return combine(262144, diag_blocks, sketch, far.reshape(8, 2048, 256), mirrors.reshape(16, 2048, 256))


def solution(mesh):
    placed = (
        P(("rows", "sub"), None, None),
        P(("rows", "sub"), None, None, None),
        P(("rows", "sub"), None),
        P(("rows", "sub"), None),
    )
    return jax.shard_map(
        on_device,
        mesh=mesh,
        in_specs=placed,
        out_specs=(P(("rows", "sub"), None), P()),
        check_vma=False,
    )
```

```python
import functools

import jax
import jax.numpy as jnp
from jax import lax
from jax.experimental import pallas as pl
from jax.experimental.pallas import tpu as pltpu
from jax.sharding import PartitionSpec as P

MESH = pl.DeviceIdType.MESH
HIGHEST = lax.Precision.HIGHEST


def dot(a, b, dims, precision=HIGHEST):
    return lax.dot_general(a, b, (dims, ((), ())), precision=precision, preferred_element_type=jnp.float32)


def factor_half(work, s):
    n = s.shape[0]
    lane = lax.broadcasted_iota(jnp.int32, (n, n), 1)
    sub = lax.broadcasted_iota(jnp.int32, (n, 1), 0)
    lane1 = lax.broadcasted_iota(jnp.int32, (1, n), 1)
    work[:, :n] = s
    work[:, n:] = (lax.broadcasted_iota(jnp.int32, (n, n), 0) == lane).astype(jnp.float32)

    def step(k, carry):
        row = work[pl.ds(k, 1), :]
        full = work[...]
        col = jnp.sum(jnp.where(lane == k, full[:, :n], 0.0), axis=1, keepdims=True)
        pivot = jnp.sum(jnp.where(lane1 == k, row[:, :n], 0.0), axis=1, keepdims=True)
        scale = 1.0 / jnp.sqrt(pivot)
        row = row * scale
        work[...] = full - jnp.where(sub > k, col * scale, 0.0) * row
        work[pl.ds(k, 1), :] = row
        return carry

    lax.fori_loop(0, n, step, 0)
    keep = lax.broadcasted_iota(jnp.int32, (n, n), 0) <= lane
    return jnp.where(keep, work[:, :n], 0.0), work[:, n:]


def finish_kernel(total_rows, image, basis, upper, gram, tiles, landed, summed, work, linv, s1, r1, s2, r2):
    rows, columns = image.shape
    n_rows, n_sub = 32, 4
    r, y = lax.axis_index("rows"), lax.axis_index("sub")
    me = r * n_sub + y
    reducer = r % 2 == 0
    mine = (r // 2) * n_sub + y
    gram[...] = jnp.zeros_like(gram)

    def partial(i, c):
        part = image[pl.ds(pl.multiple_of(i * 256, 256), 256), :]
        gram[...] += dot(part, part, ((0,), (0,)))
        return c

    lax.fori_loop(0, rows // 256, partial, 0)
    for i in range(32):
        for j in range(2):
            tiles[2 * i + j] = gram[8 * i : 8 * i + 8, 128 * j : 128 * j + 128] * (1.0 / total_rows)

    def scatter(i, c):
        t = (mine + i) % 64

        @pl.when(jnp.logical_or(i > 0, r % 2 == 1))
        def _():
            pltpu.make_async_remote_copy(
                src_ref=tiles.at[t], dst_ref=landed.at[me], send_sem=s1, recv_sem=r1,
                device_id=((t // n_sub) * 2, t % n_sub), device_id_type=MESH).start()

        return c

    lax.fori_loop(0, 64, scatter, 0)

    @pl.when(reducer)
    def _():
        landed[me] = tiles[mine]
        pltpu.make_async_copy(landed.at[pl.ds(0, 127)], landed.at[pl.ds(0, 127)], r1).wait()
        summed[mine] = jnp.sum(landed[...], axis=0)

        def spread(i, c):
            d = (me + i) % 128
            pltpu.make_async_remote_copy(
                src_ref=summed.at[mine], dst_ref=summed.at[mine], send_sem=s2, recv_sem=r2,
                device_id=(d // n_sub, d % n_sub), device_id_type=MESH).start()
            return c

        lax.fori_loop(1, 128, spread, 0)
        pltpu.make_async_copy(tiles.at[pl.ds(0, 63)], tiles.at[pl.ds(0, 63)], s1).wait()
        pltpu.make_async_copy(summed.at[pl.ds(0, 63)], summed.at[pl.ds(0, 63)], r2).wait()

    @pl.when(jnp.logical_not(reducer))
    def _():
        pltpu.make_async_copy(tiles, tiles, s1).wait()
        pltpu.make_async_copy(summed, summed, r2).wait()

    for i in range(32):
        for j in range(2):
            gram[8 * i : 8 * i + 8, 128 * j : 128 * j + 128] = summed[2 * i + j]
    r11, i11 = factor_half(work, gram[:128, :128])
    r12 = dot(i11, gram[:128, 128:], ((1,), (0,)))
    upper[:128, :128] = r11
    upper[:128, 128:] = r12
    linv[:128, :128] = i11
    linv[:128, 128:] = jnp.zeros((128, 128), jnp.float32)
    r22, i22 = factor_half(work, gram[128:, 128:] - dot(r12, r12, ((0,), (0,))))
    upper[128:, :128] = jnp.zeros((128, 128), jnp.float32)
    upper[128:, 128:] = r22
    linv[128:, :128] = -dot(i22, dot(r12, i11, ((0,), (0,))), ((1,), (0,)))
    linv[128:, 128:] = i22

    def rows_out(i, c):
        at = pl.ds(pl.multiple_of(i * 256, 256), 256)
        basis[at, :] = dot(image[at, :], linv[...], ((1,), (1,)))
        return c

    lax.fori_loop(0, rows // 256, rows_out, 0)

    @pl.when(reducer)
    def _():
        pltpu.make_async_copy(landed.at[pl.ds(0, 127)], landed.at[pl.ds(0, 127)], s2).wait()


def place():
    r, y = lax.axis_index("rows"), lax.axis_index("sub")
    return r // 8, y, (r // 2) % 4, r % 2


def remote(src, dst, sems, k, x, y, z, c):
    send, recv = sems
    return pltpu.make_async_remote_copy(
        src_ref=src, dst_ref=dst, send_sem=send.at[k], recv_sem=recv.at[k],
        device_id=((x % 4) * 8 + (z % 4) * 2 + c % 2, y % 4), device_id_type=MESH)


def line_offsets():
    return [(i, d) for i in range(4) for d in range(2) if (i, d) != (0, 0)]


def gather_kernel(packed, sketch, meta, blocks, line, plane, metas, send, recv, local):
    x, y, z, c = place()
    sems = (send, recv)
    a, b = x * (1 - c) + z * c, z * (1 - c) + x * c
    me = y * 2 + c
    own_q = a * 4 + b

    def along(i, j):
        return x + (1 - c) * i + c * j, y, z + c * i + (1 - c) * j, c

    keep = [
        pltpu.make_async_copy(sketch, plane.at[own_q], local.at[0]),
        pltpu.make_async_copy(sketch, line.at[me], local.at[1]),
        pltpu.make_async_copy(packed.at[me], blocks.at[me], local.at[2]),
        pltpu.make_async_copy(meta, metas.at[me], local.at[3]),
    ]
    first = [remote(sketch, plane.at[own_q], sems, i - 1, *along(i, 0)) for i in range(1, 4)]
    same = [remote(sketch, line.at[me], sems, 14 + i, x, y + i, z, c) for i in range(1, 4)]
    mate = [remote(sketch, line.at[me], sems, 18, x, y, z, c + 1)]
    second = [[remote(sketch, plane.at[own_q], sems, 2 + j, *along(0, j)) for j in range(1, 4)]]
    for i in range(1, 4):
        q = ((a + 4 - i) % 4) * 4 + b
        second.append([remote(plane.at[q], plane.at[q], sems, 2 + 3 * i + j, *along(0, j)) for j in range(1, 4)])
        l = ((y + 4 - i) % 4) * 2 + c
        mate.append(remote(line.at[l], line.at[l], sems, 18 + i, x, y, z, c + 1))
    across, labels = [], []
    for n, (i, d) in enumerate(line_offsets()):
        to = ((y + i) % 4) * 2 + (c + d) % 2
        across.append(remote(packed.at[to], blocks.at[me], sems, 22 + n, x, y + i, z, c + d))
        labels.append(remote(meta, metas.at[me], sems, 29 + n, x, y + i, z, c + d))
    for cp in labels + first + same + second[0] + across + mate[:1] + keep:
        cp.start()
    for i in range(1, 4):
        first[i - 1].wait_recv()
        for cp in second[i]:
            cp.start()
        same[i - 1].wait_recv()
        mate[i].start()
    for cp in first + same:
        cp.wait_send()
    for cp in labels + across + mate + [cp for group in second for cp in group] + keep:
        cp.wait()


def gather_all(packed, sketch, meta):
    anyspec = pl.BlockSpec(memory_space=pl.ANY)
    bf16 = jnp.bfloat16
    return pl.pallas_call(
        gather_kernel,
        out_shape=(
            jax.ShapeDtypeStruct((8, 32, 128, 128), bf16),
            jax.ShapeDtypeStruct((8, 2048, 256), bf16),
            jax.ShapeDtypeStruct((16, 2048, 256), bf16),
            jax.ShapeDtypeStruct((8, 8, 128), jnp.int32),
        ),
        in_specs=[anyspec] * 3,
        out_specs=(anyspec,) * 4,
        scratch_shapes=[pltpu.SemaphoreType.DMA((36,)), pltpu.SemaphoreType.DMA((36,)), pltpu.SemaphoreType.DMA((4,))],
        compiler_params=pltpu.CompilerParams(has_side_effects=True),
        name="gather",
    )(packed, sketch, meta)


def pack_kernel(slot, off, packed):
    def clear(i, carry):
        packed[i] = jnp.zeros((128, 128), jnp.bfloat16)
        return carry

    lax.fori_loop(0, 256, clear, 0, unroll=8)

    def go(e, carry):
        packed[slot[e]] = off[e]
        return carry

    lax.fori_loop(0, 128, go, 0, unroll=4)


def pack(slot, off):
    vmem = pl.BlockSpec(memory_space=pltpu.VMEM)
    return pl.pallas_call(
        pack_kernel,
        out_shape=jax.ShapeDtypeStruct((256, 128, 128), jnp.bfloat16),
        in_specs=[pl.BlockSpec(memory_space=pltpu.SMEM), vmem],
        out_specs=vmem,
        compiler_params=pltpu.CompilerParams(vmem_limit_bytes=16 << 20),
        name="pack",
    )(slot, off)


def product_kernel(count, row, col, blocks, line, plane, far, mirrors, acc, sums, stage, sem):
    s = pl.program_id(0)

    @pl.when(s == 0)
    def _():
        def clear(i, carry):
            sums[i] = jnp.zeros((128, 256), jnp.float32)
            return carry

        lax.fori_loop(0, 256, clear, 0)

    acc[...] = jnp.zeros_like(acc)

    def four(g, carry):
        at = [s * 32 + g * 4 + u for u in range(4)]
        rows, cols = [row[t] for t in at], [col[t] for t in at]
        given = [blocks[0, g * 4 + u] for u in range(4)]
        fars = [dot(given[u], plane[cols[u]], ((1,), (0,)), None) for u in range(4)]
        backs = [dot(given[u], line[0, rows[u]], ((0,), (0,)), None) for u in range(4)]
        for u in range(4):
            acc[rows[u]] += fars[u]
            sums[cols[u]] += backs[u].astype(jnp.bfloat16).astype(jnp.float32)
        return carry

    lax.fori_loop(0, (count[s] + 3) // 4, four, 0)
    far[0] = acc[...].astype(jnp.bfloat16)

    @pl.when(s == 7)
    def _():
        for n in range(16):
            if n >= 2:
                pltpu.make_async_copy(stage.at[n % 2], mirrors.at[pl.ds(16 * (n - 2), 16)], sem.at[n % 2]).wait()

            def out(i, carry):
                stage[n % 2, i] = sums[16 * n + i].astype(jnp.bfloat16)
                return carry

            lax.fori_loop(0, 16, out, 0)
            pltpu.make_async_copy(stage.at[n % 2], mirrors.at[pl.ds(16 * n, 16)], sem.at[n % 2]).start()
        for n in (14, 15):
            pltpu.make_async_copy(stage.at[n % 2], mirrors.at[pl.ds(16 * n, 16)], sem.at[n % 2]).wait()


def products(count, row, col, blocks, line, plane):
    bf16 = jnp.bfloat16
    return pl.pallas_call(
        product_kernel,
        grid_spec=pltpu.PrefetchScalarGridSpec(
            num_scalar_prefetch=3,
            grid=(8,),
            in_specs=[
                pl.BlockSpec((1, 32, 128, 128), lambda s, *_: (s, 0, 0, 0)),
                pl.BlockSpec((1, 16, 128, 256), lambda s, *_: (s, 0, 0, 0)),
                pl.BlockSpec((256, 128, 256), lambda s, *_: (0, 0, 0), pipeline_mode=pl.Buffered(1)),
            ],
            out_specs=(
                pl.BlockSpec((1, 16, 128, 256), lambda s, *_: (s, 0, 0, 0)),
                pl.BlockSpec(memory_space=pl.ANY),
            ),
            scratch_shapes=[
                pltpu.VMEM((16, 128, 256), jnp.float32),
                pltpu.VMEM((256, 128, 256), jnp.float32),
                pltpu.VMEM((2, 16, 128, 256), bf16),
                pltpu.SemaphoreType.DMA((2,)),
            ],
        ),
        out_shape=(
            jax.ShapeDtypeStruct((8, 16, 128, 256), bf16),
            jax.ShapeDtypeStruct((256, 128, 256), bf16),
        ),
        compiler_params=pltpu.CompilerParams(vmem_limit_bytes=60 << 20),
        name="products",
    )(count, row, col, blocks, line, plane)


def combine_kernel(total_rows, diag, sketch, far, mirrors, basis, upper,
                   image, own, one, sums, two, back, gram, tiles, landed, summed, work, linv,
                   send, recv, local, s1, r1, s2, r2):
    f32 = jnp.float32
    x, y, z, c = place()
    sems = (send, recv)
    a, b = x * (1 - c) + z * c, z * (1 - c) + x * c
    me = y * 2 + c

    def along(i, j):
        return x + (1 - c) * i + c * j, y, z + c * i + (1 - c) * j, c

    order = (1, 2, 3, 0)
    first = {}
    for t in order:
        for i in range(1, 4):
            q = ((a + i) % 4) * 4 + (b + t) % 4
            first[i, t] = remote(mirrors.at[q], one.at[i - 1, t], sems, 3 * t + i - 1, *along(i, 0))
    lines = []
    for n, (i, d) in enumerate(line_offsets()):
        to = ((y + i) % 4) * 2 + (c + d) % 2
        lines.append(remote(far.at[to], back.at[n + 1], sems, 12 + n, x, y + i, z, c + d))
    keep = [pltpu.make_async_copy(mirrors.at[a * 4 + (b + t) % 4], own.at[t], local.at[t]) for t in range(4)]
    keep.append(pltpu.make_async_copy(far.at[me], back.at[0], local.at[4]))
    second = [remote(sums.at[t - 1], two.at[t - 1], sems, 18 + t, *along(0, t)) for t in range(1, 4)]
    for t in order:
        for i in (1, 3, 2):
            first[i, t].start()
        if t == 1:
            for cp in lines:
                cp.start()
    for cp in keep:
        cp.start()

    def near(i, carry):
        at = pl.ds(pl.multiple_of(i * 128, 128), 128)
        image[at, :] = dot(diag[i], sketch[at, :], ((1,), (0,)), None)
        return carry

    lax.fori_loop(0, 16, near, 0)
    for t in order:
        keep[t].wait()
        for i in range(1, 4):
            first[i, t].wait_recv()

        def add(i, carry):
            at = pl.ds(pl.multiple_of(i * 128, 128), 128)
            total = own[t, at, :].astype(f32) + one[0, t, at, :].astype(f32)
            total += one[1, t, at, :].astype(f32) + one[2, t, at, :].astype(f32)
            if t:
                sums[t - 1, at, :] = total.astype(jnp.bfloat16)
            else:
                image[at, :] += total
            return carry

        lax.fori_loop(0, 16, add, 0)
        if t:
            second[t - 1].start()
    keep[4].wait()
    for cp in lines:
        cp.wait_recv()

    def add_far(i, carry):
        at = pl.ds(pl.multiple_of(i * 128, 128), 128)
        total = image[at, :]
        for n in range(8):
            total += back[n, at, :].astype(f32)
        image[at, :] = total
        return carry

    lax.fori_loop(0, 16, add_far, 0)
    for cp in second:
        cp.wait_recv()

    def add_two(i, carry):
        at = pl.ds(pl.multiple_of(i * 128, 128), 128)
        image[at, :] += two[0, at, :].astype(f32) + two[1, at, :].astype(f32) + two[2, at, :].astype(f32)
        return carry

    lax.fori_loop(0, 16, add_two, 0)
    for cp in list(first.values()) + lines + second:
        cp.wait_send()
    finish_kernel(total_rows, image, basis, upper, gram, tiles, landed, summed, work, linv, s1, r1, s2, r2)


def combine(total_rows, diag, sketch, far, mirrors):
    f32, bf16 = jnp.float32, jnp.bfloat16
    vmem = pl.BlockSpec(memory_space=pltpu.VMEM)
    anyspec = pl.BlockSpec(memory_space=pl.ANY)
    return pl.pallas_call(
        functools.partial(combine_kernel, total_rows),
        out_shape=(jax.ShapeDtypeStruct((2048, 256), f32), jax.ShapeDtypeStruct((256, 256), f32)),
        in_specs=[vmem, vmem, anyspec, anyspec],
        out_specs=(vmem, vmem),
        scratch_shapes=[
            pltpu.VMEM((2048, 256), f32),
            pltpu.VMEM((4, 2048, 256), bf16),
            pltpu.VMEM((3, 4, 2048, 256), bf16),
            pltpu.VMEM((3, 2048, 256), bf16),
            pltpu.VMEM((3, 2048, 256), bf16),
            pltpu.VMEM((8, 2048, 256), bf16),
            pltpu.VMEM((256, 256), f32),
            pltpu.VMEM((64, 8, 128), f32),
            pltpu.VMEM((128, 8, 128), f32),
            pltpu.VMEM((64, 8, 128), f32),
            pltpu.VMEM((128, 256), f32),
            pltpu.VMEM((256, 256), f32),
            pltpu.SemaphoreType.DMA((22,)),
            pltpu.SemaphoreType.DMA((22,)),
            pltpu.SemaphoreType.DMA((5,)),
        ]
        + [pltpu.SemaphoreType.DMA] * 4,
        compiler_params=pltpu.CompilerParams(has_side_effects=True, vmem_limit_bytes=48 << 20),
        name="combine",
    )(diag, sketch, far, mirrors)


def split_owner(col):
    owner = col // 16
    r, y = owner // 4, owner % 4
    c = r % 2
    x, z = r // 8, (r // 2) % 4
    a, b = jnp.where(c == 0, x, z), jnp.where(c == 0, z, x)
    return y * 2 + c, (a * 4 + b) * 16 + col % 16


def on_device(diag_blocks, off_blocks, col_blocks, sketch):
    entries = 128
    flat = col_blocks.reshape(entries)
    order = jnp.arange(entries)
    before = order[None, :] < order[:, None]
    group, _ = split_owner(flat)
    rank = jnp.sum(((group[:, None] == group[None, :]) & before).astype(jnp.int32), axis=1)
    packed = pack(group * 32 + rank, off_blocks.reshape(entries, 128, 128))
    meta = jnp.broadcast_to(flat[None, :], (8, entries))
    blocks, line, plane, metas = gather_all(packed.reshape(8, 32, 128, 128), sketch, meta)
    mine = lax.axis_index("sub") * 2 + lax.axis_index("rows") % 2
    group, spot = split_owner(metas[:, 0, :])
    hit = group == mine
    rank = jnp.sum((hit[:, None, :] & before[None]).astype(jnp.int32), axis=2)
    chosen = (hit[:, None, :] & (rank[:, None, :] == jnp.arange(32)[None, :, None])).astype(jnp.int32)
    row = jnp.sum(chosen * (order // 8)[None, None, :], axis=2).reshape(256)
    col = jnp.sum(chosen * spot[:, None, :], axis=2).reshape(256)
    count = jnp.sum(hit.astype(jnp.int32), axis=1)
    far, mirrors = products(
        count, row, col, blocks, line.reshape(8, 16, 128, 256), plane.reshape(256, 128, 256)
    )
    return combine(262144, diag_blocks, sketch, far.reshape(8, 2048, 256), mirrors.reshape(16, 2048, 256))


def solution(mesh):
    placed = (
        P(("rows", "sub"), None, None),
        P(("rows", "sub"), None, None, None),
        P(("rows", "sub"), None),
        P(("rows", "sub"), None),
    )
    return jax.shard_map(
        on_device,
        mesh=mesh,
        in_specs=placed,
        out_specs=(P(("rows", "sub"), None), P()),
        check_vma=False,
    )
```

```python
import functools

import jax
import jax.numpy as jnp
from jax import lax
from jax.experimental import pallas as pl
from jax.experimental.pallas import tpu as pltpu
from jax.sharding import PartitionSpec as P

MESH = pl.DeviceIdType.MESH
HIGHEST = lax.Precision.HIGHEST
TILES = [(i, j) for i in range(32) for j in range(2) if i < 16 or j == 1]


def dot(a, b, dims, precision=HIGHEST):
    return lax.dot_general(a, b, (dims, ((), ())), precision=precision, preferred_element_type=jnp.float32)


def split(value):
    high = value.astype(jnp.bfloat16)
    return high, (value - high.astype(jnp.float32)).astype(jnp.bfloat16)


def eliminate(s, group):
    n, wide = s.shape
    sub = lax.broadcasted_iota(jnp.int32, (n, 1), 0)

    def widen(v):
        return jnp.concatenate([v] * (wide // 128), axis=1)

    for k in range(0, n, group):
        cols = [jnp.broadcast_to(s[:, k + i : k + i + 1], (n, 128)) for i in range(group)]
        rows = [s[k + i : k + i + 1, :] for i in range(group)]
        for j in range(group):
            scale = lax.rsqrt(cols[j][k + j : k + j + 1, :])
            cols[j] = cols[j] * scale
            rows[j] = rows[j] * widen(scale)
            for i in range(j + 1, group):
                share = cols[j][k + i : k + i + 1, :]
                cols[i] = cols[i] - cols[j] * share
                rows[i] = rows[i] - rows[j] * widen(share)
        for j in range(group):
            s = s - widen(jnp.where(sub >= k + group, cols[j], 0.0)) * rows[j]
        for j in range(group):
            s = jnp.where(sub == k + j, rows[j], s)
    return s


def solve_kernel(image, tiles, basis, upper, gram, work, linv):
    for t, (i, j) in enumerate(TILES):
        gram[8 * i : 8 * i + 8, 128 * j : 128 * j + 128] = tiles[t]
    eye = lax.broadcasted_iota(jnp.int32, (128, 128), 0), lax.broadcasted_iota(jnp.int32, (128, 128), 1)
    one = (eye[0] == eye[1]).astype(jnp.float32)
    work[...] = eliminate(jnp.concatenate([gram[:128, :128], one], axis=1), 8)
    i11 = work[:, 128:]
    r12 = dot(i11, gram[:128, 128:], ((1,), (0,)))
    upper[:128, :128] = jnp.where(eye[0] <= eye[1], work[:, :128], 0.0)
    upper[:128, 128:] = r12
    linv[:128, :128] = i11
    linv[:128, 128:] = jnp.zeros((128, 128), jnp.float32)
    cross = dot(r12, i11, ((0,), (0,)))
    rest = gram[128:, 128:] - dot(r12, r12, ((0,), (0,)))
    work[...] = eliminate(jnp.concatenate([rest, one], axis=1), 8)
    i22 = work[:, 128:]
    upper[128:, :128] = jnp.zeros((128, 128), jnp.float32)
    upper[128:, 128:] = jnp.where(eye[0] <= eye[1], work[:, :128], 0.0)
    linv[128:, :128] = -dot(i22, cross, ((1,), (0,)))
    linv[128:, 128:] = i22
    high, low = split(linv[...])
    across = ((1,), (1,))

    def rows_out(i, carry):
        at = pl.ds(pl.multiple_of(i * 256, 256), 256)
        h, l = split(image[at, :])
        basis[at, :] = dot(h, high, across, None) + (dot(h, low, across, None) + dot(l, high, across, None))
        return carry

    lax.fori_loop(0, 8, rows_out, 0)


def solve(image, tiles):
    f32 = jnp.float32
    vmem = pl.BlockSpec(memory_space=pltpu.VMEM)
    return pl.pallas_call(
        solve_kernel,
        out_shape=(jax.ShapeDtypeStruct((2048, 256), f32), jax.ShapeDtypeStruct((256, 256), f32)),
        in_specs=[vmem, vmem],
        out_specs=(vmem, vmem),
        scratch_shapes=[pltpu.VMEM((256, 256), f32), pltpu.VMEM((128, 256), f32), pltpu.VMEM((256, 256), f32)],
        compiler_params=pltpu.CompilerParams(vmem_limit_bytes=16 << 20),
        name="solve",
    )(image, tiles)


def place():
    r, y = lax.axis_index("rows"), lax.axis_index("sub")
    return r // 8, y, (r // 2) % 4, r % 2


def remote(src, dst, sems, k, x, y, z, c):
    send, recv = sems
    return pltpu.make_async_remote_copy(
        src_ref=src, dst_ref=dst, send_sem=send.at[k], recv_sem=recv.at[k],
        device_id=((x % 4) * 8 + (z % 4) * 2 + c % 2, y % 4), device_id_type=MESH)


def line_offsets():
    return [(i, d) for i in range(4) for d in range(2) if (i, d) != (0, 0)]


def half(ref, h):
    return ref.at[pl.ds(1024 * h, 1024), :]


def gather_kernel(packed, sketch, meta, blocks, line, plane, metas, send, recv, local):
    x, y, z, c = place()
    sems = (send, recv)
    a, b = x * (1 - c) + z * c, z * (1 - c) + x * c
    me = y * 2 + c
    own_q = a * 4 + b

    def q(i, j):
        return ((a + i) % 4) * 4 + (b + j) % 4

    def along(i, j):
        return x + 3 * 4 + (1 - c) * i + c * j, y, z + 3 * 4 + c * i + (1 - c) * j, c

    def line_at(i, d=0):
        return x, y + 4 + i, z, c + d

    def l(i):
        return ((y + 4 + i) % 4) * 2 + c

    keep = [
        pltpu.make_async_copy(sketch, plane.at[own_q], local.at[0]),
        pltpu.make_async_copy(sketch, line.at[me], local.at[1]),
        pltpu.make_async_copy(packed.at[me], blocks.at[me], local.at[2]),
        pltpu.make_async_copy(meta, metas.at[me], local.at[3]),
    ]

    def ring(source, slot, to, base):
        return {
            (s, h): remote(half(source, h), half(slot, h), sems, base + 2 * (s < 0) + h, *to(s))
            for s in (1, -1) for h in range(2)
        }

    def onward(slots, to, base):
        return {
            s: remote(half(slots[s], h), half(slots[s], h), sems, base + h, *to(s))
            for s, h in ((1, 0), (-1, 1))
        }

    to_a = lambda s: along(s, 0)
    first = ring(sketch, plane.at[own_q], to_a, 0)
    first_on = onward({1: plane.at[q(3, 0)], -1: plane.at[q(1, 0)]}, to_a, 4)
    same = ring(sketch, line.at[me], line_at, 6)
    same_on = onward({1: line.at[l(-1)], -1: line.at[l(1)]}, line_at, 10)
    mate = [remote(sketch, line.at[me], sems, 12, *line_at(0, 1))]
    mate += [remote(line.at[l(i)], line.at[l(i)], sems, 12 + n, *line_at(0, 1)) for n, i in ((1, -1), (2, 1), (3, 2))]
    to_b = lambda s: along(0, s)
    second, second_on = [], []
    for n, i in enumerate((0, 3, 1, 2)):
        source = sketch if i == 0 else plane.at[q(i, 0)]
        second.append(ring(source, plane.at[q(i, 0)], to_b, 16 + 6 * n))
        second_on.append(onward({1: plane.at[q(i, 3)], -1: plane.at[q(i, 1)]}, to_b, 20 + 6 * n))
    across, labels = [], []
    for n, (i, d) in enumerate(line_offsets()):
        to = ((y + i) % 4) * 2 + (c + d) % 2
        across.append(remote(packed.at[to], blocks.at[me], sems, 40 + n, *line_at(i, d)))
        labels.append(remote(meta, metas.at[me], sems, 47 + n, *line_at(i, d)))
    for cp in (list(first.values()) + list(same.values()) + list(second[0].values())
               + labels + mate[:1] + across + keep):
        cp.start()

    def pass_on(ring_, on_):
        ring_[1, 0].wait_recv()
        on_[1].start()
        ring_[-1, 1].wait_recv()
        on_[-1].start()

    pass_on(first, first_on)
    pass_on(same, same_on)
    first[1, 1].wait_recv()
    for cp in second[1].values():
        cp.start()
    first[-1, 0].wait_recv()
    for cp in second[2].values():
        cp.start()
    same[1, 1].wait_recv()
    mate[1].start()
    same[-1, 0].wait_recv()
    mate[2].start()
    pass_on(second[0], second_on[0])
    for s in (1, -1):
        first_on[s].wait_recv()
    for cp in second[3].values():
        cp.start()
    for s in (1, -1):
        same_on[s].wait_recv()
    mate[3].start()
    for n in (1, 2, 3):
        pass_on(second[n], second_on[n])
    for n in range(4):
        second[n][1, 1].wait_recv()
        second[n][-1, 0].wait_recv()
        for s in (1, -1):
            second_on[n][s].wait_recv()
    for cp in labels + across + mate + keep:
        cp.wait()
    for group in [first, first_on, same, same_on] + second + second_on:
        for cp in group.values():
            cp.wait_send()


def gather_all(packed, sketch, meta):
    anyspec = pl.BlockSpec(memory_space=pl.ANY)
    bf16 = jnp.bfloat16
    return pl.pallas_call(
        gather_kernel,
        out_shape=(
            jax.ShapeDtypeStruct((8, 32, 128, 128), bf16),
            jax.ShapeDtypeStruct((8, 2048, 256), bf16),
            jax.ShapeDtypeStruct((16, 2048, 256), bf16),
            jax.ShapeDtypeStruct((8, 8, 128), jnp.int32),
        ),
        in_specs=[anyspec] * 3,
        out_specs=(anyspec,) * 4,
        scratch_shapes=[pltpu.SemaphoreType.DMA((54,)), pltpu.SemaphoreType.DMA((54,)), pltpu.SemaphoreType.DMA((4,))],
        compiler_params=pltpu.CompilerParams(has_side_effects=True),
        name="gather",
    )(packed, sketch, meta)


def pack_kernel(slot, off, packed):
    def clear(i, carry):
        packed[i] = jnp.zeros((128, 128), jnp.bfloat16)
        return carry

    lax.fori_loop(0, 256, clear, 0, unroll=8)

    def go(e, carry):
        packed[slot[e]] = off[e]
        return carry

    lax.fori_loop(0, 128, go, 0, unroll=4)


def pack(slot, off):
    vmem = pl.BlockSpec(memory_space=pltpu.VMEM)
    return pl.pallas_call(
        pack_kernel,
        out_shape=jax.ShapeDtypeStruct((256, 128, 128), jnp.bfloat16),
        in_specs=[pl.BlockSpec(memory_space=pltpu.SMEM), vmem],
        out_specs=vmem,
        compiler_params=pltpu.CompilerParams(vmem_limit_bytes=16 << 20),
        name="pack",
    )(slot, off)


def product_kernel(count, row, col, blocks, line, plane, far, mirrors, acc, sums, stage, sem):
    s = pl.program_id(0)

    @pl.when(s == 0)
    def _():
        def clear(i, carry):
            sums[i] = jnp.zeros((128, 256), jnp.float32)
            return carry

        lax.fori_loop(0, 256, clear, 0)

    acc[...] = jnp.zeros_like(acc)

    def four(g, carry):
        at = [s * 32 + g * 4 + u for u in range(4)]
        rows, cols = [row[t] for t in at], [col[t] for t in at]
        given = [blocks[0, g * 4 + u] for u in range(4)]
        fars = [dot(given[u], plane[cols[u]], ((1,), (0,)), None) for u in range(4)]
        backs = [dot(given[u], line[0, rows[u]], ((0,), (0,)), None) for u in range(4)]
        for u in range(4):
            acc[rows[u]] += fars[u]
            sums[cols[u]] += backs[u].astype(jnp.bfloat16).astype(jnp.float32)
        return carry

    lax.fori_loop(0, (count[s] + 3) // 4, four, 0)
    far[0] = acc[...].astype(jnp.bfloat16)

    @pl.when(s == 7)
    def _():
        for n in range(16):
            if n >= 2:
                pltpu.make_async_copy(stage.at[n % 2], mirrors.at[pl.ds(16 * (n - 2), 16)], sem.at[n % 2]).wait()

            def out(i, carry):
                stage[n % 2, i] = sums[16 * n + i].astype(jnp.bfloat16)
                return carry

            lax.fori_loop(0, 16, out, 0)
            pltpu.make_async_copy(stage.at[n % 2], mirrors.at[pl.ds(16 * n, 16)], sem.at[n % 2]).start()
        for n in (14, 15):
            pltpu.make_async_copy(stage.at[n % 2], mirrors.at[pl.ds(16 * n, 16)], sem.at[n % 2]).wait()


def products(count, row, col, blocks, line, plane):
    bf16 = jnp.bfloat16
    return pl.pallas_call(
        product_kernel,
        grid_spec=pltpu.PrefetchScalarGridSpec(
            num_scalar_prefetch=3,
            grid=(8,),
            in_specs=[
                pl.BlockSpec((1, 32, 128, 128), lambda s, *_: (s, 0, 0, 0)),
                pl.BlockSpec((1, 16, 128, 256), lambda s, *_: (s, 0, 0, 0)),
                pl.BlockSpec((256, 128, 256), lambda s, *_: (0, 0, 0), pipeline_mode=pl.Buffered(1)),
            ],
            out_specs=(
                pl.BlockSpec((1, 16, 128, 256), lambda s, *_: (s, 0, 0, 0)),
                pl.BlockSpec(memory_space=pl.ANY),
            ),
            scratch_shapes=[
                pltpu.VMEM((16, 128, 256), jnp.float32),
                pltpu.VMEM((256, 128, 256), jnp.float32),
                pltpu.VMEM((2, 16, 128, 256), bf16),
                pltpu.SemaphoreType.DMA((2,)),
            ],
        ),
        out_shape=(
            jax.ShapeDtypeStruct((8, 16, 128, 256), bf16),
            jax.ShapeDtypeStruct((256, 128, 256), bf16),
        ),
        compiler_params=pltpu.CompilerParams(vmem_limit_bytes=60 << 20),
        name="products",
    )(count, row, col, blocks, line, plane)


def combine_kernel(total_rows, diag, sketch, far, mirrors, image, total_tiles,
                   own, one, sums, two, back, gram, tiles, from_line, part, from_plane,
                   send, recv, local, gsend, grecv):
    f32 = jnp.float32
    x, y, z, c = place()
    sems = (send, recv)
    a, b = x * (1 - c) + z * c, z * (1 - c) + x * c
    me = y * 2 + c

    def along(i, j):
        return x + (1 - c) * i + c * j, y, z + c * i + (1 - c) * j, c

    order = (1, 2, 3, 0)
    first = {}
    for t in order:
        for i in range(1, 4):
            q = ((a + i) % 4) * 4 + (b + t) % 4
            first[i, t] = remote(mirrors.at[q], one.at[i - 1, t], sems, 3 * t + i - 1, *along(i, 0))
    lines = []
    for n, (i, d) in enumerate(line_offsets()):
        to = ((y + i) % 4) * 2 + (c + d) % 2
        lines.append(remote(far.at[to], back.at[n + 1], sems, 12 + n, x, y + i, z, c + d))
    keep = [pltpu.make_async_copy(mirrors.at[a * 4 + (b + t) % 4], own.at[t], local.at[t]) for t in range(4)]
    keep.append(pltpu.make_async_copy(far.at[me], back.at[0], local.at[4]))
    second = [remote(sums.at[t - 1], two.at[t - 1], sems, 18 + t, *along(0, t)) for t in range(1, 4)]
    for t in order:
        for i in (1, 3, 2):
            first[i, t].start()
        if t == 1:
            for cp in lines:
                cp.start()
    for cp in keep:
        cp.start()

    def near(i, carry):
        at = pl.ds(pl.multiple_of(i * 128, 128), 128)
        image[at, :] = dot(diag[i], sketch[at, :], ((1,), (0,)), None)
        return carry

    lax.fori_loop(0, 16, near, 0)
    for t in order:
        keep[t].wait()
        for i in range(1, 4):
            first[i, t].wait_recv()

        def add(i, carry):
            at = pl.ds(pl.multiple_of(i * 128, 128), 128)
            total = own[t, at, :].astype(f32) + one[0, t, at, :].astype(f32)
            total += one[1, t, at, :].astype(f32) + one[2, t, at, :].astype(f32)
            if t:
                sums[t - 1, at, :] = total.astype(jnp.bfloat16)
            else:
                image[at, :] += total
            return carry

        lax.fori_loop(0, 16, add, 0)
        if t:
            second[t - 1].start()
    keep[4].wait()
    for cp in lines:
        cp.wait_recv()

    def add_far(i, carry):
        at = pl.ds(pl.multiple_of(i * 128, 128), 128)
        total = image[at, :]
        for n in range(8):
            total += back[n, at, :].astype(f32)
        image[at, :] = total
        return carry

    lax.fori_loop(0, 16, add_far, 0)
    for cp in second:
        cp.wait_recv()

    def add_two(i, carry):
        at = pl.ds(pl.multiple_of(i * 128, 128), 128)
        image[at, :] += two[0, at, :].astype(f32) + two[1, at, :].astype(f32) + two[2, at, :].astype(f32)
        return carry

    lax.fori_loop(0, 16, add_two, 0)
    for cp in list(first.values()) + lines + second:
        cp.wait_send()
    gram[...] = jnp.zeros_like(gram)

    def partial(i, carry):
        h, l = split(image[pl.ds(pl.multiple_of(i * 512, 512), 512), :])
        down = ((0,), (0,))
        gram[...] += dot(h, h, down, None) + (dot(h, l, down, None) + dot(l, h, down, None))
        return carry

    lax.fori_loop(0, 4, partial, 0)
    for t, (i, j) in enumerate(TILES):
        tiles[t] = gram[8 * i : 8 * i + 8, 128 * j : 128 * j + 128] * (1.0 / total_rows)
    gsems = (gsend, grecv)
    offsets = line_offsets()
    out = []
    for n, (i, d) in enumerate(offsets):
        to = ((y + i) % 4) * 2 + (c + d) % 2
        out.append(remote(tiles.at[pl.ds(to * 6, 6)], from_line.at[me], gsems, n, x, y + i, z, c + d))
    for cp in out:
        cp.start()
    from_line[me] = tiles[pl.ds(me * 6, 6)]
    for cp in out:
        cp.wait()
    part[...] = jnp.sum(from_line[...], axis=0)
    q = a * 4 + b
    spread = []
    for n in range(1, 16):
        spread.append(remote(part, from_plane.at[q], gsems, 6 + n, *along(n // 4, n % 4)))
    for cp in spread:
        cp.start()
    from_plane[q] = part[...]
    for cp in spread:
        cp.wait()
    total_tiles[pl.ds(me * 6, 6)] = jnp.sum(from_plane[...], axis=0)
    everyone = []
    for n, (i, d) in enumerate(offsets):
        mine = total_tiles.at[pl.ds(me * 6, 6)]
        everyone.append(remote(mine, mine, gsems, 22 + n, x, y + i, z, c + d))
    for cp in everyone:
        cp.start()
    for cp in everyone:
        cp.wait()


def combine(total_rows, diag, sketch, far, mirrors):
    f32, bf16 = jnp.float32, jnp.bfloat16
    vmem = pl.BlockSpec(memory_space=pltpu.VMEM)
    anyspec = pl.BlockSpec(memory_space=pl.ANY)
    return pl.pallas_call(
        functools.partial(combine_kernel, total_rows),
        out_shape=(jax.ShapeDtypeStruct((2048, 256), f32), jax.ShapeDtypeStruct((48, 8, 128), f32)),
        in_specs=[vmem, vmem, anyspec, anyspec],
        out_specs=(vmem, vmem),
        scratch_shapes=[
            pltpu.VMEM((4, 2048, 256), bf16),
            pltpu.VMEM((3, 4, 2048, 256), bf16),
            pltpu.VMEM((3, 2048, 256), bf16),
            pltpu.VMEM((3, 2048, 256), bf16),
            pltpu.VMEM((8, 2048, 256), bf16),
            pltpu.VMEM((256, 256), f32),
            pltpu.VMEM((48, 8, 128), f32),
            pltpu.VMEM((8, 6, 8, 128), f32),
            pltpu.VMEM((6, 8, 128), f32),
            pltpu.VMEM((16, 6, 8, 128), f32),
            pltpu.SemaphoreType.DMA((22,)),
            pltpu.SemaphoreType.DMA((22,)),
            pltpu.SemaphoreType.DMA((5,)),
            pltpu.SemaphoreType.DMA((29,)),
            pltpu.SemaphoreType.DMA((29,)),
        ],
        compiler_params=pltpu.CompilerParams(has_side_effects=True, vmem_limit_bytes=48 << 20),
        name="combine",
    )(diag, sketch, far, mirrors)


def split_owner(col):
    owner = col // 16
    r, y = owner // 4, owner % 4
    c = r % 2
    x, z = r // 8, (r // 2) % 4
    a, b = jnp.where(c == 0, x, z), jnp.where(c == 0, z, x)
    return y * 2 + c, (a * 4 + b) * 16 + col % 16


def on_device(diag_blocks, off_blocks, col_blocks, sketch):
    entries = 128
    flat = col_blocks.reshape(entries)
    order = jnp.arange(entries)
    before = order[None, :] < order[:, None]
    group, _ = split_owner(flat)
    rank = jnp.sum(((group[:, None] == group[None, :]) & before).astype(jnp.int32), axis=1)
    packed = pack(group * 32 + rank, off_blocks.reshape(entries, 128, 128))
    meta = jnp.broadcast_to(flat[None, :], (8, entries))
    blocks, line, plane, metas = gather_all(packed.reshape(8, 32, 128, 128), sketch, meta)
    mine = lax.axis_index("sub") * 2 + lax.axis_index("rows") % 2
    group, spot = split_owner(metas[:, 0, :])
    hit = group == mine
    rank = jnp.sum((hit[:, None, :] & before[None]).astype(jnp.int32), axis=2)
    chosen = (hit[:, None, :] & (rank[:, None, :] == jnp.arange(32)[None, :, None])).astype(jnp.int32)
    row = jnp.sum(chosen * (order // 8)[None, None, :], axis=2).reshape(256)
    col = jnp.sum(chosen * spot[:, None, :], axis=2).reshape(256)
    count = jnp.sum(hit.astype(jnp.int32), axis=1)
    far, mirrors = products(
        count, row, col, blocks, line.reshape(8, 16, 128, 256), plane.reshape(256, 128, 256)
    )
    image, tiles = combine(
        262144, diag_blocks, sketch, far.reshape(8, 2048, 256), mirrors.reshape(16, 2048, 256)
    )
    return solve(image, tiles)


def solution(mesh):
    placed = (
        P(("rows", "sub"), None, None),
        P(("rows", "sub"), None, None, None),
        P(("rows", "sub"), None),
        P(("rows", "sub"), None),
    )
    return jax.shard_map(
        on_device,
        mesh=mesh,
        in_specs=placed,
        out_specs=(P(("rows", "sub"), None), P()),
        check_vma=False,
    )
```

```python
import functools

import jax
import jax.numpy as jnp
from jax import lax
from jax.experimental import pallas as pl
from jax.experimental.pallas import tpu as pltpu
from jax.sharding import PartitionSpec as P

MESH = pl.DeviceIdType.MESH
HIGHEST = lax.Precision.HIGHEST
TILES = [(i, j) for i in range(32) for j in range(2) if i < 16 or j == 1]


def dot(a, b, dims, precision=HIGHEST):
    return lax.dot_general(a, b, (dims, ((), ())), precision=precision, preferred_element_type=jnp.float32)


def split(value):
    high = value.astype(jnp.bfloat16)
    return high, (value - high.astype(jnp.float32)).astype(jnp.bfloat16)


def eliminate(s, group):
    n, wide = s.shape
    sub = lax.broadcasted_iota(jnp.int32, (n, 1), 0)

    def widen(v):
        return jnp.concatenate([v] * (wide // 128), axis=1)

    for k in range(0, n, group):
        cols = [jnp.broadcast_to(s[:, k + i : k + i + 1], (n, 128)) for i in range(group)]
        rows = [s[k + i : k + i + 1, :] for i in range(group)]
        for j in range(group):
            scale = lax.rsqrt(cols[j][k + j : k + j + 1, :])
            cols[j] = cols[j] * scale
            rows[j] = rows[j] * widen(scale)
            for i in range(j + 1, group):
                share = cols[j][k + i : k + i + 1, :]
                cols[i] = cols[i] - cols[j] * share
                rows[i] = rows[i] - rows[j] * widen(share)
        for j in range(group):
            s = s - widen(jnp.where(sub >= k + group, cols[j], 0.0)) * rows[j]
        for j in range(group):
            s = jnp.where(sub == k + j, rows[j], s)
    return s


def solve_kernel(image, tiles, basis, upper, gram, work, linv):
    for t, (i, j) in enumerate(TILES):
        gram[8 * i : 8 * i + 8, 128 * j : 128 * j + 128] = tiles[t]
    eye = lax.broadcasted_iota(jnp.int32, (128, 128), 0), lax.broadcasted_iota(jnp.int32, (128, 128), 1)
    one = (eye[0] == eye[1]).astype(jnp.float32)
    work[...] = eliminate(jnp.concatenate([gram[:128, :128], one], axis=1), 8)
    i11 = work[:, 128:]
    r12 = dot(i11, gram[:128, 128:], ((1,), (0,)))
    upper[:128, :128] = jnp.where(eye[0] <= eye[1], work[:, :128], 0.0)
    upper[:128, 128:] = r12
    linv[:128, :128] = i11
    linv[:128, 128:] = jnp.zeros((128, 128), jnp.float32)
    cross = dot(r12, i11, ((0,), (0,)))
    rest = gram[128:, 128:] - dot(r12, r12, ((0,), (0,)))
    work[...] = eliminate(jnp.concatenate([rest, one], axis=1), 8)
    i22 = work[:, 128:]
    upper[128:, :128] = jnp.zeros((128, 128), jnp.float32)
    upper[128:, 128:] = jnp.where(eye[0] <= eye[1], work[:, :128], 0.0)
    linv[128:, :128] = -dot(i22, cross, ((1,), (0,)))
    linv[128:, 128:] = i22
    high, low = split(linv[...])
    across = ((1,), (1,))

    def rows_out(i, carry):
        at = pl.ds(pl.multiple_of(i * 256, 256), 256)
        h, l = split(image[at, :])
        basis[at, :] = dot(h, high, across, None) + (dot(h, low, across, None) + dot(l, high, across, None))
        return carry

    lax.fori_loop(0, 8, rows_out, 0)


def solve(image, tiles):
    f32 = jnp.float32
    vmem = pl.BlockSpec(memory_space=pltpu.VMEM)
    return pl.pallas_call(
        solve_kernel,
        out_shape=(jax.ShapeDtypeStruct((2048, 256), f32), jax.ShapeDtypeStruct((256, 256), f32)),
        in_specs=[vmem, vmem],
        out_specs=(vmem, vmem),
        scratch_shapes=[pltpu.VMEM((256, 256), f32), pltpu.VMEM((128, 256), f32), pltpu.VMEM((256, 256), f32)],
        compiler_params=pltpu.CompilerParams(vmem_limit_bytes=16 << 20),
        name="solve",
    )(image, tiles)


def place():
    r, y = lax.axis_index("rows"), lax.axis_index("sub")
    return r // 8, y, (r // 2) % 4, r % 2


def remote(src, dst, sems, k, x, y, z, c):
    send, recv = sems
    return pltpu.make_async_remote_copy(
        src_ref=src, dst_ref=dst, send_sem=send.at[k], recv_sem=recv.at[k],
        device_id=((x % 4) * 8 + (z % 4) * 2 + c % 2, y % 4), device_id_type=MESH)


def line_offsets():
    return [(i, d) for i in range(4) for d in range(2) if (i, d) != (0, 0)]


def half(ref, h):
    return ref.at[pl.ds(1024 * h, 1024), :]


def gather_kernel(packed, sketch, meta, blocks, line, plane, metas, held, kept, send, recv, local):
    x, y, z, c = place()
    sems = (send, recv)
    a, b = x * (1 - c) + z * c, z * (1 - c) + x * c
    me = y * 2 + c
    own_q = a * 4 + b

    def q(i, j):
        return ((a + i) % 4) * 4 + (b + j) % 4

    def along(i, j):
        return x + 3 * 4 + (1 - c) * i + c * j, y, z + 3 * 4 + c * i + (1 - c) * j, c

    def line_at(i, d=0):
        return x, y + 4 + i, z, c + d

    def l(i):
        return ((y + 4 + i) % 4) * 2 + c

    fetch = [
        pltpu.make_async_copy(sketch, held, local.at[0]),
        pltpu.make_async_copy(packed.at[me], kept, local.at[1]),
    ]
    keep = [
        pltpu.make_async_copy(held, plane.at[own_q], local.at[2]),
        pltpu.make_async_copy(held, line.at[me], local.at[3]),
        pltpu.make_async_copy(kept, blocks.at[me], local.at[4]),
        pltpu.make_async_copy(meta, metas.at[me], local.at[5]),
    ]

    def ring(source, slot, to, base):
        return {
            (s, h): remote(half(source, h), half(slot, h), sems, base + 2 * (s < 0) + h, *to(s))
            for s in (1, -1) for h in range(2)
        }

    def onward(slots, to, base):
        return {
            s: remote(half(slots[s], h), half(slots[s], h), sems, base + h, *to(s))
            for s, h in ((1, 0), (-1, 1))
        }

    to_a = lambda s: along(s, 0)
    first = ring(sketch, plane.at[own_q], to_a, 0)
    first_on = onward({1: plane.at[q(3, 0)], -1: plane.at[q(1, 0)]}, to_a, 4)
    same = ring(sketch, line.at[me], line_at, 6)
    same_on = onward({1: line.at[l(-1)], -1: line.at[l(1)]}, line_at, 10)
    mate = [remote(sketch, line.at[me], sems, 12, *line_at(0, 1))]
    mate += [remote(line.at[l(i)], line.at[l(i)], sems, 12 + n, *line_at(0, 1)) for n, i in ((1, -1), (2, 1), (3, 2))]
    to_b = lambda s: along(0, s)
    second, second_on = [], []
    for n, i in enumerate((0, 3, 1, 2)):
        source = sketch if i == 0 else plane.at[q(i, 0)]
        second.append(ring(source, plane.at[q(i, 0)], to_b, 16 + 6 * n))
        second_on.append(onward({1: plane.at[q(i, 3)], -1: plane.at[q(i, 1)]}, to_b, 20 + 6 * n))
    across, labels = [], []
    for n, (i, d) in enumerate(line_offsets()):
        to = ((y + i) % 4) * 2 + (c + d) % 2
        across.append(remote(packed.at[to], blocks.at[me], sems, 40 + n, *line_at(i, d)))
        labels.append(remote(meta, metas.at[me], sems, 47 + n, *line_at(i, d)))
    for cp in (list(first.values()) + list(same.values()) + list(second[0].values())
               + labels + mate[:1] + across + fetch):
        cp.start()
    for cp in fetch:
        cp.wait()
    for cp in keep:
        cp.start()

    def pass_on(ring_, on_):
        ring_[1, 0].wait_recv()
        on_[1].start()
        ring_[-1, 1].wait_recv()
        on_[-1].start()

    pass_on(first, first_on)
    pass_on(same, same_on)
    first[1, 1].wait_recv()
    for cp in second[1].values():
        cp.start()
    first[-1, 0].wait_recv()
    for cp in second[2].values():
        cp.start()
    same[1, 1].wait_recv()
    mate[1].start()
    same[-1, 0].wait_recv()
    mate[2].start()
    pass_on(second[0], second_on[0])
    for s in (1, -1):
        first_on[s].wait_recv()
    for cp in second[3].values():
        cp.start()
    for s in (1, -1):
        same_on[s].wait_recv()
    mate[3].start()
    for n in (1, 2, 3):
        pass_on(second[n], second_on[n])
    for n in range(4):
        second[n][1, 1].wait_recv()
        second[n][-1, 0].wait_recv()
        for s in (1, -1):
            second_on[n][s].wait_recv()
    for cp in labels + across + mate + keep:
        cp.wait()
    for group in [first, first_on, same, same_on] + second + second_on:
        for cp in group.values():
            cp.wait_send()


def gather_all(packed, sketch, meta):
    anyspec = pl.BlockSpec(memory_space=pl.ANY)
    bf16 = jnp.bfloat16
    return pl.pallas_call(
        gather_kernel,
        out_shape=(
            jax.ShapeDtypeStruct((8, 32, 128, 128), bf16),
            jax.ShapeDtypeStruct((8, 2048, 256), bf16),
            jax.ShapeDtypeStruct((16, 2048, 256), bf16),
            jax.ShapeDtypeStruct((8, 8, 128), jnp.int32),
        ),
        in_specs=[anyspec] * 3,
        out_specs=(anyspec,) * 4,
        scratch_shapes=[
            pltpu.VMEM((2048, 256), bf16),
            pltpu.VMEM((32, 128, 128), bf16),
            pltpu.SemaphoreType.DMA((54,)),
            pltpu.SemaphoreType.DMA((54,)),
            pltpu.SemaphoreType.DMA((6,)),
        ],
        compiler_params=pltpu.CompilerParams(has_side_effects=True),
        name="gather",
    )(packed, sketch, meta)


def pack_kernel(slot, off, packed):
    def clear(i, carry):
        packed[i] = jnp.zeros((128, 128), jnp.bfloat16)
        return carry

    lax.fori_loop(0, 256, clear, 0, unroll=8)

    def go(e, carry):
        packed[slot[e]] = off[e]
        return carry

    lax.fori_loop(0, 128, go, 0, unroll=4)


def pack(slot, off):
    vmem = pl.BlockSpec(memory_space=pltpu.VMEM)
    return pl.pallas_call(
        pack_kernel,
        out_shape=jax.ShapeDtypeStruct((256, 128, 128), jnp.bfloat16),
        in_specs=[pl.BlockSpec(memory_space=pltpu.SMEM), vmem],
        out_specs=vmem,
        compiler_params=pltpu.CompilerParams(vmem_limit_bytes=16 << 20),
        name="pack",
    )(slot, off)


def product_kernel(count, row, col, blocks, line, plane_all, far, mirrors, acc, sums, plane, stage, sem, plane_sem):
    s = pl.program_id(0)

    @pl.when(s == 0)
    def _():
        load = pltpu.make_async_copy(plane_all, plane, plane_sem)
        load.start()

        def clear(i, carry):
            sums[i] = jnp.zeros((128, 256), jnp.float32)
            return carry

        lax.fori_loop(0, 256, clear, 0, unroll=4)
        load.wait()

    acc[...] = jnp.zeros_like(acc)

    def four(g, carry):
        at = [s * 32 + g * 4 + u for u in range(4)]
        rows, cols = [row[t] for t in at], [col[t] for t in at]
        given = [blocks[0, g * 4 + u] for u in range(4)]
        fars = [dot(given[u], plane[cols[u]], ((1,), (0,)), None) for u in range(4)]
        backs = [dot(given[u], line[0, rows[u]], ((0,), (0,)), None) for u in range(4)]
        for u in range(4):
            acc[rows[u]] += fars[u]
            sums[cols[u]] += backs[u].astype(jnp.bfloat16).astype(jnp.float32)
        return carry

    lax.fori_loop(0, (count[s] + 3) // 4, four, 0)
    far[0] = acc[...].astype(jnp.bfloat16)

    @pl.when(s == 7)
    def _():
        for n in range(16):
            if n >= 2:
                pltpu.make_async_copy(stage.at[n % 2], mirrors.at[pl.ds(16 * (n - 2), 16)], sem.at[n % 2]).wait()

            def out(i, carry):
                stage[n % 2, i] = sums[16 * n + i].astype(jnp.bfloat16)
                return carry

            lax.fori_loop(0, 16, out, 0, unroll=2)
            pltpu.make_async_copy(stage.at[n % 2], mirrors.at[pl.ds(16 * n, 16)], sem.at[n % 2]).start()
        for n in (14, 15):
            pltpu.make_async_copy(stage.at[n % 2], mirrors.at[pl.ds(16 * n, 16)], sem.at[n % 2]).wait()


def products(count, row, col, blocks, line, plane):
    bf16 = jnp.bfloat16
    return pl.pallas_call(
        product_kernel,
        grid_spec=pltpu.PrefetchScalarGridSpec(
            num_scalar_prefetch=3,
            grid=(8,),
            in_specs=[
                pl.BlockSpec((1, 32, 128, 128), lambda s, *_: (s, 0, 0, 0)),
                pl.BlockSpec((1, 16, 128, 256), lambda s, *_: (s, 0, 0, 0)),
                pl.BlockSpec(memory_space=pl.ANY),
            ],
            out_specs=(
                pl.BlockSpec((1, 16, 128, 256), lambda s, *_: (s, 0, 0, 0)),
                pl.BlockSpec(memory_space=pl.ANY),
            ),
            scratch_shapes=[
                pltpu.VMEM((16, 128, 256), jnp.float32),
                pltpu.VMEM((256, 128, 256), jnp.float32),
                pltpu.VMEM((256, 128, 256), bf16),
                pltpu.VMEM((2, 16, 128, 256), bf16),
                pltpu.SemaphoreType.DMA((2,)),
                pltpu.SemaphoreType.DMA,
            ],
        ),
        out_shape=(
            jax.ShapeDtypeStruct((8, 16, 128, 256), bf16),
            jax.ShapeDtypeStruct((256, 128, 256), bf16),
        ),
        compiler_params=pltpu.CompilerParams(vmem_limit_bytes=60 << 20),
        name="products",
    )(count, row, col, blocks, line, plane)


def combine_kernel(total_rows, diag, sketch, far, mirrors, image, total_tiles,
                   own, one, pre, next_to, sums, two, back, gram, tiles, from_line, part, from_plane,
                   send, recv, local, gsend, grecv):
    f32 = jnp.float32
    x, y, z, c = place()
    sems = (send, recv)
    a, b = x * (1 - c) + z * c, z * (1 - c) + x * c
    me = y * 2 + c

    def along(i, j):
        return x + (1 - c) * i + c * j, y, z + c * i + (1 - c) * j, c

    order = (1, 2, 3, 0)

    def q(i, t):
        return ((a + 4 + i) % 4) * 4 + (b + t) % 4

    opposite, straight, onward, near_own, keep = {}, {}, {}, {}, []
    for n, t in enumerate(order):
        for side, (s, h) in enumerate(((1, 0), (-1, 1))):
            k = 6 * n + side
            opposite[t, side] = remote(half(mirrors.at[q(2, t)], h), pre.at[side, t], sems, k, *along(4 + s, 0))
            straight[t, side] = remote(
                half(mirrors.at[q(s, t)], 1 - h), half(one.at[side, t], 1 - h), sems, k + 2, *along(4 + s, 0))
            onward[t, side] = remote(next_to.at[side, t], half(one.at[side, t], h), sems, k + 4, *along(4 + s, 0))
            near_own[t, side] = pltpu.make_async_copy(
                half(mirrors.at[q(s, t)], h), next_to.at[side, t], local.at[5 + 2 * n + side])
    lines = []
    for n, (i, d) in enumerate(line_offsets()):
        to = ((y + i) % 4) * 2 + (c + d) % 2
        lines.append(remote(far.at[to], back.at[n + 1], sems, 24 + n, x, y + i, z, c + d))
    keep = [pltpu.make_async_copy(mirrors.at[q(0, t)], own.at[t], local.at[t]) for t in range(4)]
    keep.append(pltpu.make_async_copy(far.at[me], back.at[0], local.at[4]))
    second = [remote(sums.at[t - 1], two.at[t - 1], sems, 30 + t, *along(0, t)) for t in range(1, 4)]
    for group in (opposite, near_own):
        for t in order:
            for side in range(2):
                group[t, side].start()
    for t in order:
        for side in range(2):
            straight[t, side].start()
        if t == 1:
            for cp in lines:
                cp.start()
    for cp in keep:
        cp.start()

    def near(i, carry):
        at = pl.ds(pl.multiple_of(i * 128, 128), 128)
        image[at, :] = dot(diag[i], sketch[at, :], ((1,), (0,)), None)
        return carry

    lax.fori_loop(0, 16, near, 0)
    for t in order:
        for side in range(2):
            near_own[t, side].wait()
            opposite[t, side].wait_recv()

            def join(i, carry):
                at = pl.ds(pl.multiple_of(i * 128, 128), 128)
                total = next_to[side, t, at, :].astype(f32) + pre[side, t, at, :].astype(f32)
                next_to[side, t, at, :] = total.astype(jnp.bfloat16)
                return carry

            lax.fori_loop(0, 8, join, 0)
            onward[t, side].start()
    for t in order:
        keep[t].wait()
        for side in range(2):
            straight[t, side].wait_recv()
            onward[t, side].wait_recv()

        def add(i, carry):
            at = pl.ds(pl.multiple_of(i * 128, 128), 128)
            total = own[t, at, :].astype(f32) + one[0, t, at, :].astype(f32) + one[1, t, at, :].astype(f32)
            if t:
                sums[t - 1, at, :] = total.astype(jnp.bfloat16)
            else:
                image[at, :] += total
            return carry

        lax.fori_loop(0, 16, add, 0)
        if t:
            second[t - 1].start()
    keep[4].wait()
    for cp in lines:
        cp.wait_recv()

    def add_far(i, carry):
        at = pl.ds(pl.multiple_of(i * 128, 128), 128)
        total = image[at, :]
        for n in range(8):
            total += back[n, at, :].astype(f32)
        image[at, :] = total
        return carry

    lax.fori_loop(0, 16, add_far, 0)
    for cp in second:
        cp.wait_recv()

    def add_two(i, carry):
        at = pl.ds(pl.multiple_of(i * 128, 128), 128)
        image[at, :] += two[0, at, :].astype(f32) + two[1, at, :].astype(f32) + two[2, at, :].astype(f32)
        return carry

    lax.fori_loop(0, 16, add_two, 0)
    for cp in [*opposite.values(), *straight.values(), *onward.values()] + lines + second:
        cp.wait_send()
    gram[...] = jnp.zeros_like(gram)

    def partial(i, carry):
        h, l = split(image[pl.ds(pl.multiple_of(i * 512, 512), 512), :])
        down = ((0,), (0,))
        gram[...] += dot(h, h, down, None) + (dot(h, l, down, None) + dot(l, h, down, None))
        return carry

    lax.fori_loop(0, 4, partial, 0)
    for t, (i, j) in enumerate(TILES):
        tiles[t] = gram[8 * i : 8 * i + 8, 128 * j : 128 * j + 128] * (1.0 / total_rows)
    gsems = (gsend, grecv)
    offsets = line_offsets()
    out = []
    for n, (i, d) in enumerate(offsets):
        to = ((y + i) % 4) * 2 + (c + d) % 2
        out.append(remote(tiles.at[pl.ds(to * 6, 6)], from_line.at[me], gsems, n, x, y + i, z, c + d))
    for cp in out:
        cp.start()
    from_line[me] = tiles[pl.ds(me * 6, 6)]
    for cp in out:
        cp.wait()
    part[...] = jnp.sum(from_line[...], axis=0)
    own_q = a * 4 + b
    spread = []
    for n in range(1, 16):
        spread.append(remote(part, from_plane.at[own_q], gsems, 6 + n, *along(n // 4, n % 4)))
    for cp in spread:
        cp.start()
    from_plane[own_q] = part[...]
    for cp in spread:
        cp.wait()
    total_tiles[pl.ds(me * 6, 6)] = jnp.sum(from_plane[...], axis=0)
    everyone = []
    for n, (i, d) in enumerate(offsets):
        mine = total_tiles.at[pl.ds(me * 6, 6)]
        everyone.append(remote(mine, mine, gsems, 22 + n, x, y + i, z, c + d))
    for cp in everyone:
        cp.start()
    for cp in everyone:
        cp.wait()


def combine(total_rows, diag, sketch, far, mirrors):
    f32, bf16 = jnp.float32, jnp.bfloat16
    vmem = pl.BlockSpec(memory_space=pltpu.VMEM)
    anyspec = pl.BlockSpec(memory_space=pl.ANY)
    return pl.pallas_call(
        functools.partial(combine_kernel, total_rows),
        out_shape=(jax.ShapeDtypeStruct((2048, 256), f32), jax.ShapeDtypeStruct((48, 8, 128), f32)),
        in_specs=[vmem, vmem, anyspec, anyspec],
        out_specs=(vmem, vmem),
        scratch_shapes=[
            pltpu.VMEM((4, 2048, 256), bf16),
            pltpu.VMEM((2, 4, 2048, 256), bf16),
            pltpu.VMEM((2, 4, 1024, 256), bf16),
            pltpu.VMEM((2, 4, 1024, 256), bf16),
            pltpu.VMEM((3, 2048, 256), bf16),
            pltpu.VMEM((3, 2048, 256), bf16),
            pltpu.VMEM((8, 2048, 256), bf16),
            pltpu.VMEM((256, 256), f32),
            pltpu.VMEM((48, 8, 128), f32),
            pltpu.VMEM((8, 6, 8, 128), f32),
            pltpu.VMEM((6, 8, 128), f32),
            pltpu.VMEM((16, 6, 8, 128), f32),
            pltpu.SemaphoreType.DMA((34,)),
            pltpu.SemaphoreType.DMA((34,)),
            pltpu.SemaphoreType.DMA((13,)),
            pltpu.SemaphoreType.DMA((29,)),
            pltpu.SemaphoreType.DMA((29,)),
        ],
        compiler_params=pltpu.CompilerParams(has_side_effects=True, vmem_limit_bytes=48 << 20),
        name="combine",
    )(diag, sketch, far, mirrors)


def split_owner(col):
    owner = col // 16
    r, y = owner // 4, owner % 4
    c = r % 2
    x, z = r // 8, (r // 2) % 4
    a, b = jnp.where(c == 0, x, z), jnp.where(c == 0, z, x)
    return y * 2 + c, (a * 4 + b) * 16 + col % 16


def on_device(diag_blocks, off_blocks, col_blocks, sketch):
    entries = 128
    flat = col_blocks.reshape(entries)
    order = jnp.arange(entries)
    before = order[None, :] < order[:, None]
    group, _ = split_owner(flat)
    rank = jnp.sum(((group[:, None] == group[None, :]) & before).astype(jnp.int32), axis=1)
    packed = pack(group * 32 + rank, off_blocks.reshape(entries, 128, 128))
    meta = jnp.broadcast_to(flat[None, :], (8, entries))
    blocks, line, plane, metas = gather_all(packed.reshape(8, 32, 128, 128), sketch, meta)
    mine = lax.axis_index("sub") * 2 + lax.axis_index("rows") % 2
    group, spot = split_owner(metas[:, 0, :])
    hit = group == mine
    rank = jnp.sum((hit[:, None, :] & before[None]).astype(jnp.int32), axis=2)
    chosen = (hit[:, None, :] & (rank[:, None, :] == jnp.arange(32)[None, :, None])).astype(jnp.int32)
    row = jnp.sum(chosen * (order // 8)[None, None, :], axis=2).reshape(256)
    col = jnp.sum(chosen * spot[:, None, :], axis=2).reshape(256)
    count = jnp.sum(hit.astype(jnp.int32), axis=1)
    far, mirrors = products(
        count, row, col, blocks, line.reshape(8, 16, 128, 256), plane.reshape(256, 128, 256)
    )
    image, tiles = combine(
        262144, diag_blocks, sketch, far.reshape(8, 2048, 256), mirrors.reshape(16, 2048, 256)
    )
    return solve(image, tiles)


def solution(mesh):
    placed = (
        P(("rows", "sub"), None, None),
        P(("rows", "sub"), None, None, None),
        P(("rows", "sub"), None),
        P(("rows", "sub"), None),
    )
    return jax.shard_map(
        on_device,
        mesh=mesh,
        in_specs=placed,
        out_specs=(P(("rows", "sub"), None), P()),
        check_vma=False,
    )
```

```python
import functools

import jax
import jax.numpy as jnp
from jax import lax
from jax.experimental import pallas as pl
from jax.experimental.pallas import tpu as pltpu
from jax.sharding import PartitionSpec as P

MESH = pl.DeviceIdType.MESH
HIGHEST = lax.Precision.HIGHEST
TILES = [(i, j) for i in range(32) for j in range(2) if i < 16 or j == 1]


def dot(a, b, dims, precision=HIGHEST):
    return lax.dot_general(a, b, (dims, ((), ())), precision=precision, preferred_element_type=jnp.float32)


def split(value):
    high = value.astype(jnp.bfloat16)
    return high, (value - high.astype(jnp.float32)).astype(jnp.bfloat16)


def eliminate(s, group):
    n, wide = s.shape
    sub = lax.broadcasted_iota(jnp.int32, (n, 1), 0)

    def widen(v):
        return jnp.concatenate([v] * (wide // 128), axis=1)

    for k in range(0, n, group):
        cols = [jnp.broadcast_to(s[:, k + i : k + i + 1], (n, 128)) for i in range(group)]
        rows = [s[k + i : k + i + 1, :] for i in range(group)]
        for j in range(group):
            scale = lax.rsqrt(cols[j][k + j : k + j + 1, :])
            cols[j] = cols[j] * scale
            rows[j] = rows[j] * widen(scale)
            for i in range(j + 1, group):
                share = cols[j][k + i : k + i + 1, :]
                cols[i] = cols[i] - cols[j] * share
                rows[i] = rows[i] - rows[j] * widen(share)
        for j in range(group):
            s = s - widen(jnp.where(sub >= k + group, cols[j], 0.0)) * rows[j]
        for j in range(group):
            s = jnp.where(sub == k + j, rows[j], s)
    return s


def solve_kernel(image, tiles, basis, upper, gram, work, linv):
    for t, (i, j) in enumerate(TILES):
        gram[8 * i : 8 * i + 8, 128 * j : 128 * j + 128] = tiles[t]
    eye = lax.broadcasted_iota(jnp.int32, (128, 128), 0), lax.broadcasted_iota(jnp.int32, (128, 128), 1)
    one = (eye[0] == eye[1]).astype(jnp.float32)
    work[...] = eliminate(jnp.concatenate([gram[:128, :128], one], axis=1), 8)
    i11 = work[:, 128:]
    r12 = dot(i11, gram[:128, 128:], ((1,), (0,)))
    upper[:128, :128] = jnp.where(eye[0] <= eye[1], work[:, :128], 0.0)
    upper[:128, 128:] = r12
    linv[:128, :128] = i11
    linv[:128, 128:] = jnp.zeros((128, 128), jnp.float32)
    cross = dot(r12, i11, ((0,), (0,)))
    rest = gram[128:, 128:] - dot(r12, r12, ((0,), (0,)))
    work[...] = eliminate(jnp.concatenate([rest, one], axis=1), 8)
    i22 = work[:, 128:]
    upper[128:, :128] = jnp.zeros((128, 128), jnp.float32)
    upper[128:, 128:] = jnp.where(eye[0] <= eye[1], work[:, :128], 0.0)
    linv[128:, :128] = -dot(i22, cross, ((1,), (0,)))
    linv[128:, 128:] = i22
    high, low = split(linv[...])
    across = ((1,), (1,))

    def rows_out(i, carry):
        at = pl.ds(pl.multiple_of(i * 256, 256), 256)
        h, l = split(image[at, :])
        basis[at, :] = dot(h, high, across, None) + (dot(h, low, across, None) + dot(l, high, across, None))
        return carry

    lax.fori_loop(0, 8, rows_out, 0)


def solve(image, tiles):
    f32 = jnp.float32
    vmem = pl.BlockSpec(memory_space=pltpu.VMEM)
    return pl.pallas_call(
        solve_kernel,
        out_shape=(jax.ShapeDtypeStruct((2048, 256), f32), jax.ShapeDtypeStruct((256, 256), f32)),
        in_specs=[vmem, vmem],
        out_specs=(vmem, vmem),
        scratch_shapes=[pltpu.VMEM((256, 256), f32), pltpu.VMEM((128, 256), f32), pltpu.VMEM((256, 256), f32)],
        compiler_params=pltpu.CompilerParams(vmem_limit_bytes=16 << 20),
        name="solve",
    )(image, tiles)


def place():
    r, y = lax.axis_index("rows"), lax.axis_index("sub")
    return r // 8, y, (r // 2) % 4, r % 2


def remote(src, dst, sems, k, x, y, z, c):
    send, recv = sems
    return pltpu.make_async_remote_copy(
        src_ref=src, dst_ref=dst, send_sem=send.at[k], recv_sem=recv.at[k],
        device_id=((x % 4) * 8 + (z % 4) * 2 + c % 2, y % 4), device_id_type=MESH)


def line_offsets():
    return [(i, d) for i in range(4) for d in range(2) if (i, d) != (0, 0)]


def half(ref, h):
    return ref.at[pl.ds(1024 * h, 1024), :]


def gather_kernel(pick, off, sketch, meta, blocks, line, plane, metas, given, packed, held, send, recv, local):
    x, y, z, c = place()
    sems = (send, recv)
    a, b = x * (1 - c) + z * c, z * (1 - c) + x * c
    me = y * 2 + c
    own_q = a * 4 + b

    def q(i, j):
        return ((a + i) % 4) * 4 + (b + j) % 4

    def along(i, j):
        return x + 3 * 4 + (1 - c) * i + c * j, y, z + 3 * 4 + c * i + (1 - c) * j, c

    def line_at(i, d=0):
        return x, y + 4 + i, z, c + d

    def l(i):
        return ((y + 4 + i) % 4) * 2 + c

    def slots(j):
        return packed.at[pl.ds(j * 32, 32)]

    take = pltpu.make_async_copy(off, given, local.at[0])
    fetch = pltpu.make_async_copy(sketch, held, local.at[1])
    keep = [
        pltpu.make_async_copy(held, plane.at[own_q], local.at[2]),
        pltpu.make_async_copy(held, line.at[me], local.at[3]),
        pltpu.make_async_copy(slots(me), blocks.at[me], local.at[4]),
        pltpu.make_async_copy(meta.at[me], metas.at[me], local.at[5]),
    ]

    def ring(source, slot, to, base):
        return {
            (s, h): remote(half(source, h), half(slot, h), sems, base + 2 * (s < 0) + h, *to(s))
            for s in (1, -1) for h in range(2)
        }

    def onward(slots, to, base):
        return {
            s: remote(half(slots[s], h), half(slots[s], h), sems, base + h, *to(s))
            for s, h in ((1, 0), (-1, 1))
        }

    to_a = lambda s: along(s, 0)
    first = ring(sketch, plane.at[own_q], to_a, 0)
    first_on = onward({1: plane.at[q(3, 0)], -1: plane.at[q(1, 0)]}, to_a, 4)
    same = ring(sketch, line.at[me], line_at, 6)
    same_on = onward({1: line.at[l(-1)], -1: line.at[l(1)]}, line_at, 10)
    mate = [remote(sketch, line.at[me], sems, 12, *line_at(0, 1))]
    mate += [remote(line.at[l(i)], line.at[l(i)], sems, 12 + n, *line_at(0, 1)) for n, i in ((1, -1), (2, 1), (3, 2))]
    to_b = lambda s: along(0, s)
    second, second_on = [], []
    for n, i in enumerate((0, 3, 1, 2)):
        source = sketch if i == 0 else plane.at[q(i, 0)]
        second.append(ring(source, plane.at[q(i, 0)], to_b, 16 + 6 * n))
        second_on.append(onward({1: plane.at[q(i, 3)], -1: plane.at[q(i, 1)]}, to_b, 20 + 6 * n))
    across, labels = [], []
    for n, (i, d) in enumerate(line_offsets()):
        to = ((y + i) % 4) * 2 + (c + d) % 2
        across.append(remote(slots(to), blocks.at[me], sems, 40 + n, *line_at(i, d)))
        labels.append(remote(meta.at[to], metas.at[me], sems, 47 + n, *line_at(i, d)))
    take.start()
    for cp in list(same.values()) + list(first.values()) + list(second[0].values()) + mate[:1] + labels:
        cp.start()
    fetch.start()
    take.wait()

    def place_block(t, carry):
        packed[t] = given[pick[t]]
        return carry

    lax.fori_loop(0, 256, place_block, 0, unroll=8)
    for cp in across:
        cp.start()
    fetch.wait()
    for cp in keep:
        cp.start()

    def pass_on(ring_, on_):
        ring_[1, 0].wait_recv()
        on_[1].start()
        ring_[-1, 1].wait_recv()
        on_[-1].start()

    pass_on(same, same_on)
    pass_on(first, first_on)
    first[1, 1].wait_recv()
    for cp in second[1].values():
        cp.start()
    first[-1, 0].wait_recv()
    for cp in second[2].values():
        cp.start()
    same[1, 1].wait_recv()
    mate[1].start()
    same[-1, 0].wait_recv()
    mate[2].start()
    pass_on(second[0], second_on[0])
    for s in (1, -1):
        first_on[s].wait_recv()
    for cp in second[3].values():
        cp.start()
    for n in (1, 2, 3):
        pass_on(second[n], second_on[n])
    for s in (1, -1):
        same_on[s].wait_recv()
    mate[3].start()
    for n in range(4):
        second[n][1, 1].wait_recv()
        second[n][-1, 0].wait_recv()
        for s in (1, -1):
            second_on[n][s].wait_recv()
    for cp in labels + across + mate + keep:
        cp.wait()
    for group in [first, first_on, same, same_on] + second + second_on:
        for cp in group.values():
            cp.wait_send()


def gather_all(pick, off, sketch, meta):
    anyspec = pl.BlockSpec(memory_space=pl.ANY)
    bf16 = jnp.bfloat16
    return pl.pallas_call(
        gather_kernel,
        out_shape=(
            jax.ShapeDtypeStruct((8, 32, 128, 128), bf16),
            jax.ShapeDtypeStruct((8, 2048, 256), bf16),
            jax.ShapeDtypeStruct((16, 2048, 256), bf16),
            jax.ShapeDtypeStruct((8, 8, 128), jnp.int32),
        ),
        in_specs=[pl.BlockSpec(memory_space=pltpu.SMEM)] + [anyspec] * 3,
        out_specs=(anyspec,) * 4,
        scratch_shapes=[
            pltpu.VMEM((128, 128, 128), bf16),
            pltpu.VMEM((256, 128, 128), bf16),
            pltpu.VMEM((2048, 256), bf16),
            pltpu.SemaphoreType.DMA((54,)),
            pltpu.SemaphoreType.DMA((54,)),
            pltpu.SemaphoreType.DMA((6,)),
        ],
        compiler_params=pltpu.CompilerParams(has_side_effects=True, vmem_limit_bytes=20 << 20),
        name="gather",
    )(pick, off, sketch, meta)


def product_kernel(codes, blocks, line, plane_all, far, mirrors, acc, sums, plane, stage, sem, plane_sem):
    s = pl.program_id(0)

    @pl.when(s == 0)
    def _():
        load = pltpu.make_async_copy(plane_all, plane, plane_sem)
        load.start()

        def clear(i, carry):
            sums[i] = jnp.zeros((128, 256), jnp.float32)
            return carry

        lax.fori_loop(0, 256, clear, 0, unroll=4)
        load.wait()

    acc[...] = jnp.zeros_like(acc)

    def four(g, carry):
        code = [codes[s, g * 4 + u] for u in range(4)]
        rows, cols = [v // 512 for v in code], [v % 512 for v in code]
        given = [blocks[0, g * 4 + u] for u in range(4)]
        fars = [dot(given[u], plane[jnp.minimum(cols[u], 255)], ((1,), (0,)), None) for u in range(4)]
        backs = [dot(given[u], line[0, jnp.minimum(rows[u], 15)], ((0,), (0,)), None) for u in range(4)]
        for u in range(4):
            acc[rows[u]] += fars[u]
            sums[cols[u]] += backs[u].astype(jnp.bfloat16).astype(jnp.float32)
        return carry

    lax.fori_loop(0, (codes[s, 32] + 3) // 4, four, 0)
    far[0] = acc[:16].astype(jnp.bfloat16)

    @pl.when(s == 7)
    def _():
        for n in range(16):
            if n >= 2:
                pltpu.make_async_copy(stage.at[n % 2], mirrors.at[pl.ds(16 * (n - 2), 16)], sem.at[n % 2]).wait()

            def out(i, carry):
                stage[n % 2, i] = sums[16 * n + i].astype(jnp.bfloat16)
                return carry

            lax.fori_loop(0, 16, out, 0, unroll=2)
            pltpu.make_async_copy(stage.at[n % 2], mirrors.at[pl.ds(16 * n, 16)], sem.at[n % 2]).start()
        for n in (14, 15):
            pltpu.make_async_copy(stage.at[n % 2], mirrors.at[pl.ds(16 * n, 16)], sem.at[n % 2]).wait()


def products(codes, blocks, line, plane):
    bf16 = jnp.bfloat16
    return pl.pallas_call(
        product_kernel,
        grid_spec=pltpu.PrefetchScalarGridSpec(
            num_scalar_prefetch=1,
            grid=(8,),
            in_specs=[
                pl.BlockSpec((1, 32, 128, 128), lambda s, *_: (s, 0, 0, 0)),
                pl.BlockSpec((1, 16, 128, 256), lambda s, *_: (s, 0, 0, 0)),
                pl.BlockSpec(memory_space=pl.ANY),
            ],
            out_specs=(
                pl.BlockSpec((1, 16, 128, 256), lambda s, *_: (s, 0, 0, 0)),
                pl.BlockSpec(memory_space=pl.ANY),
            ),
            scratch_shapes=[
                pltpu.VMEM((17, 128, 256), jnp.float32),
                pltpu.VMEM((257, 128, 256), jnp.float32),
                pltpu.VMEM((256, 128, 256), bf16),
                pltpu.VMEM((2, 16, 128, 256), bf16),
                pltpu.SemaphoreType.DMA((2,)),
                pltpu.SemaphoreType.DMA,
            ],
        ),
        out_shape=(
            jax.ShapeDtypeStruct((8, 16, 128, 256), bf16),
            jax.ShapeDtypeStruct((256, 128, 256), bf16),
        ),
        compiler_params=pltpu.CompilerParams(vmem_limit_bytes=60 << 20),
        name="products",
    )(codes, blocks, line, plane)


def combine_kernel(total_rows, diag, sketch, far, mirrors, image, total_tiles,
                   own, one, pre, next_to, sums, two, back, gram, tiles, from_line, part, from_plane,
                   send, recv, local, gsend, grecv):
    f32 = jnp.float32
    x, y, z, c = place()
    sems = (send, recv)
    a, b = x * (1 - c) + z * c, z * (1 - c) + x * c
    me = y * 2 + c

    def along(i, j):
        return x + (1 - c) * i + c * j, y, z + c * i + (1 - c) * j, c

    order = (1, 2, 3, 0)

    def q(i, t):
        return ((a + 4 + i) % 4) * 4 + (b + t) % 4

    opposite, straight, onward, near_own, keep = {}, {}, {}, {}, []
    for n, t in enumerate(order):
        for side, (s, h) in enumerate(((1, 0), (-1, 1))):
            k = 6 * n + side
            opposite[t, side] = remote(half(mirrors.at[q(2, t)], h), pre.at[side, t], sems, k, *along(4 + s, 0))
            straight[t, side] = remote(
                half(mirrors.at[q(s, t)], 1 - h), half(one.at[side, t], 1 - h), sems, k + 2, *along(4 + s, 0))
            onward[t, side] = remote(next_to.at[side, t], half(one.at[side, t], h), sems, k + 4, *along(4 + s, 0))
            near_own[t, side] = pltpu.make_async_copy(
                half(mirrors.at[q(s, t)], h), next_to.at[side, t], local.at[5 + 2 * n + side])
    lines = []
    for n, (i, d) in enumerate(line_offsets()):
        to = ((y + i) % 4) * 2 + (c + d) % 2
        lines.append(remote(far.at[to], back.at[n + 1], sems, 24 + n, x, y + i, z, c + d))
    keep = [pltpu.make_async_copy(mirrors.at[q(0, t)], own.at[t], local.at[t]) for t in range(4)]
    keep.append(pltpu.make_async_copy(far.at[me], back.at[0], local.at[4]))
    second = [remote(sums.at[t - 1], two.at[t - 1], sems, 30 + t, *along(0, t)) for t in range(1, 4)]
    for group in (opposite, near_own):
        for t in order:
            for side in range(2):
                group[t, side].start()
    for t in order:
        for side in range(2):
            straight[t, side].start()
        if t == 1:
            for cp in lines:
                cp.start()
    for cp in keep:
        cp.start()

    def near(i, carry):
        at = pl.ds(pl.multiple_of(i * 128, 128), 128)
        image[at, :] = dot(diag[i], sketch[at, :], ((1,), (0,)), None)
        return carry

    lax.fori_loop(0, 16, near, 0)
    for t in order:
        for side in range(2):
            near_own[t, side].wait()
            opposite[t, side].wait_recv()

            def join(i, carry):
                at = pl.ds(pl.multiple_of(i * 128, 128), 128)
                total = next_to[side, t, at, :].astype(f32) + pre[side, t, at, :].astype(f32)
                next_to[side, t, at, :] = total.astype(jnp.bfloat16)
                return carry

            lax.fori_loop(0, 8, join, 0)
            onward[t, side].start()
    for t in order:
        keep[t].wait()
        for side in range(2):
            straight[t, side].wait_recv()
            onward[t, side].wait_recv()

        def add(i, carry):
            at = pl.ds(pl.multiple_of(i * 128, 128), 128)
            total = own[t, at, :].astype(f32) + one[0, t, at, :].astype(f32) + one[1, t, at, :].astype(f32)
            if t:
                sums[t - 1, at, :] = total.astype(jnp.bfloat16)
            else:
                image[at, :] += total
            return carry

        lax.fori_loop(0, 16, add, 0)
        if t:
            second[t - 1].start()
    keep[4].wait()
    for cp in lines:
        cp.wait_recv()

    def add_far(i, carry):
        at = pl.ds(pl.multiple_of(i * 128, 128), 128)
        total = image[at, :]
        for n in range(8):
            total += back[n, at, :].astype(f32)
        image[at, :] = total
        return carry

    lax.fori_loop(0, 16, add_far, 0)
    for cp in second:
        cp.wait_recv()

    def add_two(i, carry):
        at = pl.ds(pl.multiple_of(i * 128, 128), 128)
        image[at, :] += two[0, at, :].astype(f32) + two[1, at, :].astype(f32) + two[2, at, :].astype(f32)
        return carry

    lax.fori_loop(0, 16, add_two, 0)
    for cp in [*opposite.values(), *straight.values(), *onward.values()] + lines + second:
        cp.wait_send()
    gram[...] = jnp.zeros_like(gram)

    def partial(i, carry):
        h, l = split(image[pl.ds(pl.multiple_of(i * 512, 512), 512), :])
        down = ((0,), (0,))
        gram[...] += dot(h, h, down, None) + (dot(h, l, down, None) + dot(l, h, down, None))
        return carry

    lax.fori_loop(0, 4, partial, 0)
    for t, (i, j) in enumerate(TILES):
        tiles[t] = gram[8 * i : 8 * i + 8, 128 * j : 128 * j + 128] * (1.0 / total_rows)
    gsems = (gsend, grecv)
    offsets = line_offsets()
    out = []
    for n, (i, d) in enumerate(offsets):
        to = ((y + i) % 4) * 2 + (c + d) % 2
        out.append(remote(tiles.at[pl.ds(to * 6, 6)], from_line.at[me], gsems, n, x, y + i, z, c + d))
    for cp in out:
        cp.start()
    from_line[me] = tiles[pl.ds(me * 6, 6)]
    for cp in out:
        cp.wait()
    part[...] = jnp.sum(from_line[...], axis=0)
    own_q = a * 4 + b
    spread = []
    for n in range(1, 16):
        spread.append(remote(part, from_plane.at[own_q], gsems, 6 + n, *along(n // 4, n % 4)))
    for cp in spread:
        cp.start()
    from_plane[own_q] = part[...]
    for cp in spread:
        cp.wait()
    total_tiles[pl.ds(me * 6, 6)] = jnp.sum(from_plane[...], axis=0)
    everyone = []
    for n, (i, d) in enumerate(offsets):
        mine = total_tiles.at[pl.ds(me * 6, 6)]
        everyone.append(remote(mine, mine, gsems, 22 + n, x, y + i, z, c + d))
    for cp in everyone:
        cp.start()
    for cp in everyone:
        cp.wait()


def combine(total_rows, diag, sketch, far, mirrors):
    f32, bf16 = jnp.float32, jnp.bfloat16
    vmem = pl.BlockSpec(memory_space=pltpu.VMEM)
    anyspec = pl.BlockSpec(memory_space=pl.ANY)
    return pl.pallas_call(
        functools.partial(combine_kernel, total_rows),
        out_shape=(jax.ShapeDtypeStruct((2048, 256), f32), jax.ShapeDtypeStruct((48, 8, 128), f32)),
        in_specs=[vmem, vmem, anyspec, anyspec],
        out_specs=(vmem, vmem),
        scratch_shapes=[
            pltpu.VMEM((4, 2048, 256), bf16),
            pltpu.VMEM((2, 4, 2048, 256), bf16),
            pltpu.VMEM((2, 4, 1024, 256), bf16),
            pltpu.VMEM((2, 4, 1024, 256), bf16),
            pltpu.VMEM((3, 2048, 256), bf16),
            pltpu.VMEM((3, 2048, 256), bf16),
            pltpu.VMEM((8, 2048, 256), bf16),
            pltpu.VMEM((256, 256), f32),
            pltpu.VMEM((48, 8, 128), f32),
            pltpu.VMEM((8, 6, 8, 128), f32),
            pltpu.VMEM((6, 8, 128), f32),
            pltpu.VMEM((16, 6, 8, 128), f32),
            pltpu.SemaphoreType.DMA((34,)),
            pltpu.SemaphoreType.DMA((34,)),
            pltpu.SemaphoreType.DMA((13,)),
            pltpu.SemaphoreType.DMA((29,)),
            pltpu.SemaphoreType.DMA((29,)),
        ],
        compiler_params=pltpu.CompilerParams(has_side_effects=True, vmem_limit_bytes=48 << 20),
        name="combine",
    )(diag, sketch, far, mirrors)


def split_owner(col):
    owner = col // 16
    r, y = owner // 4, owner % 4
    c = r % 2
    x, z = r // 8, (r // 2) % 4
    a, b = jnp.where(c == 0, x, z), jnp.where(c == 0, z, x)
    return y * 2 + c, (a * 4 + b) * 16 + col % 16


def on_device(diag_blocks, off_blocks, col_blocks, sketch):
    entries = 128
    flat = col_blocks.reshape(entries)
    order = jnp.arange(entries)
    before = order[None, :] < order[:, None]
    group, spot = split_owner(flat)
    rank = jnp.sum(((group[:, None] == group[None, :]) & before).astype(jnp.int32), axis=1)
    slot = group * 32 + rank
    chosen = (slot[None, :] == jnp.arange(256)[:, None]).astype(jnp.int32)
    unused = 1 - jnp.sum(chosen, axis=1)
    pick = jnp.sum(chosen * order[None, :], axis=1)
    code = jnp.sum(chosen * ((order // 8) * 512 + spot)[None, :], axis=1) + unused * (16 * 512 + 256)
    count = 32 - jnp.sum(unused.reshape(8, 32), axis=1, keepdims=True)
    codes = jnp.concatenate([code.reshape(8, 32), jnp.broadcast_to(count, (8, 96))], axis=1)
    meta = jnp.broadcast_to(codes[:, None, :], (8, 8, 128))
    blocks, line, plane, metas = gather_all(pick, off_blocks.reshape(entries, 128, 128), sketch, meta)
    far, mirrors = products(
        metas[:, 0, :], blocks, line.reshape(8, 16, 128, 256), plane.reshape(256, 128, 256)
    )
    image, tiles = combine(
        262144, diag_blocks, sketch, far.reshape(8, 2048, 256), mirrors.reshape(16, 2048, 256)
    )
    return solve(image, tiles)


def solution(mesh):
    placed = (
        P(("rows", "sub"), None, None),
        P(("rows", "sub"), None, None, None),
        P(("rows", "sub"), None),
        P(("rows", "sub"), None),
    )
    return jax.shard_map(
        on_device,
        mesh=mesh,
        in_specs=placed,
        out_specs=(P(("rows", "sub"), None), P()),
        check_vma=False,
    )
```

```python
import functools

import jax
import jax.numpy as jnp
from jax import lax
from jax.experimental import pallas as pl
from jax.experimental.pallas import tpu as pltpu
from jax.sharding import PartitionSpec as P

MESH = pl.DeviceIdType.MESH
HIGHEST = lax.Precision.HIGHEST
TILES = [(i, j) for i in range(32) for j in range(2) if i < 16 or j == 1]


def dot(a, b, dims, precision=HIGHEST):
    return lax.dot_general(a, b, (dims, ((), ())), precision=precision, preferred_element_type=jnp.float32)


def split(value):
    high = value.astype(jnp.bfloat16)
    return high, (value - high.astype(jnp.float32)).astype(jnp.bfloat16)


def eliminate(s, group):
    n, wide = s.shape
    sub = lax.broadcasted_iota(jnp.int32, (n, 1), 0)

    def widen(v):
        return jnp.concatenate([v] * (wide // 128), axis=1)

    for k in range(0, n, group):
        cols = [jnp.broadcast_to(s[:, k + i : k + i + 1], (n, 128)) for i in range(group)]
        rows = [s[k + i : k + i + 1, :] for i in range(group)]
        for j in range(group):
            scale = lax.rsqrt(cols[j][k + j : k + j + 1, :])
            cols[j] = cols[j] * scale
            rows[j] = rows[j] * widen(scale)
            for i in range(j + 1, group):
                share = cols[j][k + i : k + i + 1, :]
                cols[i] = cols[i] - cols[j] * share
                rows[i] = rows[i] - rows[j] * widen(share)
        for j in range(group):
            s = s - widen(jnp.where(sub >= k + group, cols[j], 0.0)) * rows[j]
        for j in range(group):
            s = jnp.where(sub == k + j, rows[j], s)
    return s


def solve_kernel(image, tiles, basis, upper, gram, work, linv):
    for t, (i, j) in enumerate(TILES):
        gram[8 * i : 8 * i + 8, 128 * j : 128 * j + 128] = tiles[t]
    eye = lax.broadcasted_iota(jnp.int32, (128, 128), 0), lax.broadcasted_iota(jnp.int32, (128, 128), 1)
    one = (eye[0] == eye[1]).astype(jnp.float32)
    work[...] = eliminate(jnp.concatenate([gram[:128, :128], one], axis=1), 8)
    i11 = work[:, 128:]
    r12 = dot(i11, gram[:128, 128:], ((1,), (0,)))
    upper[:128, :128] = jnp.where(eye[0] <= eye[1], work[:, :128], 0.0)
    upper[:128, 128:] = r12
    linv[:128, :128] = i11
    linv[:128, 128:] = jnp.zeros((128, 128), jnp.float32)
    cross = dot(r12, i11, ((0,), (0,)))
    rest = gram[128:, 128:] - dot(r12, r12, ((0,), (0,)))
    work[...] = eliminate(jnp.concatenate([rest, one], axis=1), 8)
    i22 = work[:, 128:]
    upper[128:, :128] = jnp.zeros((128, 128), jnp.float32)
    upper[128:, 128:] = jnp.where(eye[0] <= eye[1], work[:, :128], 0.0)
    linv[128:, :128] = -dot(i22, cross, ((1,), (0,)))
    linv[128:, 128:] = i22
    high, low = split(linv[...])
    across = ((1,), (1,))

    def rows_out(i, carry):
        at = pl.ds(pl.multiple_of(i * 256, 256), 256)
        h, l = split(image[at, :])
        basis[at, :] = dot(h, high, across, None) + (dot(h, low, across, None) + dot(l, high, across, None))
        return carry

    lax.fori_loop(0, 8, rows_out, 0)


def solve(image, tiles):
    f32 = jnp.float32
    vmem = pl.BlockSpec(memory_space=pltpu.VMEM)
    return pl.pallas_call(
        solve_kernel,
        out_shape=(jax.ShapeDtypeStruct((2048, 256), f32), jax.ShapeDtypeStruct((256, 256), f32)),
        in_specs=[vmem, vmem],
        out_specs=(vmem, vmem),
        scratch_shapes=[pltpu.VMEM((256, 256), f32), pltpu.VMEM((128, 256), f32), pltpu.VMEM((256, 256), f32)],
        compiler_params=pltpu.CompilerParams(vmem_limit_bytes=16 << 20),
        name="solve",
    )(image, tiles)


def place():
    r, y = lax.axis_index("rows"), lax.axis_index("sub")
    return r // 8, y, (r // 2) % 4, r % 2


def remote(src, dst, sems, k, x, y, z, c):
    send, recv = sems
    return pltpu.make_async_remote_copy(
        src_ref=src, dst_ref=dst, send_sem=send.at[k], recv_sem=recv.at[k],
        device_id=((x % 4) * 8 + (z % 4) * 2 + c % 2, y % 4), device_id_type=MESH)


def meet(partners):
    barrier = pltpu.get_barrier_semaphore()
    for x, y, z, c in partners:
        device = ((x % 4) * 8 + (z % 4) * 2 + c % 2, y % 4)
        pl.semaphore_signal(barrier, inc=1, device_id=device, device_id_type=MESH)
    pl.semaphore_wait(barrier, len(partners))


def line_offsets():
    return [(i, d) for i in range(4) for d in range(2) if (i, d) != (0, 0)]


def half(ref, h):
    return ref.at[pl.ds(1024 * h, 1024), :]


def gather_kernel(pick, off, sketch, meta, blocks, line, plane, metas, given, packed, held, send, recv, local):
    x, y, z, c = place()
    sems = (send, recv)
    a, b = x * (1 - c) + z * c, z * (1 - c) + x * c
    me = y * 2 + c
    own_q = a * 4 + b

    def q(i, j):
        return ((a + i) % 4) * 4 + (b + j) % 4

    def along(i, j):
        return x + 3 * 4 + (1 - c) * i + c * j, y, z + 3 * 4 + c * i + (1 - c) * j, c

    def line_at(i, d=0):
        return x, y + 4 + i, z, c + d

    def l(i):
        return ((y + 4 + i) % 4) * 2 + c

    meet([along(1, 0), along(-1, 0), along(0, 1), along(0, -1)] + [line_at(i, d) for i, d in line_offsets()])

    def slots(j):
        return packed.at[pl.ds(j * 32, 32)]

    take = pltpu.make_async_copy(off, given, local.at[0])
    fetch = pltpu.make_async_copy(sketch, held, local.at[1])
    keep = [
        pltpu.make_async_copy(held, plane.at[own_q], local.at[2]),
        pltpu.make_async_copy(held, line.at[me], local.at[3]),
        pltpu.make_async_copy(slots(me), blocks.at[me], local.at[4]),
        pltpu.make_async_copy(meta.at[me], metas.at[me], local.at[5]),
    ]

    def ring(source, slot, to, base):
        return {
            (s, h): remote(half(source, h), half(slot, h), sems, base + 2 * (s < 0) + h, *to(s))
            for s in (1, -1) for h in range(2)
        }

    def onward(slots, to, base):
        return {
            s: remote(half(slots[s], h), half(slots[s], h), sems, base + h, *to(s))
            for s, h in ((1, 0), (-1, 1))
        }

    to_a = lambda s: along(s, 0)
    first = ring(sketch, plane.at[own_q], to_a, 0)
    first_on = onward({1: plane.at[q(3, 0)], -1: plane.at[q(1, 0)]}, to_a, 4)
    same = ring(sketch, line.at[me], line_at, 6)
    same_on = onward({1: line.at[l(-1)], -1: line.at[l(1)]}, line_at, 10)
    mate = [remote(sketch, line.at[me], sems, 12, *line_at(0, 1))]
    mate += [remote(line.at[l(i)], line.at[l(i)], sems, 12 + n, *line_at(0, 1)) for n, i in ((1, -1), (2, 1), (3, 2))]
    to_b = lambda s: along(0, s)
    second, second_on = [], []
    for n, i in enumerate((0, 3, 1, 2)):
        source = sketch if i == 0 else plane.at[q(i, 0)]
        second.append(ring(source, plane.at[q(i, 0)], to_b, 16 + 6 * n))
        second_on.append(onward({1: plane.at[q(i, 3)], -1: plane.at[q(i, 1)]}, to_b, 20 + 6 * n))
    across, labels = [], []
    for n, (i, d) in enumerate(line_offsets()):
        to = ((y + i) % 4) * 2 + (c + d) % 2
        across.append(remote(slots(to), blocks.at[me], sems, 40 + n, *line_at(i, d)))
        labels.append(remote(meta.at[to], metas.at[me], sems, 47 + n, *line_at(i, d)))
    take.start()
    for cp in list(same.values()) + list(first.values()) + list(second[0].values()) + mate[:1] + labels:
        cp.start()
    fetch.start()
    take.wait()

    def place_block(t, carry):
        packed[t] = given[pick[t]]
        return carry

    lax.fori_loop(0, 256, place_block, 0, unroll=8)
    for cp in across:
        cp.start()
    fetch.wait()
    for cp in keep:
        cp.start()

    def pass_on(ring_, on_):
        ring_[1, 0].wait_recv()
        on_[1].start()
        ring_[-1, 1].wait_recv()
        on_[-1].start()

    pass_on(same, same_on)
    pass_on(first, first_on)
    first[1, 1].wait_recv()
    for cp in second[1].values():
        cp.start()
    first[-1, 0].wait_recv()
    for cp in second[2].values():
        cp.start()
    same[1, 1].wait_recv()
    mate[1].start()
    same[-1, 0].wait_recv()
    mate[2].start()
    pass_on(second[0], second_on[0])
    for s in (1, -1):
        first_on[s].wait_recv()
    for cp in second[3].values():
        cp.start()
    for n in (1, 2, 3):
        pass_on(second[n], second_on[n])
    for s in (1, -1):
        same_on[s].wait_recv()
    mate[3].start()
    for n in range(4):
        second[n][1, 1].wait_recv()
        second[n][-1, 0].wait_recv()
        for s in (1, -1):
            second_on[n][s].wait_recv()
    for cp in labels + across + mate + keep:
        cp.wait()
    for group in [first, first_on, same, same_on] + second + second_on:
        for cp in group.values():
            cp.wait_send()


def gather_all(pick, off, sketch, meta):
    anyspec = pl.BlockSpec(memory_space=pl.ANY)
    bf16 = jnp.bfloat16
    return pl.pallas_call(
        gather_kernel,
        out_shape=(
            jax.ShapeDtypeStruct((8, 32, 128, 128), bf16),
            jax.ShapeDtypeStruct((8, 2048, 256), bf16),
            jax.ShapeDtypeStruct((16, 2048, 256), bf16),
            jax.ShapeDtypeStruct((8, 8, 128), jnp.int32),
        ),
        in_specs=[pl.BlockSpec(memory_space=pltpu.SMEM)] + [anyspec] * 3,
        out_specs=(anyspec,) * 4,
        scratch_shapes=[
            pltpu.VMEM((128, 128, 128), bf16),
            pltpu.VMEM((256, 128, 128), bf16),
            pltpu.VMEM((2048, 256), bf16),
            pltpu.SemaphoreType.DMA((54,)),
            pltpu.SemaphoreType.DMA((54,)),
            pltpu.SemaphoreType.DMA((6,)),
        ],
        compiler_params=pltpu.CompilerParams(has_side_effects=True, collective_id=0, vmem_limit_bytes=60 << 20),
        name="gather",
    )(pick, off, sketch, meta)


def product_kernel(codes, blocks, line, plane_all, far, mirrors, acc, sums, plane, stage, row_used, col_used, sem, plane_sem):
    step = pl.program_id(0)
    s = step % 8
    load = pltpu.make_async_copy(plane_all, plane, plane_sem)
    groups = (codes[s, 32] + 3) // 4

    @pl.when(step == 0)
    def _():
        load.start()

        def unused(i, carry):
            col_used[i] = 0
            return carry

        lax.fori_loop(0, 257, unused, 0)

    def add(total, used, at, value):
        total[at] = jnp.where(used[at] > 0, total[at], 0.0) + value
        used[at] = 1

    @pl.when(step < 8)
    def _():
        def four(g, carry):
            code = [codes[s, g * 4 + u] for u in range(4)]
            backs = [
                dot(blocks[0, g * 4 + u], line[0, jnp.minimum(code[u] // 512, 15)], ((0,), (0,)), None)
                for u in range(4)
            ]
            for u in range(4):
                add(sums, col_used, code[u] % 512, backs[u].astype(jnp.bfloat16).astype(jnp.float32))
            return carry

        lax.fori_loop(0, groups, four, 0)

    @pl.when(step == 8)
    def _():
        load.wait()

    def written(n):
        return pltpu.make_async_copy(stage.at[n % 2], mirrors.at[pl.ds(16 * n, 16)], sem.at[n % 2])

    @pl.when(step >= 8)
    def _():
        for i in range(17):
            row_used[i] = 0

        def four(g, carry):
            code = [codes[s, g * 4 + u] for u in range(4)]
            fars = [
                dot(blocks[0, g * 4 + u], plane[jnp.minimum(code[u] % 512, 255)], ((1,), (0,)), None)
                for u in range(4)
            ]
            for u in range(4):
                add(acc, row_used, code[u] // 512, fars[u])
            return carry

        lax.fori_loop(0, groups, four, 0)

        def out_far(i, carry):
            far[0, i] = jnp.where(row_used[i] > 0, acc[i], 0.0).astype(jnp.bfloat16)
            return carry

        lax.fori_loop(0, 16, out_far, 0, unroll=2)
        for h in range(2):
            n = 2 * s + h

            @pl.when(s > 0)
            def _():
                written(n - 2).wait()

            def out(i, carry):
                at = 16 * n + i
                stage[h, i] = jnp.where(col_used[at] > 0, sums[at], 0.0).astype(jnp.bfloat16)
                return carry

            lax.fori_loop(0, 16, out, 0, unroll=2)
            written(n).start()

    @pl.when(step == 15)
    def _():
        for n in (14, 15):
            written(n).wait()


def products(codes, blocks, line, plane):
    bf16 = jnp.bfloat16
    return pl.pallas_call(
        product_kernel,
        grid_spec=pltpu.PrefetchScalarGridSpec(
            num_scalar_prefetch=1,
            grid=(16,),
            in_specs=[
                pl.BlockSpec((1, 32, 128, 128), lambda s, *_: (s % 8, 0, 0, 0)),
                pl.BlockSpec((1, 16, 128, 256), lambda s, *_: (jnp.minimum(s, 7), 0, 0, 0)),
                pl.BlockSpec(memory_space=pl.ANY),
            ],
            out_specs=(
                pl.BlockSpec((1, 16, 128, 256), lambda s, *_: (jnp.maximum(s - 8, 0), 0, 0, 0)),
                pl.BlockSpec(memory_space=pl.ANY),
            ),
            scratch_shapes=[
                pltpu.VMEM((17, 128, 256), jnp.float32),
                pltpu.VMEM((257, 128, 256), jnp.float32),
                pltpu.VMEM((256, 128, 256), bf16),
                pltpu.VMEM((2, 16, 128, 256), bf16),
                pltpu.SMEM((17,), jnp.int32),
                pltpu.SMEM((257,), jnp.int32),
                pltpu.SemaphoreType.DMA((2,)),
                pltpu.SemaphoreType.DMA,
            ],
        ),
        out_shape=(
            jax.ShapeDtypeStruct((8, 16, 128, 256), bf16),
            jax.ShapeDtypeStruct((256, 128, 256), bf16),
        ),
        compiler_params=pltpu.CompilerParams(vmem_limit_bytes=60 << 20),
        name="products",
    )(codes, blocks, line, plane)


def combine_kernel(total_rows, diag, sketch, far, mirrors, image, total_tiles,
                   own, one, pre, next_to, sums, two, back, gram, tiles, from_line, part, from_plane,
                   send, recv, local, gsend, grecv):
    f32 = jnp.float32
    x, y, z, c = place()
    sems = (send, recv)
    a, b = x * (1 - c) + z * c, z * (1 - c) + x * c
    me = y * 2 + c

    def along(i, j):
        return x + (1 - c) * i + c * j, y, z + c * i + (1 - c) * j, c

    order = (1, 2, 3, 0)
    meet([along(n // 4, n % 4) for n in range(1, 16)] + [(x, y + i, z, c + d) for i, d in line_offsets()])

    def q(i, t):
        return ((a + 4 + i) % 4) * 4 + (b + t) % 4

    opposite, straight, onward, near_own, keep = {}, {}, {}, {}, []
    for n, t in enumerate(order):
        for side, (s, h) in enumerate(((1, 0), (-1, 1))):
            k = 6 * n + side
            opposite[t, side] = remote(half(mirrors.at[q(2, t)], h), pre.at[side, t], sems, k, *along(4 + s, 0))
            straight[t, side] = remote(
                half(mirrors.at[q(s, t)], 1 - h), half(one.at[side, t], 1 - h), sems, k + 2, *along(4 + s, 0))
            onward[t, side] = remote(next_to.at[side, t], half(one.at[side, t], h), sems, k + 4, *along(4 + s, 0))
            near_own[t, side] = pltpu.make_async_copy(
                half(mirrors.at[q(s, t)], h), next_to.at[side, t], local.at[5 + 2 * n + side])
    lines = []
    for n, (i, d) in enumerate(line_offsets()):
        to = ((y + i) % 4) * 2 + (c + d) % 2
        lines.append(remote(far.at[to], back.at[n + 1], sems, 24 + n, x, y + i, z, c + d))
    keep = [pltpu.make_async_copy(mirrors.at[q(0, t)], own.at[t], local.at[t]) for t in range(4)]
    keep.append(pltpu.make_async_copy(far.at[me], back.at[0], local.at[4]))
    second = [remote(sums.at[t - 1], two.at[t - 1], sems, 30 + t, *along(0, t)) for t in range(1, 4)]
    for group in (opposite, near_own):
        for t in order:
            for side in range(2):
                group[t, side].start()
    for t in order:
        for side in range(2):
            straight[t, side].start()
        if t == 1:
            for cp in lines:
                cp.start()
    for cp in keep:
        cp.start()

    def near(i, carry):
        at = pl.ds(pl.multiple_of(i * 128, 128), 128)
        image[at, :] = dot(diag[i], sketch[at, :], ((1,), (0,)), None)
        return carry

    lax.fori_loop(0, 16, near, 0)
    for t in order:
        for side in range(2):
            near_own[t, side].wait()
            opposite[t, side].wait_recv()

            def join(i, carry):
                at = pl.ds(pl.multiple_of(i * 128, 128), 128)
                total = next_to[side, t, at, :].astype(f32) + pre[side, t, at, :].astype(f32)
                next_to[side, t, at, :] = total.astype(jnp.bfloat16)
                return carry

            lax.fori_loop(0, 8, join, 0)
            onward[t, side].start()
    for t in order:
        keep[t].wait()
        for side in range(2):
            straight[t, side].wait_recv()
            onward[t, side].wait_recv()

        def add(i, carry):
            at = pl.ds(pl.multiple_of(i * 128, 128), 128)
            total = own[t, at, :].astype(f32) + one[0, t, at, :].astype(f32) + one[1, t, at, :].astype(f32)
            if t:
                sums[t - 1, at, :] = total.astype(jnp.bfloat16)
            else:
                image[at, :] += total
            return carry

        lax.fori_loop(0, 16, add, 0)
        if t:
            second[t - 1].start()
    keep[4].wait()
    for cp in lines:
        cp.wait_recv()

    def add_far(i, carry):
        at = pl.ds(pl.multiple_of(i * 128, 128), 128)
        total = image[at, :]
        for n in range(8):
            total += back[n, at, :].astype(f32)
        image[at, :] = total
        return carry

    lax.fori_loop(0, 16, add_far, 0)
    for cp in second:
        cp.wait_recv()

    def add_two(i, carry):
        at = pl.ds(pl.multiple_of(i * 128, 128), 128)
        image[at, :] += two[0, at, :].astype(f32) + two[1, at, :].astype(f32) + two[2, at, :].astype(f32)
        return carry

    lax.fori_loop(0, 16, add_two, 0)
    for cp in [*opposite.values(), *straight.values(), *onward.values()] + lines + second:
        cp.wait_send()
    gram[...] = jnp.zeros_like(gram)

    def partial(i, carry):
        h, l = split(image[pl.ds(pl.multiple_of(i * 512, 512), 512), :])
        down = ((0,), (0,))
        gram[...] += dot(h, h, down, None) + (dot(h, l, down, None) + dot(l, h, down, None))
        return carry

    lax.fori_loop(0, 4, partial, 0)
    for t, (i, j) in enumerate(TILES):
        tiles[t] = gram[8 * i : 8 * i + 8, 128 * j : 128 * j + 128] * (1.0 / total_rows)
    gsems = (gsend, grecv)
    offsets = line_offsets()
    out = []
    for n, (i, d) in enumerate(offsets):
        to = ((y + i) % 4) * 2 + (c + d) % 2
        out.append(remote(tiles.at[pl.ds(to * 6, 6)], from_line.at[me], gsems, n, x, y + i, z, c + d))
    for cp in out:
        cp.start()
    from_line[me] = tiles[pl.ds(me * 6, 6)]
    for cp in out:
        cp.wait()
    part[...] = jnp.sum(from_line[...], axis=0)
    own_q = a * 4 + b
    spread = []
    for n in range(1, 16):
        spread.append(remote(part, from_plane.at[own_q], gsems, 6 + n, *along(n // 4, n % 4)))
    for cp in spread:
        cp.start()
    from_plane[own_q] = part[...]
    for cp in spread:
        cp.wait()
    total_tiles[pl.ds(me * 6, 6)] = jnp.sum(from_plane[...], axis=0)
    everyone = []
    for n, (i, d) in enumerate(offsets):
        mine = total_tiles.at[pl.ds(me * 6, 6)]
        everyone.append(remote(mine, mine, gsems, 22 + n, x, y + i, z, c + d))
    for cp in everyone:
        cp.start()
    for cp in everyone:
        cp.wait()


def combine(total_rows, diag, sketch, far, mirrors):
    f32, bf16 = jnp.float32, jnp.bfloat16
    vmem = pl.BlockSpec(memory_space=pltpu.VMEM)
    anyspec = pl.BlockSpec(memory_space=pl.ANY)
    return pl.pallas_call(
        functools.partial(combine_kernel, total_rows),
        out_shape=(jax.ShapeDtypeStruct((2048, 256), f32), jax.ShapeDtypeStruct((48, 8, 128), f32)),
        in_specs=[vmem, vmem, anyspec, anyspec],
        out_specs=(vmem, vmem),
        scratch_shapes=[
            pltpu.VMEM((4, 2048, 256), bf16),
            pltpu.VMEM((2, 4, 2048, 256), bf16),
            pltpu.VMEM((2, 4, 1024, 256), bf16),
            pltpu.VMEM((2, 4, 1024, 256), bf16),
            pltpu.VMEM((3, 2048, 256), bf16),
            pltpu.VMEM((3, 2048, 256), bf16),
            pltpu.VMEM((8, 2048, 256), bf16),
            pltpu.VMEM((256, 256), f32),
            pltpu.VMEM((48, 8, 128), f32),
            pltpu.VMEM((8, 6, 8, 128), f32),
            pltpu.VMEM((6, 8, 128), f32),
            pltpu.VMEM((16, 6, 8, 128), f32),
            pltpu.SemaphoreType.DMA((34,)),
            pltpu.SemaphoreType.DMA((34,)),
            pltpu.SemaphoreType.DMA((13,)),
            pltpu.SemaphoreType.DMA((29,)),
            pltpu.SemaphoreType.DMA((29,)),
        ],
        compiler_params=pltpu.CompilerParams(has_side_effects=True, collective_id=1, vmem_limit_bytes=48 << 20),
        name="combine",
    )(diag, sketch, far, mirrors)


def split_owner(col):
    owner = col // 16
    r, y = owner // 4, owner % 4
    c = r % 2
    x, z = r // 8, (r // 2) % 4
    a, b = jnp.where(c == 0, x, z), jnp.where(c == 0, z, x)
    return y * 2 + c, (a * 4 + b) * 16 + col % 16


def on_device(diag_blocks, off_blocks, col_blocks, sketch):
    entries = 128
    flat = col_blocks.reshape(entries)
    order = jnp.arange(entries)
    before = order[None, :] < order[:, None]
    group, spot = split_owner(flat)
    rank = jnp.sum(((group[:, None] == group[None, :]) & before).astype(jnp.int32), axis=1)
    slot = group * 32 + rank
    chosen = (slot[None, :] == jnp.arange(256)[:, None]).astype(jnp.int32)
    unused = 1 - jnp.sum(chosen, axis=1)
    pick = jnp.sum(chosen * order[None, :], axis=1)
    code = jnp.sum(chosen * ((order // 8) * 512 + spot)[None, :], axis=1) + unused * (16 * 512 + 256)
    count = 32 - jnp.sum(unused.reshape(8, 32), axis=1, keepdims=True)
    codes = jnp.concatenate([code.reshape(8, 32), jnp.broadcast_to(count, (8, 96))], axis=1)
    meta = jnp.broadcast_to(codes[:, None, :], (8, 8, 128))
    blocks, line, plane, metas = gather_all(pick, off_blocks.reshape(entries, 128, 128), sketch, meta)
    far, mirrors = products(
        metas[:, 0, :], blocks, line.reshape(8, 16, 128, 256), plane.reshape(256, 128, 256)
    )
    image, tiles = combine(
        262144, diag_blocks, sketch, far.reshape(8, 2048, 256), mirrors.reshape(16, 2048, 256)
    )
    return solve(image, tiles)


def solution(mesh):
    placed = (
        P(("rows", "sub"), None, None),
        P(("rows", "sub"), None, None, None),
        P(("rows", "sub"), None),
        P(("rows", "sub"), None),
    )
    return jax.shard_map(
        on_device,
        mesh=mesh,
        in_specs=placed,
        out_specs=(P(("rows", "sub"), None), P()),
        check_vma=False,
    )
```

```python
import functools

import jax
import jax.numpy as jnp
from jax import lax
from jax.experimental import pallas as pl
from jax.experimental.pallas import tpu as pltpu
from jax.sharding import PartitionSpec as P

MESH = pl.DeviceIdType.MESH
HIGHEST = lax.Precision.HIGHEST
TILES = [(i, j) for i in range(32) for j in range(2) if i < 16 or j == 1]


def dot(a, b, dims, precision=HIGHEST):
    return lax.dot_general(a, b, (dims, ((), ())), precision=precision, preferred_element_type=jnp.float32)


def split(value):
    high = value.astype(jnp.bfloat16)
    return high, (value - high.astype(jnp.float32)).astype(jnp.bfloat16)


def eliminate(s, group):
    n, wide = s.shape
    sub = lax.broadcasted_iota(jnp.int32, (n, 1), 0)

    def widen(v):
        return jnp.concatenate([v] * (wide // 128), axis=1)

    for k in range(0, n, group):
        cols = [jnp.broadcast_to(s[:, k + i : k + i + 1], (n, 128)) for i in range(group)]
        rows = [s[k + i : k + i + 1, :] for i in range(group)]
        for j in range(group):
            scale = lax.rsqrt(cols[j][k + j : k + j + 1, :])
            cols[j] = cols[j] * scale
            rows[j] = rows[j] * widen(scale)
            for i in range(j + 1, group):
                share = cols[j][k + i : k + i + 1, :]
                cols[i] = cols[i] - cols[j] * share
                rows[i] = rows[i] - rows[j] * widen(share)
        for j in range(group):
            s = s - widen(jnp.where(sub >= k + group, cols[j], 0.0)) * rows[j]
        for j in range(group):
            s = jnp.where(sub == k + j, rows[j], s)
    return s


def solve_kernel(image, tiles, basis, upper, gram, work, linv):
    for t, (i, j) in enumerate(TILES):
        gram[8 * i : 8 * i + 8, 128 * j : 128 * j + 128] = tiles[t]
    eye = lax.broadcasted_iota(jnp.int32, (128, 128), 0), lax.broadcasted_iota(jnp.int32, (128, 128), 1)
    one = (eye[0] == eye[1]).astype(jnp.float32)
    work[...] = eliminate(jnp.concatenate([gram[:128, :128], one], axis=1), 8)
    i11 = work[:, 128:]
    r12 = dot(i11, gram[:128, 128:], ((1,), (0,)))
    upper[:128, :128] = jnp.where(eye[0] <= eye[1], work[:, :128], 0.0)
    upper[:128, 128:] = r12
    linv[:128, :128] = i11
    linv[:128, 128:] = jnp.zeros((128, 128), jnp.float32)
    cross = dot(r12, i11, ((0,), (0,)))
    rest = gram[128:, 128:] - dot(r12, r12, ((0,), (0,)))
    work[...] = eliminate(jnp.concatenate([rest, one], axis=1), 8)
    i22 = work[:, 128:]
    upper[128:, :128] = jnp.zeros((128, 128), jnp.float32)
    upper[128:, 128:] = jnp.where(eye[0] <= eye[1], work[:, :128], 0.0)
    linv[128:, :128] = -dot(i22, cross, ((1,), (0,)))
    linv[128:, 128:] = i22
    high, low = split(linv[...])
    across = ((1,), (1,))

    def rows_out(i, carry):
        at = pl.ds(pl.multiple_of(i * 256, 256), 256)
        h, l = split(image[at, :])
        basis[at, :] = dot(h, high, across, None) + (dot(h, low, across, None) + dot(l, high, across, None))
        return carry

    lax.fori_loop(0, 8, rows_out, 0)


def solve(image, tiles):
    f32 = jnp.float32
    vmem = pl.BlockSpec(memory_space=pltpu.VMEM)
    return pl.pallas_call(
        solve_kernel,
        out_shape=(jax.ShapeDtypeStruct((2048, 256), f32), jax.ShapeDtypeStruct((256, 256), f32)),
        in_specs=[vmem, vmem],
        out_specs=(vmem, vmem),
        scratch_shapes=[pltpu.VMEM((256, 256), f32), pltpu.VMEM((128, 256), f32), pltpu.VMEM((256, 256), f32)],
        compiler_params=pltpu.CompilerParams(vmem_limit_bytes=16 << 20),
        name="solve",
    )(image, tiles)


def place():
    r, y = lax.axis_index("rows"), lax.axis_index("sub")
    return r // 8, y, (r // 2) % 4, r % 2


def remote(src, dst, sems, k, x, y, z, c):
    send, recv = sems
    return pltpu.make_async_remote_copy(
        src_ref=src, dst_ref=dst, send_sem=send.at[k], recv_sem=recv.at[k],
        device_id=((x % 4) * 8 + (z % 4) * 2 + c % 2, y % 4), device_id_type=MESH)


def meet(partners):
    barrier = pltpu.get_barrier_semaphore()
    for x, y, z, c in partners:
        device = ((x % 4) * 8 + (z % 4) * 2 + c % 2, y % 4)
        pl.semaphore_signal(barrier, inc=1, device_id=device, device_id_type=MESH)
    pl.semaphore_wait(barrier, len(partners))


def line_offsets():
    return [(i, d) for i in range(4) for d in range(2) if (i, d) != (0, 0)]


def half(ref, h):
    return ref.at[pl.ds(1024 * h, 1024), :]


def gather_kernel(pick, off, sketch, meta, blocks, line, plane, metas, given, packed, held, send, recv, local):
    x, y, z, c = place()
    sems = (send, recv)
    a, b = x * (1 - c) + z * c, z * (1 - c) + x * c
    me = y * 2 + c
    own_q = a * 4 + b

    def q(i, j):
        return ((a + i) % 4) * 4 + (b + j) % 4

    def along(i, j):
        return x + 3 * 4 + (1 - c) * i + c * j, y, z + 3 * 4 + c * i + (1 - c) * j, c

    def line_at(i, d=0):
        return x, y + 4 + i, z, c + d

    def l(i):
        return ((y + 4 + i) % 4) * 2 + c

    meet([along(1, 0), along(-1, 0), along(0, 1), along(0, -1)] + [line_at(i, d) for i, d in line_offsets()])

    def slots(j):
        return packed.at[pl.ds(j * 32, 32)]

    take = pltpu.make_async_copy(off, given, local.at[0])
    fetch = pltpu.make_async_copy(sketch, held, local.at[1])
    keep = [
        pltpu.make_async_copy(held, plane.at[own_q], local.at[2]),
        pltpu.make_async_copy(held, line.at[me], local.at[3]),
        pltpu.make_async_copy(slots(me), blocks.at[me], local.at[4]),
        pltpu.make_async_copy(meta.at[me], metas.at[me], local.at[5]),
    ]

    def ring(source, slot, to, base):
        return {
            (s, h): remote(half(source, h), half(slot, h), sems, base + 2 * (s < 0) + h, *to(s))
            for s in (1, -1) for h in range(2)
        }

    def onward(slots, to, base):
        return {
            s: remote(half(slots[s], h), half(slots[s], h), sems, base + h, *to(s))
            for s, h in ((1, 0), (-1, 1))
        }

    to_a = lambda s: along(s, 0)
    first = ring(sketch, plane.at[own_q], to_a, 0)
    first_on = onward({1: plane.at[q(3, 0)], -1: plane.at[q(1, 0)]}, to_a, 4)
    same = ring(sketch, line.at[me], line_at, 6)
    same_on = onward({1: line.at[l(-1)], -1: line.at[l(1)]}, line_at, 10)
    mate = [remote(sketch, line.at[me], sems, 12, *line_at(0, 1))]
    mate += [remote(line.at[l(i)], line.at[l(i)], sems, 12 + n, *line_at(0, 1)) for n, i in ((1, -1), (2, 1), (3, 2))]
    to_b = lambda s: along(0, s)
    second, second_on = [], []
    for n, i in enumerate((0, 3, 1, 2)):
        source = sketch if i == 0 else plane.at[q(i, 0)]
        second.append(ring(source, plane.at[q(i, 0)], to_b, 16 + 6 * n))
        second_on.append(onward({1: plane.at[q(i, 3)], -1: plane.at[q(i, 1)]}, to_b, 20 + 6 * n))
    across, labels = [], []
    for n, (i, d) in enumerate(line_offsets()):
        to = ((y + i) % 4) * 2 + (c + d) % 2
        across.append(remote(slots(to), blocks.at[me], sems, 40 + n, *line_at(i, d)))
        labels.append(remote(meta.at[to], metas.at[me], sems, 47 + n, *line_at(i, d)))
    take.start()
    for cp in list(same.values()) + list(first.values()) + list(second[0].values()) + mate[:1] + labels:
        cp.start()
    fetch.start()
    take.wait()

    def place_block(t, carry):
        packed[t] = given[pick[t]]
        return carry

    lax.fori_loop(0, 256, place_block, 0, unroll=8)
    for cp in across:
        cp.start()
    fetch.wait()
    for cp in keep:
        cp.start()

    def pass_on(ring_, on_):
        ring_[1, 0].wait_recv()
        on_[1].start()
        ring_[-1, 1].wait_recv()
        on_[-1].start()

    pass_on(same, same_on)
    pass_on(first, first_on)
    first[1, 1].wait_recv()
    for cp in second[1].values():
        cp.start()
    first[-1, 0].wait_recv()
    for cp in second[2].values():
        cp.start()
    same[1, 1].wait_recv()
    mate[1].start()
    same[-1, 0].wait_recv()
    mate[2].start()
    pass_on(second[0], second_on[0])
    for s in (1, -1):
        first_on[s].wait_recv()
    for cp in second[3].values():
        cp.start()
    for n in (1, 2, 3):
        pass_on(second[n], second_on[n])
    for s in (1, -1):
        same_on[s].wait_recv()
    mate[3].start()
    for n in range(4):
        second[n][1, 1].wait_recv()
        second[n][-1, 0].wait_recv()
        for s in (1, -1):
            second_on[n][s].wait_recv()
    for cp in labels + across + mate + keep:
        cp.wait()
    for group in [first, first_on, same, same_on] + second + second_on:
        for cp in group.values():
            cp.wait_send()


def gather_all(pick, off, sketch, meta):
    anyspec = pl.BlockSpec(memory_space=pl.ANY)
    bf16 = jnp.bfloat16
    return pl.pallas_call(
        gather_kernel,
        out_shape=(
            jax.ShapeDtypeStruct((8, 32, 128, 128), bf16),
            jax.ShapeDtypeStruct((8, 2048, 256), bf16),
            jax.ShapeDtypeStruct((16, 2048, 256), bf16),
            jax.ShapeDtypeStruct((8, 8, 128), jnp.int32),
        ),
        in_specs=[pl.BlockSpec(memory_space=pltpu.SMEM)] + [anyspec] * 3,
        out_specs=(anyspec,) * 4,
        scratch_shapes=[
            pltpu.VMEM((128, 128, 128), bf16),
            pltpu.VMEM((256, 128, 128), bf16),
            pltpu.VMEM((2048, 256), bf16),
            pltpu.SemaphoreType.DMA((54,)),
            pltpu.SemaphoreType.DMA((54,)),
            pltpu.SemaphoreType.DMA((6,)),
        ],
        compiler_params=pltpu.CompilerParams(has_side_effects=True, collective_id=0, vmem_limit_bytes=60 << 20),
        name="gather",
    )(pick, off, sketch, meta)


def product_kernel(codes, blocks_all, line_all, plane, far, mirrors, acc, sums, blocks, line, wanted, fars_out, stage,
                   in_sem, want_sem, far_sem, sem):
    def want(s, t):
        column = jnp.minimum(codes[s, t] % 512, 255)
        return pltpu.make_async_copy(plane.at[column], wanted.at[s % 2, t], want_sem.at[s % 2])

    def given_in(s):
        p = s % 2
        return (
            pltpu.make_async_copy(blocks_all.at[s], blocks.at[p], in_sem.at[p, 0]),
            pltpu.make_async_copy(line_all.at[s], line.at[p], in_sem.at[p, 1]),
        )

    def ask(s):
        for cp in given_in(s):
            cp.start()

        def one(t, carry):
            want(s, t).start()
            return carry

        lax.fori_loop(0, codes[s, 32], one, 0)

    def far_copy(s):
        return pltpu.make_async_copy(fars_out.at[s % 2], far.at[s], far_sem.at[s % 2])

    ask(0)

    def clear(i, carry):
        sums[i] = jnp.zeros((128, 256), jnp.float32)
        return carry

    lax.fori_loop(0, 256, clear, 0, unroll=4)

    def source(s, carry):
        @pl.when(s < 7)
        def _():
            ask(s + 1)

        acc[...] = jnp.zeros_like(acc)

        def arrived(t, c):
            want(s, t).wait()
            return c

        for cp in given_in(s):
            cp.wait()
        lax.fori_loop(0, codes[s, 32], arrived, 0)

        def four(g, c):
            code = [codes[s, g * 4 + u] for u in range(4)]
            rows, cols = [v // 512 for v in code], [v % 512 for v in code]
            given = [blocks[s % 2, g * 4 + u] for u in range(4)]
            fars = [dot(given[u], wanted[s % 2, g * 4 + u], ((1,), (0,)), None) for u in range(4)]
            backs = [dot(given[u], line[s % 2, jnp.minimum(rows[u], 15)], ((0,), (0,)), None) for u in range(4)]
            for u in range(4):
                acc[rows[u]] += fars[u]
                sums[cols[u]] += backs[u].astype(jnp.bfloat16).astype(jnp.float32)
            return c

        lax.fori_loop(0, (codes[s, 32] + 3) // 4, four, 0)

        @pl.when(s >= 2)
        def _():
            far_copy(s - 2).wait()

        def out_far(i, c):
            fars_out[s % 2, i] = acc[i].astype(jnp.bfloat16)
            return c

        lax.fori_loop(0, 16, out_far, 0, unroll=2)
        far_copy(s).start()
        return carry

    lax.fori_loop(0, 8, source, 0)

    def written(n):
        return pltpu.make_async_copy(stage.at[n % 8], mirrors.at[pl.ds(16 * n, 16)], sem.at[n % 8])

    for n in range(16):
        if n >= 8:
            written(n - 8).wait()

        def out(i, carry):
            stage[n % 8, i] = sums[16 * n + i].astype(jnp.bfloat16)
            return carry

        lax.fori_loop(0, 16, out, 0, unroll=2)
        written(n).start()
    for n in range(8, 16):
        written(n).wait()
    for n in (6, 7):
        far_copy(n).wait()


def products(codes, blocks, line, plane):
    bf16 = jnp.bfloat16
    anyspec = pl.BlockSpec(memory_space=pl.ANY)
    return pl.pallas_call(
        product_kernel,
        in_specs=[pl.BlockSpec(memory_space=pltpu.SMEM), anyspec, anyspec, anyspec],
        out_specs=(anyspec, anyspec),
        scratch_shapes=[
            pltpu.VMEM((17, 128, 256), jnp.float32),
            pltpu.VMEM((257, 128, 256), jnp.float32),
            pltpu.VMEM((2, 32, 128, 128), bf16),
            pltpu.VMEM((2, 16, 128, 256), bf16),
            pltpu.VMEM((2, 32, 128, 256), bf16),
            pltpu.VMEM((2, 16, 128, 256), bf16),
            pltpu.VMEM((8, 16, 128, 256), bf16),
            pltpu.SemaphoreType.DMA((2, 2)),
            pltpu.SemaphoreType.DMA((2,)),
            pltpu.SemaphoreType.DMA((2,)),
            pltpu.SemaphoreType.DMA((8,)),
        ],
        out_shape=(
            jax.ShapeDtypeStruct((8, 16, 128, 256), bf16),
            jax.ShapeDtypeStruct((256, 128, 256), bf16),
        ),
        compiler_params=pltpu.CompilerParams(vmem_limit_bytes=60 << 20),
        name="products",
    )(codes, blocks, line, plane)


def combine_kernel(total_rows, diag, sketch, far, mirrors, image, total_tiles,
                   own, one, pre, next_to, sums, two, back, gram, tiles, from_line, part, from_plane,
                   send, recv, local, gsend, grecv):
    f32 = jnp.float32
    x, y, z, c = place()
    sems = (send, recv)
    a, b = x * (1 - c) + z * c, z * (1 - c) + x * c
    me = y * 2 + c

    def along(i, j):
        return x + (1 - c) * i + c * j, y, z + c * i + (1 - c) * j, c

    order = (1, 2, 3, 0)
    meet([along(n // 4, n % 4) for n in range(1, 16)] + [(x, y + i, z, c + d) for i, d in line_offsets()])

    def q(i, t):
        return ((a + 4 + i) % 4) * 4 + (b + t) % 4

    opposite, straight, onward, near_own, keep = {}, {}, {}, {}, []
    for n, t in enumerate(order):
        for side, (s, h) in enumerate(((1, 0), (-1, 1))):
            k = 6 * n + side
            opposite[t, side] = remote(half(mirrors.at[q(2, t)], h), pre.at[side, t], sems, k, *along(4 + s, 0))
            straight[t, side] = remote(
                half(mirrors.at[q(s, t)], 1 - h), half(one.at[side, t], 1 - h), sems, k + 2, *along(4 + s, 0))
            onward[t, side] = remote(next_to.at[side, t], half(one.at[side, t], h), sems, k + 4, *along(4 + s, 0))
            near_own[t, side] = pltpu.make_async_copy(
                half(mirrors.at[q(s, t)], h), next_to.at[side, t], local.at[5 + 2 * n + side])
    lines = []
    for n, (i, d) in enumerate(line_offsets()):
        to = ((y + i) % 4) * 2 + (c + d) % 2
        lines.append(remote(far.at[to], back.at[n + 1], sems, 24 + n, x, y + i, z, c + d))
    keep = [pltpu.make_async_copy(mirrors.at[q(0, t)], own.at[t], local.at[t]) for t in range(4)]
    keep.append(pltpu.make_async_copy(far.at[me], back.at[0], local.at[4]))
    second = [remote(sums.at[t - 1], two.at[t - 1], sems, 30 + t, *along(0, t)) for t in range(1, 4)]
    for group in (opposite, near_own):
        for t in order:
            for side in range(2):
                group[t, side].start()
    for t in order:
        for side in range(2):
            straight[t, side].start()
        if t == 1:
            for cp in lines:
                cp.start()
    for cp in keep:
        cp.start()

    def near(i, carry):
        at = pl.ds(pl.multiple_of(i * 128, 128), 128)
        image[at, :] = dot(diag[i], sketch[at, :], ((1,), (0,)), None)
        return carry

    lax.fori_loop(0, 16, near, 0)
    for t in order:
        for side in range(2):
            near_own[t, side].wait()
            opposite[t, side].wait_recv()

            def join(i, carry):
                at = pl.ds(pl.multiple_of(i * 128, 128), 128)
                total = next_to[side, t, at, :].astype(f32) + pre[side, t, at, :].astype(f32)
                next_to[side, t, at, :] = total.astype(jnp.bfloat16)
                return carry

            lax.fori_loop(0, 8, join, 0)
            onward[t, side].start()
    for t in order:
        keep[t].wait()
        for side in range(2):
            straight[t, side].wait_recv()
            onward[t, side].wait_recv()

        def add(i, carry):
            at = pl.ds(pl.multiple_of(i * 128, 128), 128)
            total = own[t, at, :].astype(f32) + one[0, t, at, :].astype(f32) + one[1, t, at, :].astype(f32)
            if t:
                sums[t - 1, at, :] = total.astype(jnp.bfloat16)
            else:
                image[at, :] += total
            return carry

        lax.fori_loop(0, 16, add, 0)
        if t:
            second[t - 1].start()
    keep[4].wait()
    for cp in lines:
        cp.wait_recv()

    def add_far(i, carry):
        at = pl.ds(pl.multiple_of(i * 128, 128), 128)
        total = image[at, :]
        for n in range(8):
            total += back[n, at, :].astype(f32)
        image[at, :] = total
        return carry

    lax.fori_loop(0, 16, add_far, 0)
    for cp in second:
        cp.wait_recv()

    def add_two(i, carry):
        at = pl.ds(pl.multiple_of(i * 128, 128), 128)
        image[at, :] += two[0, at, :].astype(f32) + two[1, at, :].astype(f32) + two[2, at, :].astype(f32)
        return carry

    lax.fori_loop(0, 16, add_two, 0)
    for cp in [*opposite.values(), *straight.values(), *onward.values()] + lines + second:
        cp.wait_send()
    gram[...] = jnp.zeros_like(gram)

    def partial(i, carry):
        h, l = split(image[pl.ds(pl.multiple_of(i * 512, 512), 512), :])
        down = ((0,), (0,))
        gram[...] += dot(h, h, down, None) + (dot(h, l, down, None) + dot(l, h, down, None))
        return carry

    lax.fori_loop(0, 4, partial, 0)
    for t, (i, j) in enumerate(TILES):
        tiles[t] = gram[8 * i : 8 * i + 8, 128 * j : 128 * j + 128] * (1.0 / total_rows)
    gsems = (gsend, grecv)
    offsets = line_offsets()
    out = []
    for n, (i, d) in enumerate(offsets):
        to = ((y + i) % 4) * 2 + (c + d) % 2
        out.append(remote(tiles.at[pl.ds(to * 6, 6)], from_line.at[me], gsems, n, x, y + i, z, c + d))
    for cp in out:
        cp.start()
    from_line[me] = tiles[pl.ds(me * 6, 6)]
    for cp in out:
        cp.wait()
    part[...] = jnp.sum(from_line[...], axis=0)
    own_q = a * 4 + b
    spread = []
    for n in range(1, 16):
        spread.append(remote(part, from_plane.at[own_q], gsems, 6 + n, *along(n // 4, n % 4)))
    for cp in spread:
        cp.start()
    from_plane[own_q] = part[...]
    for cp in spread:
        cp.wait()
    total_tiles[pl.ds(me * 6, 6)] = jnp.sum(from_plane[...], axis=0)
    everyone = []
    for n, (i, d) in enumerate(offsets):
        mine = total_tiles.at[pl.ds(me * 6, 6)]
        everyone.append(remote(mine, mine, gsems, 22 + n, x, y + i, z, c + d))
    for cp in everyone:
        cp.start()
    for cp in everyone:
        cp.wait()


def combine(total_rows, diag, sketch, far, mirrors):
    f32, bf16 = jnp.float32, jnp.bfloat16
    vmem = pl.BlockSpec(memory_space=pltpu.VMEM)
    anyspec = pl.BlockSpec(memory_space=pl.ANY)
    return pl.pallas_call(
        functools.partial(combine_kernel, total_rows),
        out_shape=(jax.ShapeDtypeStruct((2048, 256), f32), jax.ShapeDtypeStruct((48, 8, 128), f32)),
        in_specs=[vmem, vmem, anyspec, anyspec],
        out_specs=(vmem, vmem),
        scratch_shapes=[
            pltpu.VMEM((4, 2048, 256), bf16),
            pltpu.VMEM((2, 4, 2048, 256), bf16),
            pltpu.VMEM((2, 4, 1024, 256), bf16),
            pltpu.VMEM((2, 4, 1024, 256), bf16),
            pltpu.VMEM((3, 2048, 256), bf16),
            pltpu.VMEM((3, 2048, 256), bf16),
            pltpu.VMEM((8, 2048, 256), bf16),
            pltpu.VMEM((256, 256), f32),
            pltpu.VMEM((48, 8, 128), f32),
            pltpu.VMEM((8, 6, 8, 128), f32),
            pltpu.VMEM((6, 8, 128), f32),
            pltpu.VMEM((16, 6, 8, 128), f32),
            pltpu.SemaphoreType.DMA((34,)),
            pltpu.SemaphoreType.DMA((34,)),
            pltpu.SemaphoreType.DMA((13,)),
            pltpu.SemaphoreType.DMA((29,)),
            pltpu.SemaphoreType.DMA((29,)),
        ],
        compiler_params=pltpu.CompilerParams(has_side_effects=True, collective_id=1, vmem_limit_bytes=48 << 20),
        name="combine",
    )(diag, sketch, far, mirrors)


def split_owner(col):
    owner = col // 16
    r, y = owner // 4, owner % 4
    c = r % 2
    x, z = r // 8, (r // 2) % 4
    a, b = jnp.where(c == 0, x, z), jnp.where(c == 0, z, x)
    return y * 2 + c, (a * 4 + b) * 16 + col % 16


def on_device(diag_blocks, off_blocks, col_blocks, sketch):
    entries = 128
    flat = col_blocks.reshape(entries)
    order = jnp.arange(entries)
    before = order[None, :] < order[:, None]
    group, spot = split_owner(flat)
    rank = jnp.sum(((group[:, None] == group[None, :]) & before).astype(jnp.int32), axis=1)
    slot = group * 32 + rank
    chosen = (slot[None, :] == jnp.arange(256)[:, None]).astype(jnp.int32)
    unused = 1 - jnp.sum(chosen, axis=1)
    pick = jnp.sum(chosen * order[None, :], axis=1)
    code = jnp.sum(chosen * ((order // 8) * 512 + spot)[None, :], axis=1) + unused * (16 * 512 + 256)
    count = 32 - jnp.sum(unused.reshape(8, 32), axis=1, keepdims=True)
    codes = jnp.concatenate([code.reshape(8, 32), jnp.broadcast_to(count, (8, 96))], axis=1)
    meta = jnp.broadcast_to(codes[:, None, :], (8, 8, 128))
    blocks, line, plane, metas = gather_all(pick, off_blocks.reshape(entries, 128, 128), sketch, meta)
    far, mirrors = products(
        metas[:, 0, :], blocks, line.reshape(8, 16, 128, 256), plane.reshape(256, 128, 256)
    )
    image, tiles = combine(
        262144, diag_blocks, sketch, far.reshape(8, 2048, 256), mirrors.reshape(16, 2048, 256)
    )
    return solve(image, tiles)


def solution(mesh):
    placed = (
        P(("rows", "sub"), None, None),
        P(("rows", "sub"), None, None, None),
        P(("rows", "sub"), None),
        P(("rows", "sub"), None),
    )
    return jax.shard_map(
        on_device,
        mesh=mesh,
        in_specs=placed,
        out_specs=(P(("rows", "sub"), None), P()),
        check_vma=False,
    )
```

```python
import functools

import jax
import jax.numpy as jnp
from jax import lax
from jax.experimental import pallas as pl
from jax.experimental.pallas import tpu as pltpu
from jax.sharding import PartitionSpec as P

MESH = pl.DeviceIdType.MESH
HIGHEST = lax.Precision.HIGHEST
TILES = [(i, j) for i in range(32) for j in range(2) if i < 16 or j == 1]


def dot(a, b, dims, precision=HIGHEST):
    return lax.dot_general(a, b, (dims, ((), ())), precision=precision, preferred_element_type=jnp.float32)


def split(value):
    high = value.astype(jnp.bfloat16)
    return high, (value - high.astype(jnp.float32)).astype(jnp.bfloat16)


def eliminate(s, group):
    n, wide = s.shape
    sub = lax.broadcasted_iota(jnp.int32, (n, 1), 0)

    def widen(v):
        return jnp.concatenate([v] * (wide // 128), axis=1)

    for k in range(0, n, group):
        cols = [jnp.broadcast_to(s[:, k + i : k + i + 1], (n, 128)) for i in range(group)]
        rows = [s[k + i : k + i + 1, :] for i in range(group)]
        for j in range(group):
            scale = lax.rsqrt(cols[j][k + j : k + j + 1, :])
            cols[j] = cols[j] * scale
            rows[j] = rows[j] * widen(scale)
            for i in range(j + 1, group):
                share = cols[j][k + i : k + i + 1, :]
                cols[i] = cols[i] - cols[j] * share
                rows[i] = rows[i] - rows[j] * widen(share)
        for j in range(group):
            s = s - widen(jnp.where(sub >= k + group, cols[j], 0.0)) * rows[j]
        for j in range(group):
            s = jnp.where(sub == k + j, rows[j], s)
    return s


def solve_kernel(image, tiles, basis, upper, gram, work, linv):
    for t, (i, j) in enumerate(TILES):
        gram[8 * i : 8 * i + 8, 128 * j : 128 * j + 128] = tiles[t]
    eye = lax.broadcasted_iota(jnp.int32, (128, 128), 0), lax.broadcasted_iota(jnp.int32, (128, 128), 1)
    one = (eye[0] == eye[1]).astype(jnp.float32)
    work[...] = eliminate(jnp.concatenate([gram[:128, :128], one], axis=1), 8)
    i11 = work[:, 128:]
    r12 = dot(i11, gram[:128, 128:], ((1,), (0,)))
    upper[:128, :128] = jnp.where(eye[0] <= eye[1], work[:, :128], 0.0)
    upper[:128, 128:] = r12
    linv[:128, :128] = i11
    linv[:128, 128:] = jnp.zeros((128, 128), jnp.float32)
    cross = dot(r12, i11, ((0,), (0,)))
    rest = gram[128:, 128:] - dot(r12, r12, ((0,), (0,)))
    work[...] = eliminate(jnp.concatenate([rest, one], axis=1), 8)
    i22 = work[:, 128:]
    upper[128:, :128] = jnp.zeros((128, 128), jnp.float32)
    upper[128:, 128:] = jnp.where(eye[0] <= eye[1], work[:, :128], 0.0)
    linv[128:, :128] = -dot(i22, cross, ((1,), (0,)))
    linv[128:, 128:] = i22
    high, low = split(linv[...])
    across = ((1,), (1,))

    def rows_out(i, carry):
        at = pl.ds(pl.multiple_of(i * 256, 256), 256)
        h, l = split(image[at, :])
        basis[at, :] = dot(h, high, across, None) + (dot(h, low, across, None) + dot(l, high, across, None))
        return carry

    lax.fori_loop(0, 8, rows_out, 0)


def solve(image, tiles):
    f32 = jnp.float32
    vmem = pl.BlockSpec(memory_space=pltpu.VMEM)
    return pl.pallas_call(
        solve_kernel,
        out_shape=(jax.ShapeDtypeStruct((2048, 256), f32), jax.ShapeDtypeStruct((256, 256), f32)),
        in_specs=[vmem, vmem],
        out_specs=(vmem, vmem),
        scratch_shapes=[pltpu.VMEM((256, 256), f32), pltpu.VMEM((128, 256), f32), pltpu.VMEM((256, 256), f32)],
        compiler_params=pltpu.CompilerParams(vmem_limit_bytes=16 << 20),
        name="solve",
    )(image, tiles)


def place():
    r, y = lax.axis_index("rows"), lax.axis_index("sub")
    return r // 8, y, (r // 2) % 4, r % 2


def remote(src, dst, sems, k, x, y, z, c):
    send, recv = sems
    return pltpu.make_async_remote_copy(
        src_ref=src, dst_ref=dst, send_sem=send.at[k], recv_sem=recv.at[k],
        device_id=((x % 4) * 8 + (z % 4) * 2 + c % 2, y % 4), device_id_type=MESH)


def meet(partners):
    barrier = pltpu.get_barrier_semaphore()
    for x, y, z, c in partners:
        device = ((x % 4) * 8 + (z % 4) * 2 + c % 2, y % 4)
        pl.semaphore_signal(barrier, inc=1, device_id=device, device_id_type=MESH)
    pl.semaphore_wait(barrier, len(partners))


def line_offsets():
    return [(i, d) for i in range(4) for d in range(2) if (i, d) != (0, 0)]


def half(ref, h):
    return ref.at[pl.ds(1024 * h, 1024), :]


def gather_kernel(pick, off, sketch, meta, blocks, line, plane, metas, given, packed, held, send, recv, local):
    x, y, z, c = place()
    sems = (send, recv)
    a, b = x * (1 - c) + z * c, z * (1 - c) + x * c
    me = y * 2 + c
    own_q = a * 4 + b

    def q(i, j):
        return ((a + i) % 4) * 4 + (b + j) % 4

    def along(i, j):
        return x + 3 * 4 + (1 - c) * i + c * j, y, z + 3 * 4 + c * i + (1 - c) * j, c

    def line_at(i, d=0):
        return x, y + 4 + i, z, c + d

    def l(i):
        return ((y + 4 + i) % 4) * 2 + c

    meet([along(1, 0), along(-1, 0), along(0, 1), along(0, -1)] + [line_at(i, d) for i, d in line_offsets()])

    def slots(j):
        return packed.at[pl.ds(j * 32, 32)]

    take = pltpu.make_async_copy(off, given, local.at[0])
    fetch = pltpu.make_async_copy(sketch, held, local.at[1])
    keep = [
        pltpu.make_async_copy(held, plane.at[own_q], local.at[2]),
        pltpu.make_async_copy(held, line.at[me], local.at[3]),
        pltpu.make_async_copy(slots(me), blocks.at[me], local.at[4]),
        pltpu.make_async_copy(meta.at[me], metas.at[me], local.at[5]),
    ]

    def ring(source, slot, to, base):
        return {
            (s, h): remote(half(source, h), half(slot, h), sems, base + 2 * (s < 0) + h, *to(s))
            for s in (1, -1) for h in range(2)
        }

    def onward(slots, to, base):
        return {
            s: remote(half(slots[s], h), half(slots[s], h), sems, base + h, *to(s))
            for s, h in ((1, 0), (-1, 1))
        }

    to_a = lambda s: along(s, 0)
    first = ring(sketch, plane.at[own_q], to_a, 0)
    first_on = onward({1: plane.at[q(3, 0)], -1: plane.at[q(1, 0)]}, to_a, 4)
    same = ring(sketch, line.at[me], line_at, 6)
    same_on = onward({1: line.at[l(-1)], -1: line.at[l(1)]}, line_at, 10)
    mate = [remote(sketch, line.at[me], sems, 12, *line_at(0, 1))]
    mate += [remote(line.at[l(i)], line.at[l(i)], sems, 12 + n, *line_at(0, 1)) for n, i in ((1, -1), (2, 1), (3, 2))]
    to_b = lambda s: along(0, s)
    second, second_on = [], []
    for n, i in enumerate((0, 3, 1, 2)):
        source = sketch if i == 0 else plane.at[q(i, 0)]
        second.append(ring(source, plane.at[q(i, 0)], to_b, 16 + 6 * n))
        second_on.append(onward({1: plane.at[q(i, 3)], -1: plane.at[q(i, 1)]}, to_b, 20 + 6 * n))
    across, labels = [], []
    for n, (i, d) in enumerate(line_offsets()):
        to = ((y + i) % 4) * 2 + (c + d) % 2
        across.append(remote(slots(to), blocks.at[me], sems, 40 + n, *line_at(i, d)))
        labels.append(remote(meta.at[to], metas.at[me], sems, 47 + n, *line_at(i, d)))
    take.start()
    for cp in list(same.values()) + list(first.values()) + list(second[0].values()) + mate[:1] + labels:
        cp.start()
    fetch.start()
    take.wait()

    def place_block(t, carry):
        packed[t] = given[pick[t]]
        return carry

    lax.fori_loop(0, 256, place_block, 0, unroll=8)
    for cp in across:
        cp.start()
    fetch.wait()
    for cp in keep:
        cp.start()

    def pass_on(ring_, on_):
        ring_[1, 0].wait_recv()
        on_[1].start()
        ring_[-1, 1].wait_recv()
        on_[-1].start()

    pass_on(same, same_on)
    pass_on(first, first_on)
    first[1, 1].wait_recv()
    for cp in second[1].values():
        cp.start()
    first[-1, 0].wait_recv()
    for cp in second[2].values():
        cp.start()
    same[1, 1].wait_recv()
    mate[1].start()
    same[-1, 0].wait_recv()
    mate[2].start()
    pass_on(second[0], second_on[0])
    for s in (1, -1):
        first_on[s].wait_recv()
    for cp in second[3].values():
        cp.start()
    for n in (1, 2, 3):
        pass_on(second[n], second_on[n])
    for s in (1, -1):
        same_on[s].wait_recv()
    mate[3].start()
    for n in range(4):
        second[n][1, 1].wait_recv()
        second[n][-1, 0].wait_recv()
        for s in (1, -1):
            second_on[n][s].wait_recv()
    for cp in labels + across + mate + keep:
        cp.wait()
    for group in [first, first_on, same, same_on] + second + second_on:
        for cp in group.values():
            cp.wait_send()


def gather_all(pick, off, sketch, meta):
    anyspec = pl.BlockSpec(memory_space=pl.ANY)
    bf16 = jnp.bfloat16
    return pl.pallas_call(
        gather_kernel,
        out_shape=(
            jax.ShapeDtypeStruct((8, 32, 128, 128), bf16),
            jax.ShapeDtypeStruct((8, 2048, 256), bf16),
            jax.ShapeDtypeStruct((16, 2048, 256), bf16),
            jax.ShapeDtypeStruct((8, 8, 128), jnp.int32),
        ),
        in_specs=[pl.BlockSpec(memory_space=pltpu.SMEM)] + [anyspec] * 3,
        out_specs=(anyspec,) * 4,
        scratch_shapes=[
            pltpu.VMEM((128, 128, 128), bf16),
            pltpu.VMEM((256, 128, 128), bf16),
            pltpu.VMEM((2048, 256), bf16),
            pltpu.SemaphoreType.DMA((54,)),
            pltpu.SemaphoreType.DMA((54,)),
            pltpu.SemaphoreType.DMA((6,)),
        ],
        compiler_params=pltpu.CompilerParams(has_side_effects=True, collective_id=0, vmem_limit_bytes=60 << 20),
        name="gather",
    )(pick, off, sketch, meta)


def product_kernel(codes, blocks_all, line_all, plane, far, mirrors, acc, sums, blocks, line, wanted, fars_out, stage,
                   in_sem, want_sem, far_sem, sem):
    def want(s, t):
        column = jnp.minimum(codes[s, 0, t] % 512, 255)
        return pltpu.make_async_copy(plane.at[column], wanted.at[s % 2, t], want_sem.at[s % 2])

    def given_in(s):
        p = s % 2
        return (
            pltpu.make_async_copy(blocks_all.at[s], blocks.at[p], in_sem.at[p, 0]),
            pltpu.make_async_copy(line_all.at[s], line.at[p], in_sem.at[p, 1]),
        )

    def ask(s):
        for cp in given_in(s):
            cp.start()

        def one(t, carry):
            want(s, t).start()
            return carry

        lax.fori_loop(0, codes[s, 0, 32], one, 0)

    def far_copy(s):
        return pltpu.make_async_copy(fars_out.at[s % 2], far.at[s], far_sem.at[s % 2])

    ask(0)

    def clear(i, carry):
        sums[i] = jnp.zeros((128, 256), jnp.float32)
        return carry

    lax.fori_loop(0, 256, clear, 0, unroll=4)

    def source(s, carry):
        @pl.when(s < 7)
        def _():
            ask(s + 1)

        acc[...] = jnp.zeros_like(acc)

        def arrived(t, c):
            want(s, t).wait()
            return c

        for cp in given_in(s):
            cp.wait()
        lax.fori_loop(0, codes[s, 0, 32], arrived, 0)

        def four(g, c):
            code = [codes[s, 0, g * 4 + u] for u in range(4)]
            rows, cols = [v // 512 for v in code], [v % 512 for v in code]
            given = [blocks[s % 2, g * 4 + u] for u in range(4)]
            fars = [dot(given[u], wanted[s % 2, g * 4 + u], ((1,), (0,)), None) for u in range(4)]
            backs = [dot(given[u], line[s % 2, jnp.minimum(rows[u], 15)], ((0,), (0,)), None) for u in range(4)]
            for u in range(4):
                acc[rows[u]] += fars[u]
                sums[cols[u]] += backs[u].astype(jnp.bfloat16).astype(jnp.float32)
            return c

        lax.fori_loop(0, (codes[s, 0, 32] + 3) // 4, four, 0)

        @pl.when(s >= 2)
        def _():
            far_copy(s - 2).wait()

        def out_far(i, c):
            fars_out[s % 2, i] = acc[i].astype(jnp.bfloat16)
            return c

        lax.fori_loop(0, 16, out_far, 0, unroll=2)
        far_copy(s).start()
        return carry

    lax.fori_loop(0, 8, source, 0)

    def written(n):
        return pltpu.make_async_copy(stage.at[n % 8], mirrors.at[pl.ds(16 * n, 16)], sem.at[n % 8])

    for n in range(16):
        if n >= 8:
            written(n - 8).wait()

        def out(i, carry):
            stage[n % 8, i] = sums[16 * n + i].astype(jnp.bfloat16)
            return carry

        lax.fori_loop(0, 16, out, 0, unroll=2)
        written(n).start()
    for n in range(8, 16):
        written(n).wait()
    for n in (6, 7):
        far_copy(n).wait()


def products(codes, blocks, line, plane):
    bf16 = jnp.bfloat16
    anyspec = pl.BlockSpec(memory_space=pl.ANY)
    return pl.pallas_call(
        product_kernel,
        in_specs=[pl.BlockSpec(memory_space=pltpu.SMEM), anyspec, anyspec, anyspec],
        out_specs=(anyspec, anyspec),
        scratch_shapes=[
            pltpu.VMEM((17, 128, 256), jnp.float32),
            pltpu.VMEM((257, 128, 256), jnp.float32),
            pltpu.VMEM((2, 32, 128, 128), bf16),
            pltpu.VMEM((2, 16, 128, 256), bf16),
            pltpu.VMEM((2, 32, 128, 256), bf16),
            pltpu.VMEM((2, 16, 128, 256), bf16),
            pltpu.VMEM((8, 16, 128, 256), bf16),
            pltpu.SemaphoreType.DMA((2, 2)),
            pltpu.SemaphoreType.DMA((2,)),
            pltpu.SemaphoreType.DMA((2,)),
            pltpu.SemaphoreType.DMA((8,)),
        ],
        out_shape=(
            jax.ShapeDtypeStruct((8, 16, 128, 256), bf16),
            jax.ShapeDtypeStruct((256, 128, 256), bf16),
        ),
        compiler_params=pltpu.CompilerParams(vmem_limit_bytes=60 << 20),
        name="products",
    )(codes, blocks, line, plane)


def combine_kernel(total_rows, diag, sketch, far, mirrors, image, total_tiles,
                   own, one, pre, next_to, sums, two, back, gram, tiles, from_line, part, from_plane,
                   send, recv, local, gsend, grecv):
    f32 = jnp.float32
    x, y, z, c = place()
    sems = (send, recv)
    a, b = x * (1 - c) + z * c, z * (1 - c) + x * c
    me = y * 2 + c

    def along(i, j):
        return x + (1 - c) * i + c * j, y, z + c * i + (1 - c) * j, c

    order = (1, 2, 3, 0)
    meet([along(n // 4, n % 4) for n in range(1, 16)] + [(x, y + i, z, c + d) for i, d in line_offsets()])

    def q(i, t):
        return ((a + 4 + i) % 4) * 4 + (b + t) % 4

    opposite, straight, onward, near_own, keep = {}, {}, {}, {}, []
    for n, t in enumerate(order):
        for side, (s, h) in enumerate(((1, 0), (-1, 1))):
            k = 6 * n + side
            opposite[t, side] = remote(half(mirrors.at[q(2, t)], h), pre.at[side, t], sems, k, *along(4 + s, 0))
            straight[t, side] = remote(
                half(mirrors.at[q(s, t)], 1 - h), half(one.at[side, t], 1 - h), sems, k + 2, *along(4 + s, 0))
            onward[t, side] = remote(next_to.at[side, t], half(one.at[side, t], h), sems, k + 4, *along(4 + s, 0))
            near_own[t, side] = pltpu.make_async_copy(
                half(mirrors.at[q(s, t)], h), next_to.at[side, t], local.at[5 + 2 * n + side])
    lines = []
    for n, (i, d) in enumerate(line_offsets()):
        to = ((y + i) % 4) * 2 + (c + d) % 2
        lines.append(remote(far.at[to], back.at[n + 1], sems, 24 + n, x, y + i, z, c + d))
    keep = [pltpu.make_async_copy(mirrors.at[q(0, t)], own.at[t], local.at[t]) for t in range(4)]
    keep.append(pltpu.make_async_copy(far.at[me], back.at[0], local.at[4]))
    second = [remote(sums.at[t - 1], two.at[t - 1], sems, 30 + t, *along(0, t)) for t in range(1, 4)]
    for group in (opposite, near_own):
        for t in order:
            for side in range(2):
                group[t, side].start()
    for t in order:
        for side in range(2):
            straight[t, side].start()
        if t == 1:
            for cp in lines:
                cp.start()
    for cp in keep:
        cp.start()

    def near(i, carry):
        at = pl.ds(pl.multiple_of(i * 128, 128), 128)
        image[at, :] = dot(diag[i], sketch[at, :], ((1,), (0,)), None)
        return carry

    lax.fori_loop(0, 16, near, 0)
    for t in order:
        for side in range(2):
            near_own[t, side].wait()
            opposite[t, side].wait_recv()

            def join(i, carry):
                at = pl.ds(pl.multiple_of(i * 128, 128), 128)
                total = next_to[side, t, at, :].astype(f32) + pre[side, t, at, :].astype(f32)
                next_to[side, t, at, :] = total.astype(jnp.bfloat16)
                return carry

            lax.fori_loop(0, 8, join, 0)
            onward[t, side].start()
    for t in order:
        keep[t].wait()
        for side in range(2):
            straight[t, side].wait_recv()
            onward[t, side].wait_recv()

        def add(i, carry):
            at = pl.ds(pl.multiple_of(i * 128, 128), 128)
            total = own[t, at, :].astype(f32) + one[0, t, at, :].astype(f32) + one[1, t, at, :].astype(f32)
            if t:
                sums[t - 1, at, :] = total.astype(jnp.bfloat16)
            else:
                image[at, :] += total
            return carry

        lax.fori_loop(0, 16, add, 0)
        if t:
            second[t - 1].start()
    keep[4].wait()
    for cp in lines:
        cp.wait_recv()

    def add_far(i, carry):
        at = pl.ds(pl.multiple_of(i * 128, 128), 128)
        total = image[at, :]
        for n in range(8):
            total += back[n, at, :].astype(f32)
        image[at, :] = total
        return carry

    lax.fori_loop(0, 16, add_far, 0)
    for cp in second:
        cp.wait_recv()

    def add_two(i, carry):
        at = pl.ds(pl.multiple_of(i * 128, 128), 128)
        image[at, :] += two[0, at, :].astype(f32) + two[1, at, :].astype(f32) + two[2, at, :].astype(f32)
        return carry

    lax.fori_loop(0, 16, add_two, 0)
    for cp in [*opposite.values(), *straight.values(), *onward.values()] + lines + second:
        cp.wait_send()
    gram[...] = jnp.zeros_like(gram)

    def partial(i, carry):
        h, l = split(image[pl.ds(pl.multiple_of(i * 512, 512), 512), :])
        down = ((0,), (0,))
        gram[...] += dot(h, h, down, None) + (dot(h, l, down, None) + dot(l, h, down, None))
        return carry

    lax.fori_loop(0, 4, partial, 0)
    for t, (i, j) in enumerate(TILES):
        tiles[t] = gram[8 * i : 8 * i + 8, 128 * j : 128 * j + 128] * (1.0 / total_rows)
    gsems = (gsend, grecv)
    here = x * 4 + z

    def spot(i, j):
        return ((x + i) % 4) * 4 + (z + j) % 4

    shifts = [(n // 4, n % 4) for n in range(1, 16)]
    shifts.sort(key=lambda v: -(min(v[0], 4 - v[0]) + min(v[1], 4 - v[1])))
    scatter = [
        remote(tiles.at[pl.ds(spot(i, j) * 3, 3)], from_plane.at[here], gsems, n, x + i, y, z + j, c)
        for n, (i, j) in enumerate(shifts)
    ]
    for cp in scatter:
        cp.start()
    from_plane[here] = tiles[pl.ds(here * 3, 3)]
    for cp in scatter:
        cp.wait_recv()
    part[...] = jnp.sum(from_plane[...], axis=0)
    trade = [
        remote(part, from_line.at[me], gsems, 15 + n, x, y + i, z, c + d)
        for n, (i, d) in enumerate(line_offsets())
    ]
    for cp in trade:
        cp.start()
    from_line[me] = part[...]
    for cp in trade:
        cp.wait_recv()
    mine = total_tiles.at[pl.ds(here * 3, 3)]
    mine[...] = jnp.sum(from_line[...], axis=0)
    everyone = [remote(mine, mine, gsems, 22 + n, x + i, y, z + j, c) for n, (i, j) in enumerate(shifts)]
    for cp in everyone:
        cp.start()
    for cp in everyone:
        cp.wait_recv()
    for cp in scatter + trade + everyone:
        cp.wait_send()


def combine(total_rows, diag, sketch, far, mirrors):
    f32, bf16 = jnp.float32, jnp.bfloat16
    vmem = pl.BlockSpec(memory_space=pltpu.VMEM)
    anyspec = pl.BlockSpec(memory_space=pl.ANY)
    return pl.pallas_call(
        functools.partial(combine_kernel, total_rows),
        out_shape=(jax.ShapeDtypeStruct((2048, 256), f32), jax.ShapeDtypeStruct((48, 8, 128), f32)),
        in_specs=[vmem, vmem, anyspec, anyspec],
        out_specs=(vmem, vmem),
        scratch_shapes=[
            pltpu.VMEM((4, 2048, 256), bf16),
            pltpu.VMEM((2, 4, 2048, 256), bf16),
            pltpu.VMEM((2, 4, 1024, 256), bf16),
            pltpu.VMEM((2, 4, 1024, 256), bf16),
            pltpu.VMEM((3, 2048, 256), bf16),
            pltpu.VMEM((3, 2048, 256), bf16),
            pltpu.VMEM((8, 2048, 256), bf16),
            pltpu.VMEM((256, 256), f32),
            pltpu.VMEM((48, 8, 128), f32),
            pltpu.VMEM((8, 3, 8, 128), f32),
            pltpu.VMEM((3, 8, 128), f32),
            pltpu.VMEM((16, 3, 8, 128), f32),
            pltpu.SemaphoreType.DMA((34,)),
            pltpu.SemaphoreType.DMA((34,)),
            pltpu.SemaphoreType.DMA((13,)),
            pltpu.SemaphoreType.DMA((37,)),
            pltpu.SemaphoreType.DMA((37,)),
        ],
        compiler_params=pltpu.CompilerParams(has_side_effects=True, collective_id=1, vmem_limit_bytes=48 << 20),
        name="combine",
    )(diag, sketch, far, mirrors)


def split_owner(col):
    owner = col // 16
    r, y = owner // 4, owner % 4
    c = r % 2
    x, z = r // 8, (r // 2) % 4
    a, b = jnp.where(c == 0, x, z), jnp.where(c == 0, z, x)
    return y * 2 + c, (a * 4 + b) * 16 + col % 16


def on_device(diag_blocks, off_blocks, col_blocks, sketch):
    entries = 128
    flat = col_blocks.reshape(entries)
    order = jnp.arange(entries)
    before = order[None, :] < order[:, None]
    group, spot = split_owner(flat)
    rank = jnp.sum(((group[:, None] == group[None, :]) & before).astype(jnp.int32), axis=1)
    slot = group * 32 + rank
    chosen = (slot[None, :] == jnp.arange(256)[:, None]).astype(jnp.int32)
    unused = 1 - jnp.sum(chosen, axis=1)
    pick = jnp.sum(chosen * order[None, :], axis=1)
    code = jnp.sum(chosen * ((order // 8) * 512 + spot)[None, :], axis=1) + unused * (16 * 512 + 256)
    count = 32 - jnp.sum(unused.reshape(8, 32), axis=1, keepdims=True)
    codes = jnp.concatenate([code.reshape(8, 32), jnp.broadcast_to(count, (8, 96))], axis=1)
    meta = jnp.broadcast_to(codes[:, None, :], (8, 8, 128))
    blocks, line, plane, metas = gather_all(pick, off_blocks.reshape(entries, 128, 128), sketch, meta)
    far, mirrors = products(
        metas, blocks, line.reshape(8, 16, 128, 256), plane.reshape(256, 128, 256)
    )
    image, tiles = combine(
        262144, diag_blocks, sketch, far.reshape(8, 2048, 256), mirrors.reshape(16, 2048, 256)
    )
    return solve(image, tiles)


def solution(mesh):
    placed = (
        P(("rows", "sub"), None, None),
        P(("rows", "sub"), None, None, None),
        P(("rows", "sub"), None),
        P(("rows", "sub"), None),
    )
    return jax.shard_map(
        on_device,
        mesh=mesh,
        in_specs=placed,
        out_specs=(P(("rows", "sub"), None), P()),
        check_vma=False,
    )
```

```python
import functools

import jax
import jax.numpy as jnp
from jax import lax
from jax.experimental import pallas as pl
from jax.experimental.pallas import tpu as pltpu
from jax.sharding import PartitionSpec as P

MESH = pl.DeviceIdType.MESH
HIGHEST = lax.Precision.HIGHEST
TILES = [(i, j) for i in range(32) for j in range(2) if i < 16 or j == 1]


def dot(a, b, dims, precision=HIGHEST):
    return lax.dot_general(a, b, (dims, ((), ())), precision=precision, preferred_element_type=jnp.float32)


def split(value):
    high = value.astype(jnp.bfloat16)
    return high, (value - high.astype(jnp.float32)).astype(jnp.bfloat16)


def eliminate(s):
    n, wide = s.shape
    strips = [s[8 * i : 8 * i + 8, :] for i in range(n // 8)]
    sub = lax.broadcasted_iota(jnp.int32, (8, 1), 0)

    def widen(v):
        return jnp.concatenate([v] * (wide // 128), axis=1)

    for p in range(n // 8):
        k = 8 * p
        cols = [
            [jnp.broadcast_to(strip[:, k + j : k + j + 1], (8, 128)) for strip in strips[p:]] for j in range(8)
        ]
        rows = [strips[p][j : j + 1, :] for j in range(8)]
        for j in range(8):
            scale = lax.rsqrt(cols[j][0][j : j + 1, :])
            cols[j] = [v * scale for v in cols[j]]
            rows[j] = rows[j] * widen(scale)
            for i in range(j + 1, 8):
                share = cols[j][0][i : i + 1, :]
                cols[i] = [u - v * share for u, v in zip(cols[i], cols[j])]
                rows[i] = rows[i] - rows[j] * widen(share)
        for j in range(8):
            for m in range(p + 1, n // 8):
                strips[m] = strips[m] - widen(cols[j][m - p]) * rows[j]
        pivot = strips[p]
        for j in range(8):
            pivot = jnp.where(sub == j, rows[j], pivot)
        strips[p] = pivot
    return strips


def solve_kernel(image, tiles, basis, upper, gram, work, linv):
    for t, (i, j) in enumerate(TILES):
        gram[8 * i : 8 * i + 8, 128 * j : 128 * j + 128] = tiles[t]
    eye = lax.broadcasted_iota(jnp.int32, (128, 128), 0), lax.broadcasted_iota(jnp.int32, (128, 128), 1)
    one = (eye[0] == eye[1]).astype(jnp.float32)
    for i, strip in enumerate(eliminate(jnp.concatenate([gram[:128, :128], one], axis=1))):
        work[8 * i : 8 * i + 8, :] = strip
    i11 = work[:, 128:]
    r12 = dot(i11, gram[:128, 128:], ((1,), (0,)))
    upper[:128, :128] = jnp.where(eye[0] <= eye[1], work[:, :128], 0.0)
    upper[:128, 128:] = r12
    linv[:128, :128] = i11
    linv[:128, 128:] = jnp.zeros((128, 128), jnp.float32)
    cross = dot(r12, i11, ((0,), (0,)))
    rest = gram[128:, 128:] - dot(r12, r12, ((0,), (0,)))
    for i, strip in enumerate(eliminate(jnp.concatenate([rest, one], axis=1))):
        work[8 * i : 8 * i + 8, :] = strip
    i22 = work[:, 128:]
    upper[128:, :128] = jnp.zeros((128, 128), jnp.float32)
    upper[128:, 128:] = jnp.where(eye[0] <= eye[1], work[:, :128], 0.0)
    linv[128:, :128] = -dot(i22, cross, ((1,), (0,)))
    linv[128:, 128:] = i22
    high, low = split(linv[...])
    across = ((1,), (1,))

    def rows_out(i, carry):
        at = pl.ds(pl.multiple_of(i * 256, 256), 256)
        h, l = split(image[at, :])
        basis[at, :] = dot(h, high, across, None) + (dot(h, low, across, None) + dot(l, high, across, None))
        return carry

    lax.fori_loop(0, 8, rows_out, 0)


def solve(image, tiles):
    f32 = jnp.float32
    vmem = pl.BlockSpec(memory_space=pltpu.VMEM)
    return pl.pallas_call(
        solve_kernel,
        out_shape=(jax.ShapeDtypeStruct((2048, 256), f32), jax.ShapeDtypeStruct((256, 256), f32)),
        in_specs=[vmem, vmem],
        out_specs=(vmem, vmem),
        scratch_shapes=[pltpu.VMEM((256, 256), f32), pltpu.VMEM((128, 256), f32), pltpu.VMEM((256, 256), f32)],
        compiler_params=pltpu.CompilerParams(vmem_limit_bytes=16 << 20),
        name="solve",
    )(image, tiles)


def place():
    r, y = lax.axis_index("rows"), lax.axis_index("sub")
    return r // 8, y, (r // 2) % 4, r % 2


def place_in_line():
    return lax.axis_index("sub") * 2 + lax.axis_index("rows") % 2


def remote(src, dst, sems, k, x, y, z, c):
    send, recv = sems
    return pltpu.make_async_remote_copy(
        src_ref=src, dst_ref=dst, send_sem=send.at[k], recv_sem=recv.at[k],
        device_id=((x % 4) * 8 + (z % 4) * 2 + c % 2, y % 4), device_id_type=MESH)


def meet(partners):
    barrier = pltpu.get_barrier_semaphore()
    for x, y, z, c in partners:
        device = ((x % 4) * 8 + (z % 4) * 2 + c % 2, y % 4)
        pl.semaphore_signal(barrier, inc=1, device_id=device, device_id_type=MESH)
    pl.semaphore_wait(barrier, len(partners))


def line_offsets():
    return [(i, d) for i in range(4) for d in range(2) if (i, d) != (0, 0)]


def half(ref, h):
    return ref.at[pl.ds(1024 * h, 1024), :]


def gather_kernel(pick, off, sketch, meta, blocks, line, plane, metas, given, packed, held, send, recv, local):
    x, y, z, c = place()
    sems = (send, recv)
    a, b = x * (1 - c) + z * c, z * (1 - c) + x * c
    me = y * 2 + c
    own_q = a * 4 + b

    def q(i, j):
        return ((a + i) % 4) * 4 + (b + j) % 4

    def along(i, j):
        return x + 3 * 4 + (1 - c) * i + c * j, y, z + 3 * 4 + c * i + (1 - c) * j, c

    def line_at(i, d=0):
        return x, y + 4 + i, z, c + d

    def l(i):
        return ((y + 4 + i) % 4) * 2 + c

    meet([along(1, 0), along(-1, 0), along(0, 1), along(0, -1)] + [line_at(i, d) for i, d in line_offsets()])

    def slots(j):
        return packed.at[pl.ds(j * 32, 32)]

    take = pltpu.make_async_copy(off, given, local.at[0])
    fetch = pltpu.make_async_copy(sketch, held, local.at[1])
    keep = [
        pltpu.make_async_copy(held, plane.at[own_q], local.at[2]),
        pltpu.make_async_copy(held, line.at[me], local.at[3]),
        pltpu.make_async_copy(slots(me), blocks.at[me], local.at[4]),
        pltpu.make_async_copy(meta, metas.at[me], local.at[5]),
    ]

    def ring(source, slot, to, base):
        return {
            (s, h): remote(half(source, h), half(slot, h), sems, base + 2 * (s < 0) + h, *to(s))
            for s in (1, -1) for h in range(2)
        }

    def onward(slots, to, base):
        return {
            s: remote(half(slots[s], h), half(slots[s], h), sems, base + h, *to(s))
            for s, h in ((1, 0), (-1, 1))
        }

    to_a = lambda s: along(s, 0)
    first = ring(sketch, plane.at[own_q], to_a, 0)
    first_on = onward({1: plane.at[q(3, 0)], -1: plane.at[q(1, 0)]}, to_a, 4)
    same = ring(sketch, line.at[me], line_at, 6)
    same_on = onward({1: line.at[l(-1)], -1: line.at[l(1)]}, line_at, 10)
    mate = [remote(sketch, line.at[me], sems, 12, *line_at(0, 1))]
    mate += [remote(line.at[l(i)], line.at[l(i)], sems, 12 + n, *line_at(0, 1)) for n, i in ((1, -1), (2, 1), (3, 2))]
    to_b = lambda s: along(0, s)
    second, second_on = [], []
    for n, i in enumerate((0, 3, 1, 2)):
        source = sketch if i == 0 else plane.at[q(i, 0)]
        second.append(ring(source, plane.at[q(i, 0)], to_b, 16 + 6 * n))
        second_on.append(onward({1: plane.at[q(i, 3)], -1: plane.at[q(i, 1)]}, to_b, 20 + 6 * n))
    across, labels = [], []
    for n, (i, d) in enumerate(line_offsets()):
        to = ((y + i) % 4) * 2 + (c + d) % 2
        across.append(remote(slots(to), blocks.at[me], sems, 40 + n, *line_at(i, d)))
        labels.append(remote(meta, metas.at[me], sems, 47 + n, *line_at(i, d)))
    take.start()
    for cp in list(same.values()) + list(first.values()) + list(second[0].values()) + mate[:1] + labels:
        cp.start()
    fetch.start()
    take.wait()

    def place_block(t, carry):
        packed[t] = given[pick[t]]
        return carry

    lax.fori_loop(0, 256, place_block, 0, unroll=8)
    for cp in across:
        cp.start()
    fetch.wait()
    for cp in keep:
        cp.start()

    def pass_on(ring_, on_):
        ring_[1, 0].wait_recv()
        on_[1].start()
        ring_[-1, 1].wait_recv()
        on_[-1].start()

    pass_on(same, same_on)
    pass_on(first, first_on)
    first[1, 1].wait_recv()
    for cp in second[1].values():
        cp.start()
    first[-1, 0].wait_recv()
    for cp in second[2].values():
        cp.start()
    same[1, 1].wait_recv()
    mate[1].start()
    same[-1, 0].wait_recv()
    mate[2].start()
    pass_on(second[0], second_on[0])
    for s in (1, -1):
        first_on[s].wait_recv()
    for cp in second[3].values():
        cp.start()
    for n in (1, 2, 3):
        pass_on(second[n], second_on[n])
    for s in (1, -1):
        same_on[s].wait_recv()
    mate[3].start()
    for n in range(4):
        second[n][1, 1].wait_recv()
        second[n][-1, 0].wait_recv()
        for s in (1, -1):
            second_on[n][s].wait_recv()
    for cp in labels + across + mate + keep:
        cp.wait()
    for group in [first, first_on, same, same_on] + second + second_on:
        for cp in group.values():
            cp.wait_send()


def gather_all(pick, off, sketch, meta):
    anyspec = pl.BlockSpec(memory_space=pl.ANY)
    bf16 = jnp.bfloat16
    return pl.pallas_call(
        gather_kernel,
        out_shape=(
            jax.ShapeDtypeStruct((8, 32, 128, 128), bf16),
            jax.ShapeDtypeStruct((8, 2048, 256), bf16),
            jax.ShapeDtypeStruct((16, 2048, 256), bf16),
            jax.ShapeDtypeStruct((8, 8, 128), jnp.int32),
        ),
        in_specs=[pl.BlockSpec(memory_space=pltpu.SMEM)] + [anyspec] * 3,
        out_specs=(anyspec,) * 4,
        scratch_shapes=[
            pltpu.VMEM((128, 128, 128), bf16),
            pltpu.VMEM((256, 128, 128), bf16),
            pltpu.VMEM((2048, 256), bf16),
            pltpu.SemaphoreType.DMA((54,)),
            pltpu.SemaphoreType.DMA((54,)),
            pltpu.SemaphoreType.DMA((6,)),
        ],
        compiler_params=pltpu.CompilerParams(has_side_effects=True, collective_id=0, vmem_limit_bytes=60 << 20),
        name="gather",
    )(pick, off, sketch, meta)


def product_kernel(codes, blocks_all, line_all, plane, far, mirrors, acc, sums, blocks, line, wanted, fars_out, stage,
                   in_sem, want_sem, far_sem, sem):
    def want(s, t):
        column = jnp.minimum(codes[s, mine, t] % 512, 255)
        return pltpu.make_async_copy(plane.at[column], wanted.at[s % 2, t], want_sem.at[s % 2])

    mine = place_in_line()

    def given_in(s):
        p = s % 2
        return (
            pltpu.make_async_copy(blocks_all.at[s], blocks.at[p], in_sem.at[p, 0]),
            pltpu.make_async_copy(line_all.at[s], line.at[p], in_sem.at[p, 1]),
        )

    def ask(s):
        for cp in given_in(s):
            cp.start()

        def one(t, carry):
            want(s, t).start()
            return carry

        lax.fori_loop(0, codes[s, mine, 32], one, 0)

    def far_copy(s):
        return pltpu.make_async_copy(fars_out.at[s % 2], far.at[s], far_sem.at[s % 2])

    ask(0)

    def clear(i, carry):
        sums[i] = jnp.zeros((128, 256), jnp.float32)
        return carry

    lax.fori_loop(0, 256, clear, 0, unroll=4)

    def source(s, carry):
        @pl.when(s < 7)
        def _():
            ask(s + 1)

        acc[...] = jnp.zeros_like(acc)

        def arrived(t, c):
            want(s, t).wait()
            return c

        for cp in given_in(s):
            cp.wait()
        lax.fori_loop(0, codes[s, mine, 32], arrived, 0)

        def eight(g, c):
            code = [codes[s, mine, g * 8 + u] for u in range(8)]
            rows, cols = [v // 512 for v in code], [v % 512 for v in code]
            given = [blocks[s % 2, g * 8 + u] for u in range(8)]
            fars = [dot(given[u], wanted[s % 2, g * 8 + u], ((1,), (0,)), None) for u in range(8)]
            backs = [dot(given[u], line[s % 2, jnp.minimum(rows[u], 15)], ((0,), (0,)), None) for u in range(8)]
            for u in range(8):
                acc[rows[u]] += fars[u]
                sums[cols[u]] += backs[u].astype(jnp.bfloat16).astype(jnp.float32)
            return c

        lax.fori_loop(0, (codes[s, mine, 32] + 7) // 8, eight, 0)

        @pl.when(s >= 2)
        def _():
            far_copy(s - 2).wait()

        def out_far(i, c):
            fars_out[s % 2, i] = acc[i].astype(jnp.bfloat16)
            return c

        lax.fori_loop(0, 16, out_far, 0, unroll=2)
        far_copy(s).start()
        return carry

    lax.fori_loop(0, 8, source, 0)

    def written(n):
        return pltpu.make_async_copy(stage.at[n % 8], mirrors.at[pl.ds(16 * n, 16)], sem.at[n % 8])

    for n in range(16):
        if n >= 8:
            written(n - 8).wait()

        def out(i, carry):
            stage[n % 8, i] = sums[16 * n + i].astype(jnp.bfloat16)
            return carry

        lax.fori_loop(0, 16, out, 0, unroll=2)
        written(n).start()
    for n in range(8, 16):
        written(n).wait()
    for n in (6, 7):
        far_copy(n).wait()


def products(codes, blocks, line, plane):
    bf16 = jnp.bfloat16
    anyspec = pl.BlockSpec(memory_space=pl.ANY)
    return pl.pallas_call(
        product_kernel,
        in_specs=[pl.BlockSpec(memory_space=pltpu.SMEM), anyspec, anyspec, anyspec],
        out_specs=(anyspec, anyspec),
        scratch_shapes=[
            pltpu.VMEM((17, 128, 256), jnp.float32),
            pltpu.VMEM((257, 128, 256), jnp.float32),
            pltpu.VMEM((2, 32, 128, 128), bf16),
            pltpu.VMEM((2, 16, 128, 256), bf16),
            pltpu.VMEM((2, 32, 128, 256), bf16),
            pltpu.VMEM((2, 16, 128, 256), bf16),
            pltpu.VMEM((8, 16, 128, 256), bf16),
            pltpu.SemaphoreType.DMA((2, 2)),
            pltpu.SemaphoreType.DMA((2,)),
            pltpu.SemaphoreType.DMA((2,)),
            pltpu.SemaphoreType.DMA((8,)),
        ],
        out_shape=(
            jax.ShapeDtypeStruct((8, 16, 128, 256), bf16),
            jax.ShapeDtypeStruct((256, 128, 256), bf16),
        ),
        compiler_params=pltpu.CompilerParams(vmem_limit_bytes=60 << 20),
        name="products",
    )(codes, blocks, line, plane)


def combine_kernel(total_rows, diag, sketch, far, mirrors, image, total_tiles,
                   own, one, pre, next_to, sums, two, back, gram, tiles, from_line, part, from_plane,
                   send, recv, local, gsend, grecv):
    f32 = jnp.float32
    x, y, z, c = place()
    sems = (send, recv)
    a, b = x * (1 - c) + z * c, z * (1 - c) + x * c
    me = y * 2 + c

    def along(i, j):
        return x + (1 - c) * i + c * j, y, z + c * i + (1 - c) * j, c

    order = (1, 2, 3, 0)
    meet([along(n // 4, n % 4) for n in range(1, 16)] + [(x, y + i, z, c + d) for i, d in line_offsets()])

    def q(i, t):
        return ((a + 4 + i) % 4) * 4 + (b + t) % 4

    opposite, straight, onward, near_own, keep = {}, {}, {}, {}, []
    for n, t in enumerate(order):
        for side, (s, h) in enumerate(((1, 0), (-1, 1))):
            k = 6 * n + side
            opposite[t, side] = remote(half(mirrors.at[q(2, t)], h), pre.at[side, t], sems, k, *along(4 + s, 0))
            straight[t, side] = remote(
                half(mirrors.at[q(s, t)], 1 - h), half(one.at[side, t], 1 - h), sems, k + 2, *along(4 + s, 0))
            onward[t, side] = remote(next_to.at[side, t], half(one.at[side, t], h), sems, k + 4, *along(4 + s, 0))
            near_own[t, side] = pltpu.make_async_copy(
                half(mirrors.at[q(s, t)], h), next_to.at[side, t], local.at[5 + 2 * n + side])
    lines = []
    for n, (i, d) in enumerate(line_offsets()):
        to = ((y + i) % 4) * 2 + (c + d) % 2
        lines.append(remote(far.at[to], back.at[n + 1], sems, 24 + n, x, y + i, z, c + d))
    keep = [pltpu.make_async_copy(mirrors.at[q(0, t)], own.at[t], local.at[t]) for t in range(4)]
    keep.append(pltpu.make_async_copy(far.at[me], back.at[0], local.at[4]))
    second = [remote(sums.at[t - 1], two.at[t - 1], sems, 30 + t, *along(0, t)) for t in range(1, 4)]
    for group in (opposite, near_own):
        for t in order:
            for side in range(2):
                group[t, side].start()
    for t in order:
        for side in range(2):
            straight[t, side].start()
        if t == 1:
            for cp in lines:
                cp.start()
    for cp in keep:
        cp.start()

    def near(i, carry):
        at = pl.ds(pl.multiple_of(i * 128, 128), 128)
        image[at, :] = dot(diag[i], sketch[at, :], ((1,), (0,)), None)
        return carry

    lax.fori_loop(0, 16, near, 0)
    for t in order:
        for side in range(2):
            near_own[t, side].wait()
            opposite[t, side].wait_recv()

            def join(i, carry):
                at = pl.ds(pl.multiple_of(i * 128, 128), 128)
                total = next_to[side, t, at, :].astype(f32) + pre[side, t, at, :].astype(f32)
                next_to[side, t, at, :] = total.astype(jnp.bfloat16)
                return carry

            lax.fori_loop(0, 8, join, 0)
            onward[t, side].start()
    for t in order:
        keep[t].wait()
        for side in range(2):
            straight[t, side].wait_recv()
            onward[t, side].wait_recv()

        def add(i, carry):
            at = pl.ds(pl.multiple_of(i * 128, 128), 128)
            total = own[t, at, :].astype(f32) + one[0, t, at, :].astype(f32) + one[1, t, at, :].astype(f32)
            if t:
                sums[t - 1, at, :] = total.astype(jnp.bfloat16)
            else:
                image[at, :] += total
            return carry

        lax.fori_loop(0, 16, add, 0)
        if t:
            second[t - 1].start()
    keep[4].wait()
    for cp in lines:
        cp.wait_recv()

    def add_far(i, carry):
        at = pl.ds(pl.multiple_of(i * 128, 128), 128)
        total = image[at, :]
        for n in range(8):
            total += back[n, at, :].astype(f32)
        image[at, :] = total
        return carry

    lax.fori_loop(0, 16, add_far, 0)
    for cp in second:
        cp.wait_recv()

    def add_two(i, carry):
        at = pl.ds(pl.multiple_of(i * 128, 128), 128)
        image[at, :] += two[0, at, :].astype(f32) + two[1, at, :].astype(f32) + two[2, at, :].astype(f32)
        return carry

    lax.fori_loop(0, 16, add_two, 0)
    for cp in [*opposite.values(), *straight.values(), *onward.values()] + lines + second:
        cp.wait_send()
    gram[...] = jnp.zeros_like(gram)

    def partial(i, carry):
        h, l = split(image[pl.ds(pl.multiple_of(i * 512, 512), 512), :])
        down = ((0,), (0,))
        gram[...] += dot(h, h, down, None) + (dot(h, l, down, None) + dot(l, h, down, None))
        return carry

    lax.fori_loop(0, 4, partial, 0)
    for t, (i, j) in enumerate(TILES):
        tiles[t] = gram[8 * i : 8 * i + 8, 128 * j : 128 * j + 128] * (1.0 / total_rows)
    gsems = (gsend, grecv)
    here = x * 4 + z

    def spot(i, j):
        return ((x + i) % 4) * 4 + (z + j) % 4

    shifts = [(n // 4, n % 4) for n in range(1, 16)]
    shifts.sort(key=lambda v: -(min(v[0], 4 - v[0]) + min(v[1], 4 - v[1])))
    scatter = [
        remote(tiles.at[pl.ds(spot(i, j) * 3, 3)], from_plane.at[here], gsems, n, x + i, y, z + j, c)
        for n, (i, j) in enumerate(shifts)
    ]
    for cp in scatter:
        cp.start()
    from_plane[here] = tiles[pl.ds(here * 3, 3)]
    for cp in scatter:
        cp.wait_recv()
    part[...] = jnp.sum(from_plane[...], axis=0)
    trade = [
        remote(part, from_line.at[me], gsems, 15 + n, x, y + i, z, c + d)
        for n, (i, d) in enumerate(line_offsets())
    ]
    for cp in trade:
        cp.start()
    from_line[me] = part[...]
    for cp in trade:
        cp.wait_recv()
    mine = total_tiles.at[pl.ds(here * 3, 3)]
    mine[...] = jnp.sum(from_line[...], axis=0)
    everyone = [remote(mine, mine, gsems, 22 + n, x + i, y, z + j, c) for n, (i, j) in enumerate(shifts)]
    for cp in everyone:
        cp.start()
    for cp in everyone:
        cp.wait_recv()
    for cp in scatter + trade + everyone:
        cp.wait_send()


def combine(total_rows, diag, sketch, far, mirrors):
    f32, bf16 = jnp.float32, jnp.bfloat16
    vmem = pl.BlockSpec(memory_space=pltpu.VMEM)
    anyspec = pl.BlockSpec(memory_space=pl.ANY)
    return pl.pallas_call(
        functools.partial(combine_kernel, total_rows),
        out_shape=(jax.ShapeDtypeStruct((2048, 256), f32), jax.ShapeDtypeStruct((48, 8, 128), f32)),
        in_specs=[vmem, vmem, anyspec, anyspec],
        out_specs=(vmem, vmem),
        scratch_shapes=[
            pltpu.VMEM((4, 2048, 256), bf16),
            pltpu.VMEM((2, 4, 2048, 256), bf16),
            pltpu.VMEM((2, 4, 1024, 256), bf16),
            pltpu.VMEM((2, 4, 1024, 256), bf16),
            pltpu.VMEM((3, 2048, 256), bf16),
            pltpu.VMEM((3, 2048, 256), bf16),
            pltpu.VMEM((8, 2048, 256), bf16),
            pltpu.VMEM((256, 256), f32),
            pltpu.VMEM((48, 8, 128), f32),
            pltpu.VMEM((8, 3, 8, 128), f32),
            pltpu.VMEM((3, 8, 128), f32),
            pltpu.VMEM((16, 3, 8, 128), f32),
            pltpu.SemaphoreType.DMA((34,)),
            pltpu.SemaphoreType.DMA((34,)),
            pltpu.SemaphoreType.DMA((13,)),
            pltpu.SemaphoreType.DMA((37,)),
            pltpu.SemaphoreType.DMA((37,)),
        ],
        compiler_params=pltpu.CompilerParams(has_side_effects=True, collective_id=1, vmem_limit_bytes=48 << 20),
        name="combine",
    )(diag, sketch, far, mirrors)


def split_owner(col):
    owner = col // 16
    r, y = owner // 4, owner % 4
    c = r % 2
    x, z = r // 8, (r // 2) % 4
    a, b = jnp.where(c == 0, x, z), jnp.where(c == 0, z, x)
    return y * 2 + c, (a * 4 + b) * 16 + col % 16


def on_device(diag_blocks, off_blocks, col_blocks, sketch):
    entries = 128
    flat = col_blocks.reshape(entries)
    order = jnp.arange(entries)
    before = order[None, :] < order[:, None]
    group, spot = split_owner(flat)
    rank = jnp.sum(((group[:, None] == group[None, :]) & before).astype(jnp.int32), axis=1)
    slot = group * 32 + rank
    chosen = (slot[None, :] == jnp.arange(256)[:, None]).astype(jnp.int32)
    unused = 1 - jnp.sum(chosen, axis=1)
    pick = jnp.sum(chosen * order[None, :], axis=1)
    code = jnp.sum(chosen * ((order // 8) * 512 + spot)[None, :], axis=1) + unused * (16 * 512 + 256)
    count = 32 - jnp.sum(unused.reshape(8, 32), axis=1, keepdims=True)
    codes = jnp.concatenate([code.reshape(8, 32), jnp.broadcast_to(count, (8, 96))], axis=1)
    blocks, line, plane, metas = gather_all(pick, off_blocks.reshape(entries, 128, 128), sketch, codes)
    far, mirrors = products(
        metas, blocks, line.reshape(8, 16, 128, 256), plane.reshape(256, 128, 256)
    )
    image, tiles = combine(
        262144, diag_blocks, sketch, far.reshape(8, 2048, 256), mirrors.reshape(16, 2048, 256)
    )
    return solve(image, tiles)


def solution(mesh):
    placed = (
        P(("rows", "sub"), None, None),
        P(("rows", "sub"), None, None, None),
        P(("rows", "sub"), None),
        P(("rows", "sub"), None),
    )
    return jax.shard_map(
        on_device,
        mesh=mesh,
        in_specs=placed,
        out_specs=(P(("rows", "sub"), None), P()),
        check_vma=False,
    )
```

```python
import functools

import jax
import jax.numpy as jnp
from jax import lax
from jax.experimental import pallas as pl
from jax.experimental.pallas import tpu as pltpu
from jax.sharding import PartitionSpec as P

MESH = pl.DeviceIdType.MESH
HIGHEST = lax.Precision.HIGHEST
TILES = [(i, j) for i in range(32) for j in range(2) if i < 16 or j == 1]


def dot(a, b, dims, precision=HIGHEST):
    return lax.dot_general(a, b, (dims, ((), ())), precision=precision, preferred_element_type=jnp.float32)


def split(value):
    high = value.astype(jnp.bfloat16)
    return high, (value - high.astype(jnp.float32)).astype(jnp.bfloat16)


def eliminate(s):
    n, wide = s.shape
    strips = [s[8 * i : 8 * i + 8, :] for i in range(n // 8)]
    sub = lax.broadcasted_iota(jnp.int32, (8, 1), 0)

    def widen(v):
        return jnp.concatenate([v] * (wide // 128), axis=1)

    for p in range(n // 8):
        k = 8 * p
        cols = [
            [jnp.broadcast_to(strip[:, k + j : k + j + 1], (8, 128)) for strip in strips[p:]] for j in range(8)
        ]
        rows = [strips[p][j : j + 1, :] for j in range(8)]
        for j in range(8):
            scale = lax.rsqrt(cols[j][0][j : j + 1, :])
            cols[j] = [v * scale for v in cols[j]]
            rows[j] = rows[j] * widen(scale)
            for i in range(j + 1, 8):
                share = cols[j][0][i : i + 1, :]
                cols[i] = [u - v * share for u, v in zip(cols[i], cols[j])]
                rows[i] = rows[i] - rows[j] * widen(share)
        for j in range(8):
            for m in range(p + 1, n // 8):
                strips[m] = strips[m] - widen(cols[j][m - p]) * rows[j]
        pivot = strips[p]
        for j in range(8):
            pivot = jnp.where(sub == j, rows[j], pivot)
        strips[p] = pivot
    return strips


def solve_kernel(image, tiles, basis, upper, gram, work, linv):
    for t, (i, j) in enumerate(TILES):
        gram[8 * i : 8 * i + 8, 128 * j : 128 * j + 128] = tiles[t]
    eye = lax.broadcasted_iota(jnp.int32, (128, 128), 0), lax.broadcasted_iota(jnp.int32, (128, 128), 1)
    one = (eye[0] == eye[1]).astype(jnp.float32)
    for i, strip in enumerate(eliminate(jnp.concatenate([gram[:128, :128], one], axis=1))):
        work[8 * i : 8 * i + 8, :] = strip
    i11 = work[:, 128:]
    r12 = dot(i11, gram[:128, 128:], ((1,), (0,)))
    upper[:128, :128] = jnp.where(eye[0] <= eye[1], work[:, :128], 0.0)
    upper[:128, 128:] = r12
    linv[:128, :128] = i11
    linv[:128, 128:] = jnp.zeros((128, 128), jnp.float32)
    cross = dot(r12, i11, ((0,), (0,)))
    rest = gram[128:, 128:] - dot(r12, r12, ((0,), (0,)))
    for i, strip in enumerate(eliminate(jnp.concatenate([rest, one], axis=1))):
        work[8 * i : 8 * i + 8, :] = strip
    i22 = work[:, 128:]
    upper[128:, :128] = jnp.zeros((128, 128), jnp.float32)
    upper[128:, 128:] = jnp.where(eye[0] <= eye[1], work[:, :128], 0.0)
    linv[128:, :128] = -dot(i22, cross, ((1,), (0,)))
    linv[128:, 128:] = i22
    high, low = split(linv[...])
    across = ((1,), (1,))

    def rows_out(i, carry):
        at = pl.ds(pl.multiple_of(i * 256, 256), 256)
        h, l = split(image[at, :])
        basis[at, :] = dot(h, high, across, None) + (dot(h, low, across, None) + dot(l, high, across, None))
        return carry

    lax.fori_loop(0, 8, rows_out, 0)


def solve(image, tiles):
    f32 = jnp.float32
    vmem = pl.BlockSpec(memory_space=pltpu.VMEM)
    return pl.pallas_call(
        solve_kernel,
        out_shape=(jax.ShapeDtypeStruct((2048, 256), f32), jax.ShapeDtypeStruct((256, 256), f32)),
        in_specs=[vmem, vmem],
        out_specs=(vmem, vmem),
        scratch_shapes=[pltpu.VMEM((256, 256), f32), pltpu.VMEM((128, 256), f32), pltpu.VMEM((256, 256), f32)],
        compiler_params=pltpu.CompilerParams(vmem_limit_bytes=16 << 20),
        name="solve",
    )(image, tiles)


def place():
    r, y = lax.axis_index("rows"), lax.axis_index("sub")
    return r // 8, y, (r // 2) % 4, r % 2


def place_in_line():
    return lax.axis_index("sub") * 2 + lax.axis_index("rows") % 2


def remote(src, dst, sems, k, x, y, z, c):
    send, recv = sems
    return pltpu.make_async_remote_copy(
        src_ref=src, dst_ref=dst, send_sem=send.at[k], recv_sem=recv.at[k],
        device_id=((x % 4) * 8 + (z % 4) * 2 + c % 2, y % 4), device_id_type=MESH)


def meet(partners):
    barrier = pltpu.get_barrier_semaphore()
    for x, y, z, c in partners:
        device = ((x % 4) * 8 + (z % 4) * 2 + c % 2, y % 4)
        pl.semaphore_signal(barrier, inc=1, device_id=device, device_id_type=MESH)
    pl.semaphore_wait(barrier, len(partners))


def line_offsets():
    return [(i, d) for i in range(4) for d in range(2) if (i, d) != (0, 0)]


def half(ref, h):
    return ref.at[pl.ds(1024 * h, 1024), :]


def gather_kernel(pick, off, sketch, meta, blocks, line, plane, metas, given, packed, held, send, recv, local):
    x, y, z, c = place()
    sems = (send, recv)
    a, b = x * (1 - c) + z * c, z * (1 - c) + x * c
    me = y * 2 + c
    own_q = a * 4 + b

    def q(i, j):
        return ((a + i) % 4) * 4 + (b + j) % 4

    def along(i, j):
        return x + 3 * 4 + (1 - c) * i + c * j, y, z + 3 * 4 + c * i + (1 - c) * j, c

    def line_at(i, d=0):
        return x, y + 4 + i, z, c + d

    def l(i):
        return ((y + 4 + i) % 4) * 2 + c


    def slots(j):
        return packed.at[pl.ds(j * 32, 32)]

    take = pltpu.make_async_copy(off, given, local.at[0])
    fetch = pltpu.make_async_copy(sketch, held, local.at[1])
    keep = [
        pltpu.make_async_copy(held, plane.at[own_q], local.at[2]),
        pltpu.make_async_copy(held, line.at[me], local.at[3]),
        pltpu.make_async_copy(slots(me), blocks.at[me], local.at[4]),
        pltpu.make_async_copy(meta, metas.at[me], local.at[5]),
    ]

    def ring(source, slot, to, base):
        return {
            (s, h): remote(half(source, h), half(slot, h), sems, base + 2 * (s < 0) + h, *to(s))
            for s in (1, -1) for h in range(2)
        }

    def onward(slots, to, base):
        return {
            s: remote(half(slots[s], h), half(slots[s], h), sems, base + h, *to(s))
            for s, h in ((1, 0), (-1, 1))
        }

    to_a = lambda s: along(s, 0)
    first = ring(sketch, plane.at[own_q], to_a, 0)
    first_on = onward({1: plane.at[q(3, 0)], -1: plane.at[q(1, 0)]}, to_a, 4)
    same = ring(sketch, line.at[me], line_at, 6)
    same_on = onward({1: line.at[l(-1)], -1: line.at[l(1)]}, line_at, 10)
    mate = [remote(sketch, line.at[me], sems, 12, *line_at(0, 1))]
    mate += [remote(line.at[l(i)], line.at[l(i)], sems, 12 + n, *line_at(0, 1)) for n, i in ((1, -1), (2, 1), (3, 2))]
    to_b = lambda s: along(0, s)
    second, second_on = [], []
    for n, i in enumerate((0, 3, 1, 2)):
        source = sketch if i == 0 else plane.at[q(i, 0)]
        second.append(ring(source, plane.at[q(i, 0)], to_b, 16 + 6 * n))
        second_on.append(onward({1: plane.at[q(i, 3)], -1: plane.at[q(i, 1)]}, to_b, 20 + 6 * n))
    across, labels = [], []
    for n, (i, d) in enumerate(line_offsets()):
        to = ((y + i) % 4) * 2 + (c + d) % 2
        across.append(remote(slots(to), blocks.at[me], sems, 40 + n, *line_at(i, d)))
        labels.append(remote(meta, metas.at[me], sems, 47 + n, *line_at(i, d)))
    take.start()
    fetch.start()
    meet([along(1, 0), along(-1, 0), along(0, 1), along(0, -1)] + [line_at(i, d) for i, d in line_offsets()])
    for cp in list(same.values()) + list(first.values()) + list(second[0].values()) + mate[:1] + labels:
        cp.start()
    take.wait()

    def place_block(t, carry):
        packed[t] = given[pick[t]]
        return carry

    lax.fori_loop(0, 256, place_block, 0, unroll=8)
    for cp in across:
        cp.start()
    fetch.wait()
    for cp in keep:
        cp.start()

    def pass_on(ring_, on_):
        ring_[1, 0].wait_recv()
        on_[1].start()
        ring_[-1, 1].wait_recv()
        on_[-1].start()

    pass_on(same, same_on)
    pass_on(first, first_on)
    first[1, 1].wait_recv()
    for cp in second[1].values():
        cp.start()
    first[-1, 0].wait_recv()
    for cp in second[2].values():
        cp.start()
    same[1, 1].wait_recv()
    mate[1].start()
    same[-1, 0].wait_recv()
    mate[2].start()
    pass_on(second[0], second_on[0])
    for s in (1, -1):
        first_on[s].wait_recv()
    for cp in second[3].values():
        cp.start()
    for n in (1, 2, 3):
        pass_on(second[n], second_on[n])
    for s in (1, -1):
        same_on[s].wait_recv()
    mate[3].start()
    for n in range(4):
        second[n][1, 1].wait_recv()
        second[n][-1, 0].wait_recv()
        for s in (1, -1):
            second_on[n][s].wait_recv()
    for cp in labels + across + mate + keep:
        cp.wait()
    for group in [first, first_on, same, same_on] + second + second_on:
        for cp in group.values():
            cp.wait_send()


def gather_all(pick, off, sketch, meta):
    anyspec = pl.BlockSpec(memory_space=pl.ANY)
    bf16 = jnp.bfloat16
    return pl.pallas_call(
        gather_kernel,
        out_shape=(
            jax.ShapeDtypeStruct((8, 32, 128, 128), bf16),
            jax.ShapeDtypeStruct((8, 2048, 256), bf16),
            jax.ShapeDtypeStruct((16, 2048, 256), bf16),
            jax.ShapeDtypeStruct((8, 8, 128), jnp.int32),
        ),
        in_specs=[pl.BlockSpec(memory_space=pltpu.SMEM)] + [anyspec] * 3,
        out_specs=(anyspec,) * 4,
        scratch_shapes=[
            pltpu.VMEM((128, 128, 128), bf16),
            pltpu.VMEM((256, 128, 128), bf16),
            pltpu.VMEM((2048, 256), bf16),
            pltpu.SemaphoreType.DMA((54,)),
            pltpu.SemaphoreType.DMA((54,)),
            pltpu.SemaphoreType.DMA((6,)),
        ],
        compiler_params=pltpu.CompilerParams(has_side_effects=True, collective_id=0, vmem_limit_bytes=60 << 20),
        name="gather",
    )(pick, off, sketch, meta)


def product_kernel(codes, blocks_all, line_all, plane, far, mirrors, acc, sums, blocks, line, wanted, fars_out, stage,
                   in_sem, want_sem, far_sem, sem):
    def want(s, t):
        column = jnp.minimum(codes[s, mine, t] % 512, 255)
        return pltpu.make_async_copy(plane.at[column], wanted.at[s % 2, t], want_sem.at[s % 2])

    mine = place_in_line()

    def given_in(s):
        p = s % 2
        return (
            pltpu.make_async_copy(blocks_all.at[s], blocks.at[p], in_sem.at[p, 0]),
            pltpu.make_async_copy(line_all.at[s], line.at[p], in_sem.at[p, 1]),
        )

    def ask(s):
        for cp in given_in(s):
            cp.start()

        def one(t, carry):
            want(s, t).start()
            return carry

        lax.fori_loop(0, codes[s, mine, 32], one, 0)

    def far_copy(s):
        return pltpu.make_async_copy(fars_out.at[s % 2], far.at[s], far_sem.at[s % 2])

    ask(0)

    def clear(i, carry):
        sums[i] = jnp.zeros((128, 256), jnp.float32)
        return carry

    lax.fori_loop(0, 256, clear, 0, unroll=4)

    def source(s, carry):
        @pl.when(s < 7)
        def _():
            ask(s + 1)

        acc[...] = jnp.zeros_like(acc)

        def arrived(t, c):
            want(s, t).wait()
            return c

        for cp in given_in(s):
            cp.wait()
        lax.fori_loop(0, codes[s, mine, 32], arrived, 0)

        def eight(g, c):
            code = [codes[s, mine, g * 8 + u] for u in range(8)]
            rows, cols = [v // 512 for v in code], [v % 512 for v in code]
            given = [blocks[s % 2, g * 8 + u] for u in range(8)]
            fars = [dot(given[u], wanted[s % 2, g * 8 + u], ((1,), (0,)), None) for u in range(8)]
            backs = [dot(given[u], line[s % 2, jnp.minimum(rows[u], 15)], ((0,), (0,)), None) for u in range(8)]
            for u in range(8):
                acc[rows[u]] += fars[u]
                sums[cols[u]] += backs[u].astype(jnp.bfloat16).astype(jnp.float32)
            return c

        lax.fori_loop(0, (codes[s, mine, 32] + 7) // 8, eight, 0)

        @pl.when(s >= 2)
        def _():
            far_copy(s - 2).wait()

        def out_far(i, c):
            fars_out[s % 2, i] = acc[i].astype(jnp.bfloat16)
            return c

        lax.fori_loop(0, 16, out_far, 0, unroll=2)
        far_copy(s).start()
        return carry

    lax.fori_loop(0, 8, source, 0)

    def written(n):
        return pltpu.make_async_copy(stage.at[n % 8], mirrors.at[pl.ds(16 * n, 16)], sem.at[n % 8])

    for n in range(16):
        if n >= 8:
            written(n - 8).wait()

        def out(i, carry):
            stage[n % 8, i] = sums[16 * n + i].astype(jnp.bfloat16)
            return carry

        lax.fori_loop(0, 16, out, 0, unroll=2)
        written(n).start()
    for n in range(8, 16):
        written(n).wait()
    for n in (6, 7):
        far_copy(n).wait()


def products(codes, blocks, line, plane):
    bf16 = jnp.bfloat16
    anyspec = pl.BlockSpec(memory_space=pl.ANY)
    return pl.pallas_call(
        product_kernel,
        in_specs=[pl.BlockSpec(memory_space=pltpu.SMEM), anyspec, anyspec, anyspec],
        out_specs=(anyspec, anyspec),
        scratch_shapes=[
            pltpu.VMEM((17, 128, 256), jnp.float32),
            pltpu.VMEM((257, 128, 256), jnp.float32),
            pltpu.VMEM((2, 32, 128, 128), bf16),
            pltpu.VMEM((2, 16, 128, 256), bf16),
            pltpu.VMEM((2, 32, 128, 256), bf16),
            pltpu.VMEM((2, 16, 128, 256), bf16),
            pltpu.VMEM((8, 16, 128, 256), bf16),
            pltpu.SemaphoreType.DMA((2, 2)),
            pltpu.SemaphoreType.DMA((2,)),
            pltpu.SemaphoreType.DMA((2,)),
            pltpu.SemaphoreType.DMA((8,)),
        ],
        out_shape=(
            jax.ShapeDtypeStruct((8, 16, 128, 256), bf16),
            jax.ShapeDtypeStruct((256, 128, 256), bf16),
        ),
        compiler_params=pltpu.CompilerParams(vmem_limit_bytes=60 << 20),
        name="products",
    )(codes, blocks, line, plane)


def combine_kernel(total_rows, diag, sketch, far, mirrors, image, total_tiles,
                   own, one, pre, next_to, sums, two, back, gram, tiles, from_line, part, from_plane,
                   send, recv, local, gsend, grecv):
    f32 = jnp.float32
    x, y, z, c = place()
    sems = (send, recv)
    a, b = x * (1 - c) + z * c, z * (1 - c) + x * c
    me = y * 2 + c

    def along(i, j):
        return x + (1 - c) * i + c * j, y, z + c * i + (1 - c) * j, c

    order = (1, 2, 3, 0)

    def q(i, t):
        return ((a + 4 + i) % 4) * 4 + (b + t) % 4

    opposite, straight, onward, near_own, keep = {}, {}, {}, {}, []
    for n, t in enumerate(order):
        for side, (s, h) in enumerate(((1, 0), (-1, 1))):
            k = 6 * n + side
            opposite[t, side] = remote(half(mirrors.at[q(2, t)], h), pre.at[side, t], sems, k, *along(4 + s, 0))
            straight[t, side] = remote(
                half(mirrors.at[q(s, t)], 1 - h), half(one.at[side, t], 1 - h), sems, k + 2, *along(4 + s, 0))
            onward[t, side] = remote(next_to.at[side, t], half(one.at[side, t], h), sems, k + 4, *along(4 + s, 0))
            near_own[t, side] = pltpu.make_async_copy(
                half(mirrors.at[q(s, t)], h), next_to.at[side, t], local.at[5 + 2 * n + side])
    lines = []
    for n, (i, d) in enumerate(line_offsets()):
        to = ((y + i) % 4) * 2 + (c + d) % 2
        lines.append(remote(far.at[to], back.at[n + 1], sems, 24 + n, x, y + i, z, c + d))
    keep = [pltpu.make_async_copy(mirrors.at[q(0, t)], own.at[t], local.at[t]) for t in range(4)]
    keep.append(pltpu.make_async_copy(far.at[me], back.at[0], local.at[4]))
    second = [remote(sums.at[t - 1], two.at[t - 1], sems, 30 + t, *along(0, t)) for t in range(1, 4)]
    for cp in list(near_own.values()) + keep:
        cp.start()
    meet([along(n // 4, n % 4) for n in range(1, 16)] + [(x, y + i, z, c + d) for i, d in line_offsets()])
    for cp in opposite.values():
        cp.start()
    for t in order:
        for side in range(2):
            straight[t, side].start()
        if t == 1:
            for cp in lines:
                cp.start()

    def near(i, carry):
        at = pl.ds(pl.multiple_of(i * 128, 128), 128)
        image[at, :] = dot(diag[i], sketch[at, :], ((1,), (0,)), None)
        return carry

    lax.fori_loop(0, 16, near, 0)
    for t in order:
        for side in range(2):
            near_own[t, side].wait()
            opposite[t, side].wait_recv()

            def join(i, carry):
                at = pl.ds(pl.multiple_of(i * 128, 128), 128)
                total = next_to[side, t, at, :].astype(f32) + pre[side, t, at, :].astype(f32)
                next_to[side, t, at, :] = total.astype(jnp.bfloat16)
                return carry

            lax.fori_loop(0, 8, join, 0)
            onward[t, side].start()
    for t in order:
        keep[t].wait()
        for side in range(2):
            straight[t, side].wait_recv()
            onward[t, side].wait_recv()

        def add(i, carry):
            at = pl.ds(pl.multiple_of(i * 128, 128), 128)
            total = own[t, at, :].astype(f32) + one[0, t, at, :].astype(f32) + one[1, t, at, :].astype(f32)
            if t:
                sums[t - 1, at, :] = total.astype(jnp.bfloat16)
            else:
                image[at, :] += total
            return carry

        lax.fori_loop(0, 16, add, 0)
        if t:
            second[t - 1].start()
    keep[4].wait()
    for cp in lines:
        cp.wait_recv()

    def add_far(i, carry):
        at = pl.ds(pl.multiple_of(i * 128, 128), 128)
        total = image[at, :]
        for n in range(8):
            total += back[n, at, :].astype(f32)
        image[at, :] = total
        return carry

    lax.fori_loop(0, 16, add_far, 0)
    for cp in second:
        cp.wait_recv()

    def add_two(i, carry):
        at = pl.ds(pl.multiple_of(i * 128, 128), 128)
        image[at, :] += two[0, at, :].astype(f32) + two[1, at, :].astype(f32) + two[2, at, :].astype(f32)
        return carry

    lax.fori_loop(0, 16, add_two, 0)
    for cp in [*opposite.values(), *straight.values(), *onward.values()] + lines + second:
        cp.wait_send()
    gram[...] = jnp.zeros_like(gram)

    def partial(i, carry):
        h, l = split(image[pl.ds(pl.multiple_of(i * 512, 512), 512), :])
        down = ((0,), (0,))
        gram[...] += dot(h, h, down, None) + (dot(h, l, down, None) + dot(l, h, down, None))
        return carry

    lax.fori_loop(0, 4, partial, 0)
    for t, (i, j) in enumerate(TILES):
        tiles[t] = gram[8 * i : 8 * i + 8, 128 * j : 128 * j + 128] * (1.0 / total_rows)
    gsems = (gsend, grecv)
    here = x * 4 + z

    def spot(i, j):
        return ((x + i) % 4) * 4 + (z + j) % 4

    shifts = [(n // 4, n % 4) for n in range(1, 16)]
    shifts.sort(key=lambda v: -(min(v[0], 4 - v[0]) + min(v[1], 4 - v[1])))
    scatter = [
        remote(tiles.at[pl.ds(spot(i, j) * 3, 3)], from_plane.at[here], gsems, n, x + i, y, z + j, c)
        for n, (i, j) in enumerate(shifts)
    ]
    for cp in scatter:
        cp.start()
    from_plane[here] = tiles[pl.ds(here * 3, 3)]
    for cp in scatter:
        cp.wait_recv()
    part[...] = jnp.sum(from_plane[...], axis=0)
    trade = [
        remote(part, from_line.at[me], gsems, 15 + n, x, y + i, z, c + d)
        for n, (i, d) in enumerate(line_offsets())
    ]
    for cp in trade:
        cp.start()
    from_line[me] = part[...]
    for cp in trade:
        cp.wait_recv()
    mine = total_tiles.at[pl.ds(here * 3, 3)]
    mine[...] = jnp.sum(from_line[...], axis=0)
    everyone = [remote(mine, mine, gsems, 22 + n, x + i, y, z + j, c) for n, (i, j) in enumerate(shifts)]
    for cp in everyone:
        cp.start()
    for cp in everyone:
        cp.wait_recv()
    for cp in scatter + trade + everyone:
        cp.wait_send()


def combine(total_rows, diag, sketch, far, mirrors):
    f32, bf16 = jnp.float32, jnp.bfloat16
    vmem = pl.BlockSpec(memory_space=pltpu.VMEM)
    anyspec = pl.BlockSpec(memory_space=pl.ANY)
    return pl.pallas_call(
        functools.partial(combine_kernel, total_rows),
        out_shape=(jax.ShapeDtypeStruct((2048, 256), f32), jax.ShapeDtypeStruct((48, 8, 128), f32)),
        in_specs=[vmem, vmem, anyspec, anyspec],
        out_specs=(vmem, vmem),
        scratch_shapes=[
            pltpu.VMEM((4, 2048, 256), bf16),
            pltpu.VMEM((2, 4, 2048, 256), bf16),
            pltpu.VMEM((2, 4, 1024, 256), bf16),
            pltpu.VMEM((2, 4, 1024, 256), bf16),
            pltpu.VMEM((3, 2048, 256), bf16),
            pltpu.VMEM((3, 2048, 256), bf16),
            pltpu.VMEM((8, 2048, 256), bf16),
            pltpu.VMEM((256, 256), f32),
            pltpu.VMEM((48, 8, 128), f32),
            pltpu.VMEM((8, 3, 8, 128), f32),
            pltpu.VMEM((3, 8, 128), f32),
            pltpu.VMEM((16, 3, 8, 128), f32),
            pltpu.SemaphoreType.DMA((34,)),
            pltpu.SemaphoreType.DMA((34,)),
            pltpu.SemaphoreType.DMA((13,)),
            pltpu.SemaphoreType.DMA((37,)),
            pltpu.SemaphoreType.DMA((37,)),
        ],
        compiler_params=pltpu.CompilerParams(has_side_effects=True, collective_id=1, vmem_limit_bytes=48 << 20),
        name="combine",
    )(diag, sketch, far, mirrors)


def split_owner(col):
    owner = col // 16
    r, y = owner // 4, owner % 4
    c = r % 2
    x, z = r // 8, (r // 2) % 4
    a, b = jnp.where(c == 0, x, z), jnp.where(c == 0, z, x)
    return y * 2 + c, (a * 4 + b) * 16 + col % 16


def on_device(diag_blocks, off_blocks, col_blocks, sketch):
    entries = 128
    flat = col_blocks.reshape(entries)
    order = jnp.arange(entries)
    before = order[None, :] < order[:, None]
    group, spot = split_owner(flat)
    rank = jnp.sum(((group[:, None] == group[None, :]) & before).astype(jnp.int32), axis=1)
    slot = group * 32 + rank
    chosen = (slot[None, :] == jnp.arange(256)[:, None]).astype(jnp.int32)
    unused = 1 - jnp.sum(chosen, axis=1)
    pick = jnp.sum(chosen * order[None, :], axis=1)
    code = jnp.sum(chosen * ((order // 8) * 512 + spot)[None, :], axis=1) + unused * (16 * 512 + 256)
    count = 32 - jnp.sum(unused.reshape(8, 32), axis=1, keepdims=True)
    codes = jnp.concatenate([code.reshape(8, 32), jnp.broadcast_to(count, (8, 96))], axis=1)
    blocks, line, plane, metas = gather_all(pick, off_blocks.reshape(entries, 128, 128), sketch, codes)
    far, mirrors = products(
        metas, blocks, line.reshape(8, 16, 128, 256), plane.reshape(256, 128, 256)
    )
    image, tiles = combine(
        262144, diag_blocks, sketch, far.reshape(8, 2048, 256), mirrors.reshape(16, 2048, 256)
    )
    return solve(image, tiles)


def solution(mesh):
    placed = (
        P(("rows", "sub"), None, None),
        P(("rows", "sub"), None, None, None),
        P(("rows", "sub"), None),
        P(("rows", "sub"), None),
    )
    return jax.shard_map(
        on_device,
        mesh=mesh,
        in_specs=placed,
        out_specs=(P(("rows", "sub"), None), P()),
        check_vma=False,
    )
```
